32 devices in a mesh: parts: 2 (over y), line: 4 (over x, core), cross: 4 (over z).
Axes of the slice: x: 2, y: 2, z: 4, core: 2. Of those that a mesh axis runs over, the one named last changes fastest.
Arguments:
- ham_tiles: float32 [128, 64, 768], P(('parts', 'line', 'cross')), parts along dimension 0, may hold values from -0.21875 to 0.21875
- ham_cols: int32 [128, 12], P(('parts', 'line', 'cross')), parts along dimension 0, may hold values from 0 to 15, as said below
- ham_count: int32 [128], P(('parts', 'line', 'cross')), parts along dimension 0, may hold values from 3 to 12, as said below
- dens_tiles: float32 [128, 64, 512], P(('parts', 'line', 'cross')), parts along dimension 0, may hold values from -6 to 6
- dens_cols: int32 [128, 8], P(('parts', 'line', 'cross')), parts along dimension 0, may hold values from 0 to 15, as said below
- dens_count: int32 [128], P(('parts', 'line', 'cross')), parts along dimension 0, may hold values from 2 to 8, as said below
- over_tiles: float32 [128, 64, 768], P(('parts', 'line', 'cross')), parts along dimension 0, may hold values from -0.21875 to 0.21875
Outputs:
- product_rows: float32 [128, 64, 1024], P(('parts', 'line', 'cross')), parts along dimension 0
- window: float32 [128, 64, 3072], P(('parts', 'line', 'cross')), parts along dimension 0
The draws below stay inside these ranges and needn't reach their ends.
There are 2 independent parts, one for each index of `parts`. The reference program is written for one: setup_inputs(seed, part) draws one part's arguments, and reference() takes and returns one part's arrays. A program takes and returns all parts, laid end to end along the dimension named above; each array names one. Nothing has to cross between parts.
Inputs may be any that keep to these rules, and one draw needn't show every extreme that they name: `ham_cols`: within a block row the column indices are distinct. Slots at or beyond the row's count are not part of the matrix. `dens_cols`: within a block row the column indices are distinct. Slots at or beyond the row's count are not part of the matrix. `ham_count`: the first block row of every region, and the block rows of one device in the middle of every region, use all 12 slots. `dens_count`: the first block row of every region, and the block rows of one device in the middle of every region, use all 8 slots.
All inputs are finite; a program needn't handle non-finite values.
Results may differ from the reference program's by a relative error of at most 0.0003.
Values sent between devices are 32-bit elements; how exact they have to be, the bound alone decides.
No kernel may reach another device: no remote copies, remote signals or barrier semaphores. Data moves between devices by JAX's collectives and lax.ppermute only.
A program may use at most 128 MiB of HBM per device.

```python
import jax
import jax.numpy as jnp
from jax import lax

TILE = 64
R_DEV = 4
KH = 12
KL = 8
B = 16
NB = 64
N_LINE = 4
N_CROSS = 4


def pattern_columns(key, list_len):
    scores = jax.random.randint(key, (NB, B), 0, 1 << 20) * B + jnp.arange(B, dtype=jnp.int32)[None, :]
    ranked = jnp.argsort(scores, axis=1)
    return ranked[:, :list_len].astype(jnp.int32)


def pattern_counts(key, list_len):
    fewest = max(1, list_len // 4)
    counts = jax.random.randint(key, (NB,), fewest, list_len + 1)
    row_ids = jnp.arange(NB, dtype=jnp.int32)
    leading = row_ids % B == 0
    core_rows = row_ids // R_DEV % N_CROSS == N_CROSS // 2
    return jnp.where(leading | core_rows, list_len, counts).astype(jnp.int32)


def draw_ham_cols(key, part):
    return pattern_columns(jax.random.fold_in(key, 11), KH)


def draw_dens_cols(key, part):
    return pattern_columns(jax.random.fold_in(key, 23), KL)


def draw_ham_count(key, part):
    return pattern_counts(jax.random.fold_in(key, 37), KH)


def draw_dens_count(key, part):
    return pattern_counts(jax.random.fold_in(key, 41), KL)


def steps_of(key, shape, shards, smallest, largest):
    level = 1.0
    for position, shards_of in shards:
        steps = jax.random.uniform(jax.random.fold_in(jax.random.fold_in(key, 6), position), (shards_of,), jnp.float32, smallest / len(shards), largest / len(shards))
        level = level * jnp.repeat(jnp.exp(steps), shape[position] // shards_of).reshape((-1,) + (1,) * (len(shape) - 1 - position))
    return level


def bell_draw(key, shape, deviation, reach, pieces=(), kind=jnp.bfloat16):
    values = jax.random.normal(key, shape, jnp.float32) * deviation
    if len(pieces) > 0:
        values = steps_of(key, shape, pieces, -0.22, 0.18) * values
    return jnp.clip(values, min=-reach, max=reach).astype(kind)


def setup_inputs(seed: int = 0, part: int = 0) -> dict:
    splits = jax.random.split(jax.random.key(seed), 8)
    part_splits = jax.random.split(jax.random.fold_in(splits[7], part), 8)
    return {
        "ham_tiles": bell_draw(part_splits[0], (NB, TILE, KH * TILE), (KH * TILE) ** -0.5, 0.21875, ((0, 16),), jnp.float32),
        "ham_cols": draw_ham_cols(jax.random.fold_in(jax.random.fold_in(splits[7], part), 71), part),
        "ham_count": draw_ham_count(jax.random.fold_in(jax.random.fold_in(splits[7], part), 71), part),
        "dens_tiles": bell_draw(part_splits[3], (NB, TILE, KL * TILE), 1.0, 6.0, ((0, 16),), jnp.float32),
        "dens_cols": draw_dens_cols(jax.random.fold_in(jax.random.fold_in(splits[7], part), 71), part),
        "dens_count": draw_dens_count(jax.random.fold_in(jax.random.fold_in(splits[7], part), 71), part),
        "over_tiles": bell_draw(part_splits[6], (NB, TILE, 3 * R_DEV * TILE), (3 * R_DEV * TILE) ** -0.5, 0.21875, ((0, 16),), jnp.float32),
    }


exact_prec = lax.Precision.HIGHEST


def densify(tiles_in, columns, counts, width_cols):
    rows_count = tiles_in.shape[0]
    tile_size = tiles_in.shape[1]
    list_len = columns.shape[1]
    in_list = jnp.arange(list_len, dtype=jnp.int32)[None, :] < counts[:, None]
    matches = columns[:, :, None] == jnp.arange(width_cols, dtype=jnp.int32)[None, None, :]
    onehot = jnp.where(matches & in_list[:, :, None], 1.0, 0.0).astype(jnp.float32)
    shaped = tiles_in.reshape(rows_count, tile_size, list_len, tile_size)
    dense_rows = jnp.einsum("nkb,nxky->nxby", onehot, shaped, precision=exact_prec)
    return dense_rows.reshape(rows_count, tile_size, width_cols * tile_size)


def reference(ham_tiles, ham_cols, ham_count, dens_tiles, dens_cols, dens_count, over_tiles):
    def region_product(index):
        lower = (index * B).astype(jnp.int32)
        ham_rows = lax.dynamic_slice_in_dim(ham_tiles, lower, B, 0)
        ham_lists = lax.dynamic_slice_in_dim(ham_cols, lower, B, 0)
        ham_used = lax.dynamic_slice_in_dim(ham_count, lower, B, 0)
        dens_rows = lax.dynamic_slice_in_dim(dens_tiles, lower, B, 0)
        dens_lists = lax.dynamic_slice_in_dim(dens_cols, lower, B, 0)
        dens_used = lax.dynamic_slice_in_dim(dens_count, lower, B, 0)
        ham_dense = densify(ham_rows, ham_lists, ham_used, B).reshape(B * TILE, B * TILE)
        dens_dense = densify(dens_rows, dens_lists, dens_used, B).reshape(B * TILE, B * TILE)
        result = jnp.dot(ham_dense, dens_dense, precision=exact_prec, preferred_element_type=jnp.float32)
        return result.reshape(B, TILE, B * TILE)

    regions = jnp.arange(N_LINE, dtype=jnp.int32)
    products = lax.map(region_product, regions)
    product_rows = products.reshape(NB, TILE, B * TILE)
    blocks = products.reshape(N_LINE, N_CROSS, R_DEV, TILE, B * TILE)
    weights = over_tiles.reshape(N_LINE, N_CROSS, R_DEV, TILE, 3, R_DEV, TILE)

    def line_terms(index):
        prev_index = (index + N_LINE - 1) % N_LINE
        next_index = (index + 1) % N_LINE
        own_term = jnp.einsum("ckxjy,ckyn->cjxn", weights[index][:, :, :, 1], blocks[index], precision=exact_prec)
        from_prev = jnp.einsum("ckxjy,ckyn->cjxn", weights[prev_index][:, :, :, 2], blocks[prev_index], precision=exact_prec)
        from_next = jnp.einsum("ckxjy,ckyn->cjxn", weights[next_index][:, :, :, 0], blocks[next_index], precision=exact_prec)
        return jnp.concatenate([from_prev, own_term, from_next], axis=-1)

    window = lax.map(line_terms, regions).reshape(NB, TILE, 3 * B * TILE)
    return (product_rows, window)
```

```python
import functools

import jax
import jax.numpy as jnp
from jax import lax
from jax.experimental import pallas as pl
from jax.experimental.pallas import tpu as pltpu
from jax.sharding import PartitionSpec as P

LANES = 128
F32 = jnp.float32
BF16 = jnp.bfloat16
VMEM = pltpu.VMEM
SMEM = pltpu.SMEM


def rotate(x, axis, by):
    count = lax.axis_size(axis)
    return lax.ppermute(x, axis, [(i, (i + by) % count) for i in range(count)])


def slot_table(columns, counts, width):
    slots = jnp.arange(columns.shape[1], dtype=jnp.int32)
    wanted = jnp.arange(width, dtype=jnp.int32)
    hit = (columns[:, None, :] == wanted[None, :, None]) & (
        slots[None, None, :] < counts[:, None, None]
    )
    return jnp.max(jnp.where(hit, slots + 1, 0), axis=2)


def split(v):
    hi = v.astype(BF16)
    return hi, (v - hi.astype(F32)).astype(BF16)


def low_lanes(rows):
    return lax.broadcasted_iota(jnp.int32, (rows, LANES), 1) < LANES // 2


def block_at(row_ref, code, upper):
    slot = jnp.maximum(code - 1, 0)
    v = row_ref[:, pl.ds(pl.multiple_of((slot >> 1) * LANES, LANES), LANES)]
    v = jnp.where((slot & 1) != upper, pltpu.roll(v, LANES // 2, 1), v)
    return jnp.where(code > 0, v, jnp.zeros_like(v))


def pair_at(row_ref, table, r, pair):
    v0 = block_at(row_ref, table[r, 2 * pair], 0)
    v1 = block_at(row_ref, table[r, 2 * pair + 1], 1)
    return jnp.where(low_lanes(v0.shape[0]), v0, v1)


def densify_half(chunk_ref, first, table, b):
    tile = chunk_ref.shape[1]
    for r in range(2):
        for pair in range(table.shape[1] // 2):
            hi, lo = split(pair_at(chunk_ref.at[first + r], table, first + r, pair))
            lanes = slice(pair * LANES, (pair + 1) * LANES)
            b[r * tile : (r + 1) * tile, lanes] = hi
            b[(2 + r) * tile : (3 + r) * tile, lanes] = lo


def times_half(a, b, lanes):
    depth = b.shape[0]
    return jnp.dot(a[:, :depth], b[:, lanes], preferred_element_type=F32) + jnp.dot(
        a[:, depth:], b[: depth // 2, lanes], preferred_element_type=F32
    )


def lane_blocks(width, step=256):
    return [slice(i, i + step) for i in range(0, width, step)]


def shard_of(step):
    count = lax.axis_size("cross")
    return lax.rem(lax.axis_index("cross") + count - step, count)


def first_kernel(ham_table, dens_table, ham, dens, a, acc, b):
    rows, tile, _ = ham.shape
    for q in range(rows):
        for pair in range(ham_table.shape[1] // 2):
            hi, lo = split(pair_at(ham.at[q], ham_table, q, pair))
            a[pair, q * tile : (q + 1) * tile, 0:LANES] = hi
            a[pair, q * tile : (q + 1) * tile, LANES : 2 * LANES] = hi
            a[pair, q * tile : (q + 1) * tile, 2 * LANES : 3 * LANES] = lo
    for half in range(rows // 2):
        densify_half(dens, 2 * half, dens_table, b)
        pair = shard_of(0) * (rows // 2) + half
        for lanes in lane_blocks(acc.shape[1]):
            part = times_half(a[pair], b, lanes)
            acc[:, lanes] = part if half == 0 else acc[:, lanes] + part


def add_kernel(step, halves, count, dens_table, a, acc_in, *rest):
    chunks, (acc, b) = rest[:count], rest[count:]
    per_shard = dens_table.shape[0] // 2
    for i, half in enumerate(halves):
        for r in range(2):
            pass
        table = dens_table.at[pl.ds(2 * half, 2)]
        densify_half(chunks[i], 0, table, b)
        pair = shard_of(step) * per_shard + half
        for lanes in lane_blocks(acc.shape[1]):
            before = acc_in if i == 0 else acc
            acc[:, lanes] = before[:, lanes] + times_half(a[pair], b, lanes)


def last_kernel(step, half, side, dens_table, a, acc_in, chunk, out, b):
    per_shard = dens_table.shape[0] // 2
    width = out.shape[1]
    table = dens_table.at[pl.ds(2 * half, 2)]
    tile = chunk.shape[1]
    first = side * width // LANES
    for r in range(2):
        for pair in range(width // LANES):
            hi, lo = split(pair_at(chunk.at[r], table, r, first + pair))
            lanes = slice(pair * LANES, (pair + 1) * LANES)
            b[r * tile : (r + 1) * tile, lanes] = hi
            b[(2 + r) * tile : (3 + r) * tile, lanes] = lo
    pair = shard_of(step) * per_shard + half
    for lanes in lane_blocks(width):
        source = slice(side * width + lanes.start, side * width + lanes.stop)
        out[:, lanes] = acc_in[:, source] + times_half(a[pair], b, lanes)


def margin_kernel(over, before, after, hi_out, lo_out):
    rows, tile, _ = over.shape
    wide = rows * tile
    for s, (ref, start) in enumerate(((before, 0), (over, wide), (after, 0))):
        for j in range(rows):
            for pair in range(rows // 2):
                at = start + j * tile
                lanes = slice(at // LANES * LANES, at // LANES * LANES + LANES)
                v0, v1 = ref[2 * pair, :, lanes], ref[2 * pair + 1, :, lanes]
                if at % LANES == 0:
                    v1 = pltpu.roll(v1, LANES // 2, 1)
                else:
                    v0 = pltpu.roll(v0, LANES // 2, 1)
                hi, lo = split(jnp.where(low_lanes(tile), v0, v1))
                to = slice(pair * LANES, (pair + 1) * LANES)
                hi_out[s, j * tile : (j + 1) * tile, to] = hi
                lo_out[s, j * tile : (j + 1) * tile, to] = lo


def weighted(m_hi, m_lo, s, p, store):
    for lanes in lane_blocks(p.shape[1]):
        hi, lo = split(p[:, lanes])
        store(
            lanes,
            jnp.dot(m_hi[s], hi, preferred_element_type=F32)
            + jnp.dot(m_hi[s], lo, preferred_element_type=F32)
            + jnp.dot(m_lo[s], hi, preferred_element_type=F32),
        )


def own_kernel(m_hi, m_lo, *rest):
    sides = len(rest) // 2 - 1
    parts = rest[:sides]
    product, window, term, sems = rest[sides:]
    rows, tile, width = product.shape
    step = width // sides
    copies = []
    for i, part in enumerate(parts):
        for q in range(rows):
            copies.append(
                pltpu.make_async_copy(
                    part.at[pl.ds(q * tile, tile)],
                    product.at[q, :, pl.ds(i * step, step)],
                    sems.at[0, i * rows + q],
                )
            )
            copies[-1].start()
    for i, part in enumerate(parts):

        def store(lanes, v, i=i):
            term[:, i * step + lanes.start : i * step + lanes.stop] = v

        weighted(m_hi, m_lo, 1, part, store)
    for q in range(rows):
        copies.append(
            pltpu.make_async_copy(
                term.at[pl.ds(q * tile, tile)],
                window.at[q, :, pl.ds(width, width)],
                sems.at[1, q],
            )
        )
        copies[-1].start()
    for copy in copies:
        copy.wait()


def arrived_kernel(side, m_hi, m_lo, before, after, window_in, window, term, sems):
    rows, tile, triple = window.shape
    width = triple // 3
    step = before.shape[1]
    copies = []
    for slot, (s, p) in enumerate(((0, before), (2, after))):

        def store(lanes, v, slot=slot):
            term[slot, :, lanes] = v

        weighted(m_hi, m_lo, s, p, store)
        for q in range(rows):
            copies.append(
                pltpu.make_async_copy(
                    term.at[slot, pl.ds(q * tile, tile)],
                    window.at[q, :, pl.ds(s * width + side * step, step)],
                    sems.at[slot, q],
                )
            )
            copies[-1].start()
    for copy in copies:
        copy.wait()


def call(kernel, name, out_shape, in_spaces, out_spaces, scratch, flops, moved, aliases=None):
    return pl.pallas_call(
        kernel,
        name=name,
        out_shape=out_shape,
        in_specs=[pl.BlockSpec(memory_space=s) for s in in_spaces],
        out_specs=jax.tree.map(lambda s: pl.BlockSpec(memory_space=s), out_spaces),
        scratch_shapes=scratch,
        input_output_aliases=aliases or {},
        cost_estimate=pl.CostEstimate(flops=flops, bytes_accessed=moved, transcendentals=0),
        compiler_params=pltpu.CompilerParams(vmem_limit_bytes=24 << 20),
    )


def shards(ham_tiles, ham_cols, ham_count, dens_tiles, dens_cols, dens_count, over_tiles):
    count = lax.axis_size("cross")
    rows, tile, _ = ham_tiles.shape
    blocks = rows * count
    width = blocks * tile
    tall = rows * tile
    per_shard = rows // 2
    sds = jax.ShapeDtypeStruct

    halves = [dens_tiles[2 * h : 2 * h + 2] for h in range(per_shard)]
    dens_table = slot_table(dens_cols, dens_count, blocks)
    ham_table = slot_table(ham_cols, ham_count, blocks)
    arrivals = []
    for step in range(1, count):
        halves = [rotate(h, "cross", 1) for h in halves]
        arrivals.append((halves, rotate(dens_table, "cross", step)))
    wide = rows * tile
    over_before = rotate(over_tiles[:, :, 2 * wide :], "line", 1)
    over_after = rotate(over_tiles[:, :, :wide], "line", -1)

    b_scratch = [VMEM((4 * tile, width), BF16)]
    a, acc = call(
        first_kernel,
        "first",
        (sds((blocks // 2, tall, 3 * LANES), BF16), sds((tall, width), F32)),
        (SMEM, SMEM, VMEM, VMEM),
        (VMEM, VMEM),
        b_scratch,
        2 * 3 * tall * tall * width,
        4 << 20,
    )(ham_table, dens_table, ham_tiles, dens_tiles)
    for step in range(1, count):
        chunks, table = arrivals[step - 1]
        last = step == count - 1
        todo = list(range(per_shard - 1 if last else per_shard))
        acc = call(
            functools.partial(add_kernel, step, todo, len(todo)),
            "add%d" % step,
            sds((tall, width), F32),
            (SMEM,) + (VMEM,) * (2 + len(todo)),
            VMEM,
            b_scratch,
            2 * 3 * tall * tall * width,
            4 << 20,
        )(table, a, acc, *[chunks[h] for h in todo])
    sides = 2
    part = width // sides
    parts = [
        call(
            functools.partial(last_kernel, count - 1, per_shard - 1, side),
            "last%d" % side,
            sds((tall, part), F32),
            (SMEM, VMEM, VMEM, VMEM),
            VMEM,
            [VMEM((4 * tile, part), BF16)],
            2 * 3 * tall * 2 * tile * part,
            2 << 20,
        )(table, a, acc, chunks[-1])
        for side in range(sides)
    ]
    before = [rotate(p, "line", 1) for p in parts]
    after = [rotate(p, "line", -1) for p in parts]

    m_hi, m_lo = call(
        margin_kernel,
        "margin",
        (sds((3, tall, tall), BF16),) * 2,
        (VMEM,) * 3,
        (VMEM, VMEM),
        [],
        1 << 20,
        2 << 20,
    )(over_tiles, over_before, over_after)
    product, window = call(
        own_kernel,
        "own",
        (sds((rows, tile, width), F32), sds((rows, tile, 3 * width), F32)),
        (VMEM,) * (2 + sides),
        (pl.ANY, pl.ANY),
        [VMEM((tall, width), F32), pltpu.SemaphoreType.DMA((2, sides * rows))],
        2 * 3 * tall * tall * width,
        4 << 20,
    )(m_hi, m_lo, *parts)
    for side in range(sides):
        window = call(
            functools.partial(arrived_kernel, side),
            "arrived%d" % side,
            sds((rows, tile, 3 * width), F32),
            (VMEM,) * 4 + (pl.ANY,),
            pl.ANY,
            [VMEM((2, tall, part), F32), pltpu.SemaphoreType.DMA((2, rows))],
            2 * 3 * tall * tall * part * 2,
            4 << 20,
            {4: 0},
        )(m_hi, m_lo, before[side], after[side], window)
    return (product, window)


def solution(mesh):
    whole = P(("parts", "line", "cross"))
    return jax.shard_map(
        shards,
        mesh=mesh,
        in_specs=(whole,) * 7,
        out_specs=(whole, whole),
        check_vma=False,
    )
```

```python
import functools

import jax
import jax.numpy as jnp
from jax import lax
from jax.experimental import pallas as pl
from jax.experimental.pallas import tpu as pltpu
from jax.sharding import PartitionSpec as P

LANES = 128
F32 = jnp.float32
BF16 = jnp.bfloat16
VMEM = pltpu.VMEM
SMEM = pltpu.SMEM


def rotate(x, axis, by):
    count = lax.axis_size(axis)
    return lax.ppermute(x, axis, [(i, (i + by) % count) for i in range(count)])


def ring_order(count):
    return list(range(0, count, 2))[:1] + list(range(1, count, 2)) + list(range(0, count, 2))[:0:-1]


def pass_on(x, by):
    order = ring_order(lax.axis_size("cross"))
    return lax.ppermute(
        x, "cross", [(d, order[(i + by) % len(order)]) for i, d in enumerate(order)]
    )


def shard_of(step):
    order = ring_order(lax.axis_size("cross"))
    me = lax.axis_index("cross")
    owner = jnp.int32(0)
    for i, d in enumerate(order):
        owner = jnp.where(me == d, order[i - step], owner)
    return owner


def slot_table(columns, counts, width):
    slots = jnp.arange(columns.shape[1], dtype=jnp.int32)
    wanted = jnp.arange(width, dtype=jnp.int32)
    hit = (columns[:, None, :] == wanted[None, :, None]) & (
        slots[None, None, :] < counts[:, None, None]
    )
    return jnp.max(jnp.where(hit, slots + 1, 0), axis=2)


def split(v):
    hi = v.astype(BF16)
    return hi, (v - hi.astype(F32)).astype(BF16)


def low_lanes(rows):
    return lax.broadcasted_iota(jnp.int32, (rows, LANES), 1) < LANES // 2


def block_at(row_ref, code, upper):
    slot = jnp.maximum(code - 1, 0)
    v = row_ref[:, pl.ds(pl.multiple_of((slot >> 1) * LANES, LANES), LANES)]
    v = jnp.where((slot & 1) != upper, pltpu.roll(v, LANES // 2, 1), v)
    return jnp.where(code > 0, v, jnp.zeros_like(v))


def pair_at(row_ref, table, r, pair):
    v0 = block_at(row_ref, table[r, 2 * pair], 0)
    v1 = block_at(row_ref, table[r, 2 * pair + 1], 1)
    return jnp.where(low_lanes(v0.shape[0]), v0, v1)


def densify_half(chunk_ref, first, table, b):
    tile = chunk_ref.shape[1]
    for r in range(2):
        for pair in range(table.shape[1] // 2):
            hi, lo = split(pair_at(chunk_ref.at[first + r], table, first + r, pair))
            lanes = slice(pair * LANES, (pair + 1) * LANES)
            b[r * tile : (r + 1) * tile, lanes] = hi
            b[(2 + r) * tile : (3 + r) * tile, lanes] = lo


def times_half(a, b, lanes):
    depth = b.shape[0]
    return jnp.dot(a[:, :depth], b[:, lanes], preferred_element_type=F32) + jnp.dot(
        a[:, depth:], b[: depth // 2, lanes], preferred_element_type=F32
    )


def lane_blocks(width, step=256):
    return [slice(i, i + step) for i in range(0, width, step)]


def first_kernel(ham_table, dens_table, ham, dens, a, acc, b):
    rows, tile, _ = ham.shape
    for q in range(rows):
        for pair in range(ham_table.shape[1] // 2):
            hi, lo = split(pair_at(ham.at[q], ham_table, q, pair))
            a[pair, q * tile : (q + 1) * tile, 0:LANES] = hi
            a[pair, q * tile : (q + 1) * tile, LANES : 2 * LANES] = hi
            a[pair, q * tile : (q + 1) * tile, 2 * LANES : 3 * LANES] = lo
    for half in range(rows // 2):
        densify_half(dens, 2 * half, dens_table, b)
        pair = shard_of(0) * (rows // 2) + half
        for lanes in lane_blocks(acc.shape[1]):
            part = times_half(a[pair], b, lanes)
            acc[:, lanes] = part if half == 0 else acc[:, lanes] + part


def add_kernel(step, halves, count, dens_table, a, acc_in, *rest):
    chunks, (acc, b) = rest[:count], rest[count:]
    per_shard = dens_table.shape[0] // 2
    for i, half in enumerate(halves):
        table = dens_table.at[pl.ds(2 * half, 2)]
        densify_half(chunks[i], 0, table, b)
        pair = shard_of(step) * per_shard + half
        for lanes in lane_blocks(acc.shape[1]):
            before = acc_in if i == 0 else acc
            acc[:, lanes] = before[:, lanes] + times_half(a[pair], b, lanes)


def last_kernel(step, half, first, widths, dens_table, a, acc_in, chunk, *rest):
    outs, b = rest[:-1], rest[-1]
    per_shard = dens_table.shape[0] // 2
    width = sum(widths)
    table = dens_table.at[pl.ds(2 * half, 2)]
    tile = chunk.shape[1]
    for r in range(2):
        for pair in range(width // LANES):
            hi, lo = split(pair_at(chunk.at[r], table, r, first // LANES + pair))
            lanes = slice(pair * LANES, (pair + 1) * LANES)
            b[r * tile : (r + 1) * tile, lanes] = hi
            b[(2 + r) * tile : (3 + r) * tile, lanes] = lo
    pair = shard_of(step) * per_shard + half
    at = 0
    for out, piece in zip(outs, widths):
        for lanes in lane_blocks(piece):
            here = slice(at + lanes.start, at + lanes.stop)
            source = slice(first + here.start, first + here.stop)
            out[:, lanes] = acc_in[:, source] + times_half(a[pair], b, here)
        at += piece


def margin_kernel(over, before, after, hi_out, lo_out):
    rows, tile, _ = over.shape
    wide = rows * tile
    for s, (ref, start) in enumerate(((before, 0), (over, wide), (after, 0))):
        for j in range(rows):
            for pair in range(rows // 2):
                at = start + j * tile
                lanes = slice(at // LANES * LANES, at // LANES * LANES + LANES)
                v0, v1 = ref[2 * pair, :, lanes], ref[2 * pair + 1, :, lanes]
                if at % LANES == 0:
                    v1 = pltpu.roll(v1, LANES // 2, 1)
                else:
                    v0 = pltpu.roll(v0, LANES // 2, 1)
                hi, lo = split(jnp.where(low_lanes(tile), v0, v1))
                to = slice(pair * LANES, (pair + 1) * LANES)
                hi_out[s, j * tile : (j + 1) * tile, to] = hi
                lo_out[s, j * tile : (j + 1) * tile, to] = lo


def weighted(m_hi, m_lo, s, p, store):
    for lanes in lane_blocks(p.shape[1]):
        hi, lo = split(p[:, lanes])
        store(
            lanes,
            jnp.dot(m_hi[s], hi, preferred_element_type=F32)
            + jnp.dot(m_hi[s], lo, preferred_element_type=F32)
            + jnp.dot(m_lo[s], hi, preferred_element_type=F32),
        )


def own_kernel(pieces, m_hi, m_lo, *rest):
    parts = rest[: len(pieces)]
    product, window, term, sems = rest[len(pieces) :]
    rows, tile, width = product.shape
    copies = []
    at = 0
    for i, part in enumerate(parts):
        step = part.shape[1]
        for q in range(rows):
            copies.append(
                pltpu.make_async_copy(
                    part.at[pl.ds(q * tile, tile)],
                    product.at[q, :, pl.ds(at, step)],
                    sems.at[i, q],
                )
            )
            copies[-1].start()
        at += step
    at = 0
    for part in parts:

        def store(lanes, v, at=at):
            term[:, at + lanes.start : at + lanes.stop] = v

        weighted(m_hi, m_lo, 1, part, store)
        at += part.shape[1]
    for q in range(rows):
        copies.append(
            pltpu.make_async_copy(
                term.at[pl.ds(q * tile, tile)],
                window.at[q, :, pl.ds(width, width)],
                sems.at[len(parts), q],
            )
        )
        copies[-1].start()
    for copy in copies:
        copy.wait()


def arrived_kernel(at, m_hi, m_lo, before, after, window_in, window, term, sems):
    rows, tile, triple = window.shape
    width = triple // 3
    copies = []
    for slot, (s, p) in enumerate(((0, before), (2, after))):

        def store(lanes, v, slot=slot, s=s):
            term[slot, :, lanes] = v
            for q in range(rows):
                copies.append(
                    pltpu.make_async_copy(
                        term.at[slot, pl.ds(q * tile, tile), lanes],
                        window.at[q, :, pl.ds(s * width + at + lanes.start, lanes.stop - lanes.start)],
                        sems.at[len(copies)],
                    )
                )
                copies[-1].start()

        weighted(m_hi, m_lo, s, p, store)
    for copy in copies:
        copy.wait()


def call(kernel, name, out_shape, in_spaces, out_spaces, scratch, flops, moved, aliases=None):
    return pl.pallas_call(
        kernel,
        name=name,
        out_shape=out_shape,
        in_specs=[pl.BlockSpec(memory_space=s) for s in in_spaces],
        out_specs=jax.tree.map(lambda s: pl.BlockSpec(memory_space=s), out_spaces),
        scratch_shapes=scratch,
        input_output_aliases=aliases or {},
        cost_estimate=pl.CostEstimate(flops=flops, bytes_accessed=moved, transcendentals=0),
        compiler_params=pltpu.CompilerParams(vmem_limit_bytes=24 << 20),
    )


def shards(ham_tiles, ham_cols, ham_count, dens_tiles, dens_cols, dens_count, over_tiles):
    count = lax.axis_size("cross")
    rows, tile, _ = ham_tiles.shape
    blocks = rows * count
    width = blocks * tile
    tall = rows * tile
    per_shard = rows // 2
    sds = jax.ShapeDtypeStruct

    halves = [dens_tiles[2 * h : 2 * h + 2] for h in range(per_shard)]
    halves, dens_cols, dens_count = lax.optimization_barrier((halves, dens_cols, dens_count))
    dens_table = slot_table(dens_cols, dens_count, blocks)
    ham_table = slot_table(ham_cols, ham_count, blocks)
    over_before = rotate(over_tiles[:, :, 2 * tall :], "line", 1)
    over_after = rotate(over_tiles[:, :, :tall], "line", -1)

    b_scratch = [VMEM((4 * tile, width), BF16)]
    a, acc = call(
        first_kernel,
        "first",
        (sds((blocks // 2, tall, 3 * LANES), BF16), sds((tall, width), F32)),
        (SMEM, SMEM, VMEM, VMEM),
        (VMEM, VMEM),
        b_scratch,
        2 * 3 * tall * tall * width,
        4 << 20,
    )(ham_table, dens_table, ham_tiles, dens_tiles)
    m_hi, m_lo = call(
        margin_kernel,
        "margin",
        (sds((3, tall, tall), BF16),) * 2,
        (VMEM,) * 3,
        (VMEM, VMEM),
        [],
        1 << 20,
        2 << 20,
    )(over_tiles, over_before, over_after)
    done = acc
    for step in range(1, count):
        if step > 1:
            halves[-1], done, m_hi, m_lo = lax.optimization_barrier(
                (halves[-1], done, m_hi, m_lo) if step == 3 else (halves[-1], done)
            ) + (() if step == 3 else (m_hi, m_lo))
        chunks = halves = [pass_on(h, 1) for h in halves]
        table = pass_on(dens_table, step)
        last = step == count - 1
        todo = list(range(per_shard - 1 if last else per_shard))
        done, acc = acc, call(
            functools.partial(add_kernel, step, todo, len(todo)),
            "add%d" % step,
            sds((tall, width), F32),
            (SMEM,) + (VMEM,) * (2 + len(todo)),
            VMEM,
            b_scratch,
            2 * 3 * tall * tall * width,
            4 << 20,
        )(table, a, acc, *[chunks[h] for h in todo])
        halves = list(halves)
    pieces = (width // 2, width // 4, width // 4)
    parts = []
    for i, piece in enumerate(pieces):
        parts += call(
            functools.partial(
                last_kernel, count - 1, per_shard - 1, sum(pieces[:i]), (piece,)
            ),
            "last%d" % i,
            [sds((tall, piece), F32)],
            (SMEM, VMEM, VMEM, VMEM),
            [VMEM],
            [VMEM((4 * tile, piece), BF16)],
            1024,
            1024,
        )(table, a, acc, chunks[-1])
        if i + 1 < len(pieces):
            parts[-1], acc = lax.optimization_barrier((parts[-1], acc))
    before = [rotate(p, "line", 1) for p in parts]
    after = [rotate(p, "line", -1) for p in parts]
    product, window = call(
        functools.partial(own_kernel, pieces),
        "own",
        (sds((rows, tile, width), F32), sds((rows, tile, 3 * width), F32)),
        (VMEM,) * (2 + len(pieces)),
        (pl.ANY, pl.ANY),
        [VMEM((tall, width), F32), pltpu.SemaphoreType.DMA((len(pieces) + 1, rows))],
        1024,
        1024,
    )(m_hi, m_lo, *parts)
    at = 0
    for i, piece in enumerate(pieces):
        window = call(
            functools.partial(arrived_kernel, at),
            "arrived%d" % i,
            sds((rows, tile, 3 * width), F32),
            (VMEM,) * 4 + (pl.ANY,),
            pl.ANY,
            [VMEM((2, tall, piece), F32), pltpu.SemaphoreType.DMA((2 * rows * piece // 256,))],
            1024,
            1024,
            {4: 0},
        )(m_hi, m_lo, before[i], after[i], window)
        at += piece
    return (product, window)


def solution(mesh):
    whole = P(("parts", "line", "cross"))
    return jax.shard_map(
        shards,
        mesh=mesh,
        in_specs=(whole,) * 7,
        out_specs=(whole, whole),
        check_vma=False,
    )
```

```python
import functools

import jax
import jax.numpy as jnp
from jax import lax
from jax.experimental import pallas as pl
from jax.experimental.pallas import tpu as pltpu
from jax.sharding import PartitionSpec as P

LANES = 128
F32 = jnp.float32
BF16 = jnp.bfloat16
VMEM = pltpu.VMEM
SMEM = pltpu.SMEM


def rotate(x, axis, by):
    count = lax.axis_size(axis)
    return lax.ppermute(x, axis, [(i, (i + by) % count) for i in range(count)])


def ring_order(count):
    return list(range(0, count, 2))[:1] + list(range(1, count, 2)) + list(range(0, count, 2))[:0:-1]


def pass_on(x, by):
    order = ring_order(lax.axis_size("cross"))
    return lax.ppermute(
        x, "cross", [(d, order[(i + by) % len(order)]) for i, d in enumerate(order)]
    )


def shard_of(step):
    order = ring_order(lax.axis_size("cross"))
    me = lax.axis_index("cross")
    owner = jnp.int32(0)
    for i, d in enumerate(order):
        owner = jnp.where(me == d, order[i - step], owner)
    return owner


def fill_table(table, columns, counts):
    rows, width = table.shape
    for r in range(rows):
        for c in range(width):
            table[r, c] = 0
        for slot in range(columns.shape[1]):

            @pl.when(slot < counts[r])
            def _(r=r, slot=slot):
                table[r, columns[r, slot]] = slot + 1


def prep_kernel(columns, counts, dens, *rest):
    halves, table, sems = rest[:-2], rest[-2], rest[-1]
    copies = []
    for h, half in enumerate(halves):
        copies.append(pltpu.make_async_copy(dens.at[pl.ds(2 * h, 2)], half, sems.at[h]))
        copies[-1].start()
    fill_table(table, columns, counts)
    for copy in copies:
        copy.wait()


def split(v):
    hi = v.astype(BF16)
    return hi, (v - hi.astype(F32)).astype(BF16)


def low_lanes(rows):
    return lax.broadcasted_iota(jnp.int32, (rows, LANES), 1) < LANES // 2


def block_at(row_ref, code, upper):
    slot = jnp.maximum(code - 1, 0)
    v = row_ref[:, pl.ds(pl.multiple_of((slot >> 1) * LANES, LANES), LANES)]
    v = jnp.where((slot & 1) != upper, pltpu.roll(v, LANES // 2, 1), v)
    return jnp.where(code > 0, v, jnp.zeros_like(v))


def pair_at(row_ref, table, r, pair):
    v0 = block_at(row_ref, table[r, 2 * pair], 0)
    v1 = block_at(row_ref, table[r, 2 * pair + 1], 1)
    return jnp.where(low_lanes(v0.shape[0]), v0, v1)


def densify_half(chunk, table, half, b, first=0):
    tile = chunk.shape[1]
    for r in range(2):
        for pair in range(b.shape[1] // LANES):
            hi, lo = split(pair_at(chunk.at[r], table, 2 * half + r, first + pair))
            lanes = slice(pair * LANES, (pair + 1) * LANES)
            b[r * tile : (r + 1) * tile, lanes] = hi
            b[(2 + r) * tile : (3 + r) * tile, lanes] = lo


def times_half(a, b, lanes):
    depth = b.shape[0]
    return jnp.dot(a[:, :depth], b[:, lanes], preferred_element_type=F32) + jnp.dot(
        a[:, depth:], b[: depth // 2, lanes], preferred_element_type=F32
    )


def lane_blocks(width, step=256):
    return [slice(i, i + step) for i in range(0, width, step)]


def first_kernel(ham_cols, ham_count, dens_table, ham, *rest):
    (a, acc, ham_table, ham_here, b, sems), halves = rest[-6:], rest[:-6]
    rows, tile, _ = ham.shape
    copies = [
        pltpu.make_async_copy(ham.at[q], ham_here.at[q], sems.at[q]) for q in range(rows)
    ]
    for copy in copies:
        copy.start()
    fill_table(ham_table, ham_cols, ham_count)
    for q in range(rows):
        copies[q].wait()
        for pair in range(ham_table.shape[1] // 2):
            hi, lo = split(pair_at(ham_here.at[q], ham_table, q, pair))
            a[pair, q * tile : (q + 1) * tile, 0:LANES] = hi
            a[pair, q * tile : (q + 1) * tile, LANES : 2 * LANES] = hi
            a[pair, q * tile : (q + 1) * tile, 2 * LANES : 3 * LANES] = lo
    for h, half in enumerate(halves):
        densify_half(half, dens_table, h, b)
        pair = shard_of(0) * (rows // 2) + h
        for lanes in lane_blocks(acc.shape[1]):
            part = times_half(a[pair], b, lanes)
            acc[:, lanes] = part if h == 0 else acc[:, lanes] + part


def add_kernel(step, halves, dens_table, a, acc_in, *rest):
    chunks, (acc, b) = rest[:-2], rest[-2:]
    per_shard = dens_table.shape[0] // 2
    for i, half in enumerate(halves):
        densify_half(chunks[i], dens_table, half, b)
        pair = shard_of(step) * per_shard + half
        for lanes in lane_blocks(acc.shape[1]):
            before = acc_in if i == 0 else acc
            acc[:, lanes] = before[:, lanes] + times_half(a[pair], b, lanes)


def last_kernel(step, half, first, dens_table, a, acc_in, chunk, out, b):
    per_shard = dens_table.shape[0] // 2
    densify_half(chunk, dens_table, half, b, first // LANES)
    pair = shard_of(step) * per_shard + half
    for lanes in lane_blocks(out.shape[1]):
        source = slice(first + lanes.start, first + lanes.stop)
        out[:, lanes] = acc_in[:, source] + times_half(a[pair], b, lanes)


def margin_kernel(over, before, after, hi_out, lo_out):
    rows, tile, _ = over.shape
    wide = rows * tile
    for s, (ref, start) in enumerate(((before, 0), (over, wide), (after, 0))):
        for j in range(rows):
            for pair in range(rows // 2):
                at = start + j * tile
                lanes = slice(at // LANES * LANES, at // LANES * LANES + LANES)
                v0, v1 = ref[2 * pair, :, lanes], ref[2 * pair + 1, :, lanes]
                if at % LANES == 0:
                    v1 = pltpu.roll(v1, LANES // 2, 1)
                else:
                    v0 = pltpu.roll(v0, LANES // 2, 1)
                hi, lo = split(jnp.where(low_lanes(tile), v0, v1))
                to = slice(pair * LANES, (pair + 1) * LANES)
                hi_out[s, j * tile : (j + 1) * tile, to] = hi
                lo_out[s, j * tile : (j + 1) * tile, to] = lo


def weighted(m_hi, m_lo, s, p, store):
    for lanes in lane_blocks(p.shape[1]):
        hi, lo = split(p[:, lanes])
        store(
            lanes,
            jnp.dot(m_hi[s], hi, preferred_element_type=F32)
            + jnp.dot(m_hi[s], lo, preferred_element_type=F32)
            + jnp.dot(m_lo[s], hi, preferred_element_type=F32),
        )


def own_kernel(pieces, m_hi, m_lo, *rest):
    parts = rest[: len(pieces)]
    product, window, term, sems = rest[len(pieces) :]
    rows, tile, width = product.shape
    copies = []
    at = 0
    for i, part in enumerate(parts):
        step = part.shape[1]
        for q in range(rows):
            copies.append(
                pltpu.make_async_copy(
                    part.at[pl.ds(q * tile, tile)],
                    product.at[q, :, pl.ds(at, step)],
                    sems.at[i, q],
                )
            )
            copies[-1].start()
        at += step
    at = 0
    for part in parts:

        def store(lanes, v, at=at):
            term[:, at + lanes.start : at + lanes.stop] = v

        weighted(m_hi, m_lo, 1, part, store)
        at += part.shape[1]
    for q in range(rows):
        copies.append(
            pltpu.make_async_copy(
                term.at[pl.ds(q * tile, tile)],
                window.at[q, :, pl.ds(width, width)],
                sems.at[len(parts), q],
            )
        )
        copies[-1].start()
    for copy in copies:
        copy.wait()


def arrived_kernel(at, m_hi, m_lo, before, after, window_in, window, term, sems):
    rows, tile, triple = window.shape
    width = triple // 3
    copies = []
    for slot, (s, p) in enumerate(((0, before), (2, after))):

        def store(lanes, v, slot=slot, s=s):
            term[slot, :, lanes] = v
            for q in range(rows):
                copies.append(
                    pltpu.make_async_copy(
                        term.at[slot, pl.ds(q * tile, tile), lanes],
                        window.at[q, :, pl.ds(s * width + at + lanes.start, lanes.stop - lanes.start)],
                        sems.at[len(copies)],
                    )
                )
                copies[-1].start()

        weighted(m_hi, m_lo, s, p, store)
    for copy in copies:
        copy.wait()


def call(kernel, name, out_shape, in_spaces, out_spaces, scratch, flops, moved, aliases=None):
    return pl.pallas_call(
        kernel,
        name=name,
        out_shape=out_shape,
        in_specs=[pl.BlockSpec(memory_space=s) for s in in_spaces],
        out_specs=jax.tree.map(lambda s: pl.BlockSpec(memory_space=s), out_spaces),
        scratch_shapes=scratch,
        input_output_aliases=aliases or {},
        cost_estimate=pl.CostEstimate(flops=flops, bytes_accessed=moved, transcendentals=0),
        compiler_params=pltpu.CompilerParams(vmem_limit_bytes=24 << 20),
    )


def shards(ham_tiles, ham_cols, ham_count, dens_tiles, dens_cols, dens_count, over_tiles):
    count = lax.axis_size("cross")
    rows, tile, _ = ham_tiles.shape
    blocks = rows * count
    width = blocks * tile
    tall = rows * tile
    per_shard = rows // 2
    sds = jax.ShapeDtypeStruct

    ham_tiles, dens_tiles = (
        pltpu.with_memory_space_constraint(x, pltpu.HBM) for x in (ham_tiles, dens_tiles)
    )
    *halves, table = call(
        prep_kernel,
        "prep",
        [sds((2, tile, dens_tiles.shape[2]), F32)] * per_shard + [sds((rows, blocks), jnp.int32)],
        (SMEM, SMEM, pltpu.HBM),
        [VMEM] * per_shard + [SMEM],
        [pltpu.SemaphoreType.DMA((per_shard,))],
        1024,
        1024,
    )(dens_cols, dens_count, dens_tiles)
    tables = [pass_on(table, step) for step in range(1, count)]
    b_scratch = [VMEM((4 * tile, width), BF16)]
    a, acc = call(
        first_kernel,
        "first",
        (sds((blocks // 2, tall, 3 * LANES), BF16), sds((tall, width), F32)),
        (SMEM, SMEM, SMEM, pltpu.HBM) + (VMEM,) * per_shard,
        (VMEM, VMEM),
        [pltpu.SMEM((rows, blocks), jnp.int32), VMEM(ham_tiles.shape, F32)]
        + b_scratch
        + [pltpu.SemaphoreType.DMA((rows,))],
        1 << 20,
        1 << 20,
    )(ham_cols, ham_count, table, ham_tiles, *halves)
    halves = [pass_on(h, 1) for h in halves]
    for step in range(1, count):
        if step == 1:
            halves[0], a, acc, over_tiles = lax.optimization_barrier(
                (halves[0], a, acc, over_tiles)
            )
            halves[-1], *tables = lax.optimization_barrier((halves[-1], *tables))
            over_before = rotate(over_tiles[:, :, 2 * tall :], "line", 1)
            over_after = rotate(over_tiles[:, :, :tall], "line", -1)
            m_hi, m_lo = call(
                margin_kernel,
                "margin",
                (sds((3, tall, tall), BF16),) * 2,
                (VMEM,) * 3,
                (VMEM, VMEM),
                [],
                1 << 20,
                2 << 20,
            )(over_tiles, over_before, over_after)
        else:
            halves[0], acc = lax.optimization_barrier((halves[0], acc))
        if step == 2:
            halves[-1], m_hi, m_lo = lax.optimization_barrier((halves[-1], m_hi, m_lo))
        last = step == count - 1
        arrived = list(halves)
        if not last:
            halves = [pass_on(h, 1) for h in halves]
        todo = list(range(per_shard - 1 if last else per_shard))
        acc = call(
            functools.partial(add_kernel, step, todo),
            "add%d" % step,
            sds((tall, width), F32),
            (SMEM,) + (VMEM,) * (2 + len(todo)),
            VMEM,
            b_scratch,
            1 << 20,
            1 << 20,
        )(tables[step - 1], a, acc, *[arrived[h] for h in todo])
    pieces = (width // 2, width // 2)
    parts = []
    for i, piece in enumerate(pieces):
        parts.append(
            call(
                functools.partial(last_kernel, count - 1, per_shard - 1, sum(pieces[:i])),
                "last%d" % i,
                sds((tall, piece), F32),
                (SMEM, VMEM, VMEM, VMEM),
                VMEM,
                [VMEM((4 * tile, piece), BF16)],
                1024,
                1024,
            )(tables[-1], a, acc, halves[-1])
        )
        if i + 1 < len(pieces):
            parts[-1], acc = lax.optimization_barrier((parts[-1], acc))
    before = [rotate(p, "line", 1) for p in parts]
    after = [rotate(p, "line", -1) for p in parts]
    product, window = call(
        functools.partial(own_kernel, pieces),
        "own",
        (sds((rows, tile, width), F32), sds((rows, tile, 3 * width), F32)),
        (VMEM,) * (2 + len(pieces)),
        (pl.ANY, pl.ANY),
        [VMEM((tall, width), F32), pltpu.SemaphoreType.DMA((len(pieces) + 1, rows))],
        1024,
        1024,
    )(m_hi, m_lo, *parts)
    at = 0
    for i, piece in enumerate(pieces):
        window = call(
            functools.partial(arrived_kernel, at),
            "arrived%d" % i,
            sds((rows, tile, 3 * width), F32),
            (VMEM,) * 4 + (pl.ANY,),
            pl.ANY,
            [VMEM((2, tall, piece), F32), pltpu.SemaphoreType.DMA((2 * rows * piece // 256,))],
            1024,
            1024,
            {4: 0},
        )(m_hi, m_lo, before[i], after[i], window)
        at += piece
    return (product, window)


def solution(mesh):
    whole = P(("parts", "line", "cross"))
    return jax.shard_map(
        shards,
        mesh=mesh,
        in_specs=(whole,) * 7,
        out_specs=(whole, whole),
        check_vma=False,
    )
```

```python
import functools

import jax
import jax.numpy as jnp
from jax import lax
from jax.experimental import pallas as pl
from jax.experimental.pallas import tpu as pltpu
from jax.sharding import PartitionSpec as P

LANES = 128
F32 = jnp.float32
BF16 = jnp.bfloat16
VMEM = pltpu.VMEM
SMEM = pltpu.SMEM


AXES = ("parts", "line", "cross")


def permute(x, target):
    parts, line, cross = (lax.axis_size(axis) for axis in AXES)
    flat = lambda p, g, c: (p % parts * line + g % line) * cross + c
    places = [(p, g, c) for p in range(parts) for g in range(line) for c in range(cross)]
    return lax.ppermute(x, AXES, [(flat(*place), flat(*target(*place))) for place in places])


def rotate(x, by):
    return permute(x, lambda p, g, c: (p, g + by, c))


def ring_order(count):
    return list(range(0, count, 2))[:1] + list(range(1, count, 2)) + list(range(0, count, 2))[:0:-1]


def pass_on(x, by, parity=None):
    order = ring_order(lax.axis_size("cross"))
    after = {d: order[(i + by) % len(order)] for i, d in enumerate(order)}
    return permute(
        x,
        lambda p, g, c: (p, g, after[c]) if parity in (None, g % 2) else (p + 1, g, c),
    )


def parity_here():
    return lax.rem(lax.axis_index("line"), 2)


def shard_of(step):
    order = ring_order(lax.axis_size("cross"))
    me = lax.axis_index("cross")
    owner = jnp.int32(0)
    for i, d in enumerate(order):
        owner = jnp.where(me == d, order[i - step], owner)
    return owner


def fill_table(table, columns, counts):
    rows, width = table.shape
    for r in range(rows):
        for c in range(width):
            table[r, c] = 0
        for slot in range(columns.shape[1]):

            @pl.when(slot < counts[r])
            def _(r=r, slot=slot):
                table[r, columns[r, slot]] = slot + 1


def table_kernel(columns, counts, table):
    fill_table(table, columns, counts)


def split(v):
    hi = v.astype(BF16)
    return hi, (v - hi.astype(F32)).astype(BF16)


def low_lanes(rows):
    return lax.broadcasted_iota(jnp.int32, (rows, LANES), 1) < LANES // 2


def block_at(row_ref, code, upper):
    slot = jnp.maximum(code - 1, 0)
    v = row_ref[:, pl.ds(pl.multiple_of((slot >> 1) * LANES, LANES), LANES)]
    v = jnp.where((slot & 1) != upper, pltpu.roll(v, LANES // 2, 1), v)
    return jnp.where(code > 0, v, jnp.zeros_like(v))


def pair_at(row_ref, table, r, pair):
    v0 = block_at(row_ref, table[r, 2 * pair], 0)
    v1 = block_at(row_ref, table[r, 2 * pair + 1], 1)
    return jnp.where(low_lanes(v0.shape[0]), v0, v1)


def densify_half(chunk, table, half, b, first=0):
    tile = chunk.shape[1]
    for r in range(2):
        for pair in range(b.shape[1] // LANES):
            hi, lo = split(pair_at(chunk.at[r], table, 2 * half + r, first + pair))
            lanes = slice(pair * LANES, (pair + 1) * LANES)
            b[r * tile : (r + 1) * tile, lanes] = hi
            b[(2 + r) * tile : (3 + r) * tile, lanes] = lo


def times_half(a, b, lanes):
    depth = b.shape[0]
    return jnp.dot(a[:, :depth], b[:, lanes], preferred_element_type=F32) + jnp.dot(
        a[:, depth:], b[: depth // 2, lanes], preferred_element_type=F32
    )


def lane_blocks(width, step=256):
    return [slice(i, i + step) for i in range(0, width, step)]


def first_kernel(
    ham_cols, ham_count, dens_table, ham, dens, a, acc, ham_table, ham_here, b, sems
):
    rows, tile, _ = ham.shape
    copies = [
        pltpu.make_async_copy(ham.at[q], ham_here.at[q], sems.at[q]) for q in range(rows)
    ]
    for copy in copies:
        copy.start()
    fill_table(ham_table, ham_cols, ham_count)
    for q in range(rows):
        copies[q].wait()
        for pair in range(ham_table.shape[1] // 2):
            hi, lo = split(pair_at(ham_here.at[q], ham_table, q, pair))
            a[pair, q * tile : (q + 1) * tile, 0:LANES] = hi
            a[pair, q * tile : (q + 1) * tile, LANES : 2 * LANES] = hi
            a[pair, q * tile : (q + 1) * tile, 2 * LANES : 3 * LANES] = lo
    for h in range(rows // 2):
        densify_half(dens.at[pl.ds(2 * h, 2)], dens_table, h, b)
        pair = shard_of(0) * (rows // 2) + h
        for lanes in lane_blocks(acc.shape[1]):
            part = times_half(a[pair], b, lanes)
            acc[:, lanes] = part if h == 0 else acc[:, lanes] + part


def add_shard(step, first, dens_table, a, acc_in, shard, out, b):
    per_shard = dens_table.shape[0] // 2
    for half in range(per_shard):
        densify_half(shard.at[pl.ds(2 * half, 2)], dens_table, half, b, first // LANES)
        pair = shard_of(step) * per_shard + half
        for lanes in lane_blocks(out.shape[1]):
            if half == 0:
                before = acc_in[:, first + lanes.start : first + lanes.stop]
            else:
                before = out[:, lanes]
            out[:, lanes] = before + times_half(a[pair], b, lanes)


def add_kernel(step, dens_table, a, acc_in, even, odd, acc, b):
    for parity, shard in enumerate((even, odd)):

        @pl.when(parity_here() == parity)
        def _(shard=shard):
            add_shard(step, 0, dens_table, a, acc_in, shard, acc, b)


def even_kernel(step, dens_table, a, acc_in, shard, out, b):
    @pl.when(parity_here() == 0)
    def _():
        add_shard(step, 0, dens_table, a, acc_in, shard, out, b)


def odd_kernel(step, dens_table, a, acc_in, shard, even, *rest):
    outs, b = rest[:-1], rest[-1]
    piece = outs[0].shape[1]
    for i, out in enumerate(outs):

        @pl.when(parity_here() == 1)
        def _(i=i, out=out):
            add_shard(step, i * piece, dens_table, a, acc_in, shard, out, b)

        @pl.when(parity_here() == 0)
        def _(i=i, out=out):
            out[...] = even[:, i * piece : (i + 1) * piece]


def margin_kernel(over, before, after, hi_out, lo_out):
    rows, tile, _ = over.shape
    wide = rows * tile
    for s, (ref, start) in enumerate(((before, 0), (over, wide), (after, 0))):
        for j in range(rows):
            for pair in range(rows // 2):
                at = start + j * tile
                lanes = slice(at // LANES * LANES, at // LANES * LANES + LANES)
                v0, v1 = ref[2 * pair, :, lanes], ref[2 * pair + 1, :, lanes]
                if at % LANES == 0:
                    v1 = pltpu.roll(v1, LANES // 2, 1)
                else:
                    v0 = pltpu.roll(v0, LANES // 2, 1)
                hi, lo = split(jnp.where(low_lanes(tile), v0, v1))
                to = slice(pair * LANES, (pair + 1) * LANES)
                hi_out[s, j * tile : (j + 1) * tile, to] = hi
                lo_out[s, j * tile : (j + 1) * tile, to] = lo


def weighted(m_hi, m_lo, s, p, store):
    for lanes in lane_blocks(p.shape[1]):
        hi, lo = split(p[:, lanes])
        store(
            lanes,
            jnp.dot(m_hi[s], hi, preferred_element_type=F32)
            + jnp.dot(m_hi[s], lo, preferred_element_type=F32)
            + jnp.dot(m_lo[s], hi, preferred_element_type=F32),
        )


def own_kernel(m_hi, m_lo, *rest):
    parts, (product, window, term, sems) = rest[:-4], rest[-4:]
    rows, tile, width = product.shape
    step = width // len(parts)
    copies = []
    for i, part in enumerate(parts):
        for q in range(rows):
            copies.append(
                pltpu.make_async_copy(
                    part.at[pl.ds(q * tile, tile)],
                    product.at[q, :, pl.ds(i * step, step)],
                    sems.at[i, q],
                )
            )
            copies[-1].start()
    for i, part in enumerate(parts):

        def store(lanes, v, at=i * step):
            term[:, at + lanes.start : at + lanes.stop] = v

        weighted(m_hi, m_lo, 1, part, store)
    for q in range(rows):
        copies.append(
            pltpu.make_async_copy(
                term.at[pl.ds(q * tile, tile)],
                window.at[q, :, pl.ds(width, width)],
                sems.at[len(parts), q],
            )
        )
        copies[-1].start()
    for copy in copies:
        copy.wait()


def arrived_kernel(s, at, parity, m_hi, m_lo, p, window_in, window, term, sems):
    rows, tile, triple = window.shape
    start = s * triple // 3 + at

    def arrived():
        copies = []

        def store(lanes, v):
            term[:, lanes] = v
            for q in range(rows):
                to = pl.ds(start + lanes.start, lanes.stop - lanes.start)
                copies.append(
                    pltpu.make_async_copy(
                        term.at[pl.ds(q * tile, tile), lanes],
                        window.at[q, :, to],
                        sems.at[len(copies)],
                    )
                )
                copies[-1].start()

        weighted(m_hi, m_lo, s, p, store)
        for copy in copies:
            copy.wait()

    if parity is None:
        arrived()
    else:
        pl.when(parity_here() == parity)(arrived)


def call(kernel, name, out_shape, in_spaces, out_spaces, scratch, flops, moved, aliases=None):
    return pl.pallas_call(
        kernel,
        name=name,
        out_shape=out_shape,
        in_specs=[pl.BlockSpec(memory_space=s) for s in in_spaces],
        out_specs=jax.tree.map(lambda s: pl.BlockSpec(memory_space=s), out_spaces),
        scratch_shapes=scratch,
        input_output_aliases=aliases or {},
        cost_estimate=pl.CostEstimate(flops=flops, bytes_accessed=moved, transcendentals=0),
        compiler_params=pltpu.CompilerParams(vmem_limit_bytes=24 << 20),
    )


def shards(ham_tiles, ham_cols, ham_count, dens_tiles, dens_cols, dens_count, over_tiles):
    count = lax.axis_size("cross")
    rows, tile, _ = ham_tiles.shape
    blocks = rows * count
    width = blocks * tile
    tall = rows * tile
    per_shard = rows // 2
    sds = jax.ShapeDtypeStruct

    even = pass_on(dens_tiles, 1, 0)
    table = call(
        table_kernel,
        "table",
        sds((rows, blocks), jnp.int32),
        (SMEM, SMEM),
        SMEM,
        [],
        1024,
        1024,
    )(dens_cols, dens_count)
    tables = [pass_on(table, step) for step in range(1, count)]
    dens_late, table = lax.optimization_barrier((dens_tiles, table))
    odd = pass_on(dens_late, 1, 1)
    b_scratch = [VMEM((4 * tile, width), BF16)]
    for step in range(1, count):
        now = (even, odd)
        if step == 1:
            ham_tiles, even = lax.optimization_barrier((ham_tiles, even))
            a, acc = call(
                first_kernel,
                "first",
                (sds((blocks // 2, tall, 3 * LANES), BF16), sds((tall, width), F32)),
                (SMEM, SMEM, SMEM, pl.ANY, VMEM),
                (VMEM, VMEM),
                [pltpu.SMEM((rows, blocks), jnp.int32), VMEM(ham_tiles.shape, F32)]
                + b_scratch
                + [pltpu.SemaphoreType.DMA((rows,))],
                1 << 20,
                1 << 20,
            )(
                ham_cols,
                ham_count,
                table,
                pltpu.with_memory_space_constraint(ham_tiles, pltpu.HBM),
                dens_tiles,
            )
            odd, acc, over_tiles, *tables = lax.optimization_barrier(
                (odd, acc, over_tiles, *tables)
            )
            over_before = rotate(over_tiles[:, :, 2 * tall :], 1)
            over_after = rotate(over_tiles[:, :, :tall], -1)
            m_hi, m_lo = call(
                margin_kernel,
                "margin",
                (sds((3, tall, tall), BF16),) * 2,
                (VMEM,) * 3,
                (VMEM, VMEM),
                [],
                1 << 20,
                1 << 20,
            )(over_tiles, over_before, over_after)
        else:
            even, acc = lax.optimization_barrier((even, acc))
        if step == 2:
            odd, m_hi, m_lo = lax.optimization_barrier((odd, m_hi, m_lo))
        now = (even, odd)
        if step == count - 1:
            break
        even, odd = pass_on(even, 1, 0), pass_on(odd, 1, 1)
        acc = call(
            functools.partial(add_kernel, step),
            "add%d" % step,
            sds((tall, width), F32),
            (SMEM,) + (VMEM,) * 4,
            VMEM,
            b_scratch,
            1 << 20,
            1 << 20,
        )(tables[step - 1], a, acc, *now)

    sides = 2
    piece = width // sides
    even_part = call(
        functools.partial(even_kernel, count - 1),
        "even",
        sds((tall, width), F32),
        (SMEM, VMEM, VMEM, VMEM),
        VMEM,
        b_scratch,
        1024,
        1024,
    )(tables[-1], a, acc, even)
    parts = call(
        functools.partial(odd_kernel, count - 1),
        "odd",
        [sds((tall, piece), F32)] * sides,
        (SMEM, VMEM, VMEM, VMEM, VMEM),
        [VMEM] * sides,
        [VMEM((4 * tile, piece), BF16)],
        1024,
        1024,
    )(tables[-1], a, acc, odd, even_part)
    mate = lambda p, g, c: (p, g + 1 - g % 2 * 2, c)
    after = permute(even_part, lambda p, g, c: mate(p, g, c) if g % 2 else (p, g - 1, c))
    mates = [permute(part, mate) for part in parts]
    befores = [rotate(part, 1) for part in parts]
    product, window = call(
        own_kernel,
        "own",
        (sds((rows, tile, width), F32), sds((rows, tile, 3 * width), F32)),
        (VMEM,) * (2 + sides),
        (pl.ANY, pl.ANY),
        [VMEM((tall, width), F32), pltpu.SemaphoreType.DMA((sides + 1, rows))],
        1024,
        1024,
    )(m_hi, m_lo, *parts)
    steps = [(2, 0, 1, after)]
    steps += [(2, i * piece, 0, p) for i, p in enumerate(mates)]
    steps += [(0, i * piece, None, p) for i, p in enumerate(befores)]
    for i, (side, at, parity, p) in enumerate(steps):
        window = call(
            functools.partial(arrived_kernel, side, at, parity),
            "arrived%d" % i,
            sds((rows, tile, 3 * width), F32),
            (VMEM,) * 3 + (pl.ANY,),
            pl.ANY,
            [VMEM(p.shape, F32), pltpu.SemaphoreType.DMA((rows * p.shape[1] // 256,))],
            1024,
            1024,
            {3: 0},
        )(m_hi, m_lo, p, window)
    return (product, window)


def solution(mesh):
    whole = P(AXES)
    return jax.shard_map(
        shards,
        mesh=mesh,
        in_specs=(whole,) * 7,
        out_specs=(whole, whole),
        check_vma=False,
    )
```

```python
import functools

import jax
import jax.numpy as jnp
from jax import lax
from jax.experimental import pallas as pl
from jax.experimental.pallas import tpu as pltpu
from jax.sharding import PartitionSpec as P

LANES = 128
F32 = jnp.float32
BF16 = jnp.bfloat16
VMEM = pltpu.VMEM
SMEM = pltpu.SMEM


AXES = ("parts", "line", "cross")


def permute(x, target):
    parts, line, cross = (lax.axis_size(axis) for axis in AXES)
    flat = lambda p, g, c: (p % parts * line + g % line) * cross + c
    places = [(p, g, c) for p in range(parts) for g in range(line) for c in range(cross)]
    return lax.ppermute(x, AXES, [(flat(*place), flat(*target(*place))) for place in places])


def rotate(x, by):
    return permute(x, lambda p, g, c: (p, g + by, c))


def ring_order(count):
    return list(range(0, count, 2))[:1] + list(range(1, count, 2)) + list(range(0, count, 2))[:0:-1]


def pass_on(x, by, parity=None):
    order = ring_order(lax.axis_size("cross"))
    after = {d: order[(i + by) % len(order)] for i, d in enumerate(order)}
    return permute(
        x,
        lambda p, g, c: (p, g, after[c]) if parity in (None, g % 2) else (p + 1, g, c),
    )


def parity_here():
    return lax.rem(lax.axis_index("line"), 2)


def shard_of(step):
    order = ring_order(lax.axis_size("cross"))
    me = lax.axis_index("cross")
    owner = jnp.int32(0)
    for i, d in enumerate(order):
        owner = jnp.where(me == d, order[i - step], owner)
    return owner


def fill_table(table, columns, counts):
    rows, width = table.shape
    for r in range(rows):
        for c in range(width):
            table[r, c] = 0
        for slot in range(columns.shape[1]):

            @pl.when(slot < counts[r])
            def _(r=r, slot=slot):
                table[r, columns[r, slot]] = slot + 1


def table_kernel(columns, counts, table):
    fill_table(table, columns, counts)


def split(v):
    hi = v.astype(BF16)
    return hi, (v - hi.astype(F32)).astype(BF16)


def low_lanes(rows):
    return lax.broadcasted_iota(jnp.int32, (rows, LANES), 1) < LANES // 2


def block_at(row_ref, code, upper):
    slot = jnp.maximum(code - 1, 0)
    v = row_ref[:, pl.ds(pl.multiple_of((slot >> 1) * LANES, LANES), LANES)]
    v = jnp.where((slot & 1) != upper, pltpu.roll(v, LANES // 2, 1), v)
    return jnp.where(code > 0, v, jnp.zeros_like(v))


def pair_at(row_ref, table, r, pair):
    v0 = block_at(row_ref, table[r, 2 * pair], 0)
    v1 = block_at(row_ref, table[r, 2 * pair + 1], 1)
    return jnp.where(low_lanes(v0.shape[0]), v0, v1)


def densify_half(chunk, table, half, b, first=0):
    tile = chunk.shape[1]
    for r in range(2):
        for pair in range(b.shape[1] // LANES):
            hi, lo = split(pair_at(chunk.at[r], table, 2 * half + r, first + pair))
            lanes = slice(pair * LANES, (pair + 1) * LANES)
            b[r * tile : (r + 1) * tile, lanes] = hi
            b[(2 + r) * tile : (3 + r) * tile, lanes] = lo


def times_half(a, b, lanes):
    depth = b.shape[0]
    return jnp.dot(a[:, :depth], b[:, lanes], preferred_element_type=F32) + jnp.dot(
        a[:, depth:], b[: depth // 2, lanes], preferred_element_type=F32
    )


def lane_blocks(width, step=256):
    return [slice(i, i + step) for i in range(0, width, step)]


def ham_kernel(ham_cols, ham_count, ham, a, ham_table, ham_here, sems):
    rows, tile, _ = ham.shape
    copies = [
        pltpu.make_async_copy(ham.at[q], ham_here.at[q], sems.at[q]) for q in range(rows)
    ]
    for copy in copies:
        copy.start()
    fill_table(ham_table, ham_cols, ham_count)
    for q in range(rows):
        copies[q].wait()
        for pair in range(ham_table.shape[1] // 2):
            hi, lo = split(pair_at(ham_here.at[q], ham_table, q, pair))
            a[pair, q * tile : (q + 1) * tile, 0:LANES] = hi
            a[pair, q * tile : (q + 1) * tile, LANES : 2 * LANES] = hi
            a[pair, q * tile : (q + 1) * tile, 2 * LANES : 3 * LANES] = lo


def add_shard(step, first, dens_table, a, acc_in, shard, out, b):
    per_shard = dens_table.shape[0] // 2
    for half in range(per_shard):
        densify_half(shard.at[pl.ds(2 * half, 2)], dens_table, half, b, first // LANES)
        pair = shard_of(step) * per_shard + half
        for lanes in lane_blocks(out.shape[1]):
            part = times_half(a[pair], b, lanes)
            if half > 0:
                part += out[:, lanes]
            elif acc_in is not None:
                part += acc_in[:, first + lanes.start : first + lanes.stop]
            out[:, lanes] = part


def own_shard_kernel(dens_table, a, dens, acc, b):
    add_shard(0, 0, dens_table, a, None, dens, acc, b)


def add_kernel(step, dens_table, a, acc_in, even, odd, acc, b):
    for parity, shard in enumerate((even, odd)):

        @pl.when(parity_here() == parity)
        def _(shard=shard):
            add_shard(step, 0, dens_table, a, acc_in, shard, acc, b)


def margin_kernel(over, hi_out, lo_out):
    rows, tile, _ = over.shape
    for s in range(3):
        for j in range(rows):
            for pair in range(rows // 2):
                at = (s * rows + j) * tile
                lanes = slice(at // LANES * LANES, at // LANES * LANES + LANES)
                v0, v1 = over[2 * pair, :, lanes], over[2 * pair + 1, :, lanes]
                if at % LANES == 0:
                    v1 = pltpu.roll(v1, LANES // 2, 1)
                else:
                    v0 = pltpu.roll(v0, LANES // 2, 1)
                hi, lo = split(jnp.where(low_lanes(tile), v0, v1))
                to = slice(pair * LANES, (pair + 1) * LANES)
                hi_out[s, j * tile : (j + 1) * tile, to] = hi
                lo_out[s, j * tile : (j + 1) * tile, to] = lo


def store_at(out):
    def weigh(m_hi, m_lo, s, p):
        for lanes in lane_blocks(p.shape[1]):
            hi, lo = split(p[:, lanes])
            out[:, lanes] = (
                jnp.dot(m_hi[s], hi, preferred_element_type=F32)
                + jnp.dot(m_hi[s], lo, preferred_element_type=F32)
                + jnp.dot(m_lo[s], hi, preferred_element_type=F32)
            )

    return weigh


def even_kernel(step, dens_table, a, acc_in, shard, m_hi, m_lo, p, prev_term, b):
    @pl.when(parity_here() == 0)
    def _():
        add_shard(step, 0, dens_table, a, acc_in, shard, p, b)
        store_at(prev_term)(m_hi, m_lo, 0, p)


def odd_kernel(step, dens_table, a, acc_in, shard, m_hi, m_lo, even_p, p, prev_term, *rest):
    next_terms, b = rest[:-1], rest[-1]

    @pl.when(parity_here() == 1)
    def _():
        add_shard(step, 0, dens_table, a, acc_in, shard, p, b)

    @pl.when(parity_here() == 0)
    def _():
        p[...] = even_p[...]

    piece = next_terms[0].shape[1]
    for i, out in enumerate(next_terms):
        store_at(out)(m_hi, m_lo, 2, p.at[:, pl.ds(i * piece, piece)])

    @pl.when(parity_here() == 1)
    def _():
        store_at(prev_term)(m_hi, m_lo, 0, p)


def own_kernel(m_hi, m_lo, p, product, window, term, sems):
    rows, tile, width = product.shape

    def start(ref, out, at, kind):
        for q in range(rows):
            copies.append(
                pltpu.make_async_copy(
                    ref.at[pl.ds(q * tile, tile)], out.at[q, :, pl.ds(at, width)], sems.at[kind, q]
                )
            )
            copies[-1].start()

    copies = []
    start(p, product, 0, 0)
    store_at(term)(m_hi, m_lo, 1, p)
    start(term, window, width, 1)
    for copy in copies:
        copy.wait()


def arrived_kernel(at, parity, term, window_in, window, sems):
    rows, tile, _ = window.shape

    def move():
        copies = [
            pltpu.make_async_copy(
                term.at[pl.ds(q * tile, tile)],
                window.at[q, :, pl.ds(at, term.shape[1])],
                sems.at[q],
            )
            for q in range(rows)
        ]
        for copy in copies:
            copy.start()
        for copy in copies:
            copy.wait()

    if parity is None:
        move()
    else:
        pl.when(parity_here() == parity)(move)


def call(kernel, name, out_shape, in_spaces, out_spaces, scratch, flops, moved, aliases=None):
    return pl.pallas_call(
        kernel,
        name=name,
        out_shape=out_shape,
        in_specs=[pl.BlockSpec(memory_space=s) for s in in_spaces],
        out_specs=jax.tree.map(lambda s: pl.BlockSpec(memory_space=s), out_spaces),
        scratch_shapes=scratch,
        input_output_aliases=aliases or {},
        cost_estimate=pl.CostEstimate(flops=flops, bytes_accessed=moved, transcendentals=0),
        compiler_params=pltpu.CompilerParams(vmem_limit_bytes=24 << 20),
    )


def shards(ham_tiles, ham_cols, ham_count, dens_tiles, dens_cols, dens_count, over_tiles):
    count = lax.axis_size("cross")
    rows, tile, _ = ham_tiles.shape
    blocks = rows * count
    width = blocks * tile
    tall = rows * tile
    per_shard = rows // 2
    sds = jax.ShapeDtypeStruct

    ham_cols, ham_count, dens_cols, dens_count, ham_tiles = (
        pltpu.with_memory_space_constraint(x, pltpu.HBM)
        for x in (ham_cols, ham_count, dens_cols, dens_count, ham_tiles)
    )
    even = pass_on(dens_tiles, 1, 0)
    m_hi, m_lo = call(
        margin_kernel,
        "margin",
        (sds((3, tall, tall), BF16),) * 2,
        (VMEM,),
        (VMEM, VMEM),
        [],
        1 << 20,
        1 << 20,
    )(over_tiles)
    table = call(
        table_kernel,
        "table",
        sds((rows, blocks), jnp.int32),
        (SMEM, SMEM),
        SMEM,
        [],
        1024,
        1024,
    )(dens_cols, dens_count)
    dens_late, table = lax.optimization_barrier((dens_tiles, table))
    odd = pass_on(dens_late, 1, 1)
    tables = [pass_on(table, 1)]
    b_scratch = [VMEM((4 * tile, width), BF16)]
    evens, odds = [even], [odd]
    acc = None
    for step in range(1, count):
        even, odd = evens[-1], odds[-1]
        if step == 1:
            even, ham_tiles, table = lax.optimization_barrier((even, ham_tiles, table))
            tables += [pass_on(table, ahead) for ahead in range(2, count)]
            a = call(
                ham_kernel,
                "ham",
                sds((blocks // 2, tall, 3 * LANES), BF16),
                (SMEM, SMEM, pltpu.HBM),
                VMEM,
                [
                    pltpu.SMEM((rows, blocks), jnp.int32),
                    VMEM(ham_tiles.shape, F32),
                    pltpu.SemaphoreType.DMA((rows,)),
                ],
                1 << 20,
                1 << 20,
            )(ham_cols, ham_count, ham_tiles)
            odd, a, dens_own = lax.optimization_barrier((odd, a, dens_tiles))
            acc = call(
                own_shard_kernel,
                "own_shard",
                sds((tall, width), F32),
                (SMEM, VMEM, VMEM),
                VMEM,
                b_scratch,
                1 << 20,
                1 << 20,
            )(table, a, dens_own)
        else:
            even, acc, *tables = lax.optimization_barrier((even, acc, *tables))
            acc = call(
                functools.partial(add_kernel, step - 1),
                "add%d" % (step - 1),
                sds((tall, width), F32),
                (SMEM,) + (VMEM,) * 4,
                VMEM,
                b_scratch,
                1 << 20,
                1 << 20,
            )(tables[step - 2], a, acc, evens[-2], odds[-2])
            if step < count - 1:
                odd, acc = lax.optimization_barrier((odd, acc))
            if step == 2:
                odd, m_hi, m_lo = lax.optimization_barrier((odd, m_hi, m_lo))
        evens[-1], odds[-1] = even, odd
        if step < count - 1:
            evens.append(pass_on(even, 1, 0))
            odds.append(pass_on(odd, 1, 1))

    sides = 2
    piece = width // sides
    whole = sds((tall, width), F32)
    even_p, even_term = call(
        functools.partial(even_kernel, count - 1),
        "even",
        (whole, whole),
        (SMEM,) + (VMEM,) * 5,
        (VMEM, VMEM),
        b_scratch,
        1024,
        1024,
    )(tables[-1], a, acc, evens[-1], m_hi, m_lo)
    p, odd_term, *next_terms = call(
        functools.partial(odd_kernel, count - 1),
        "odd",
        [whole, whole] + [sds((tall, piece), F32)] * sides,
        (SMEM,) + (VMEM,) * 6,
        [VMEM] * (2 + sides),
        b_scratch,
        1024,
        1024,
    )(tables[-1], a, acc, odds[-1], m_hi, m_lo, even_p)
    mate = lambda p, g, c: (p, g + 1 - g % 2 * 2, c)
    over_x = permute(even_term, lambda p, g, c: mate(p, g, c) if g % 2 else (p, g - 1, c))
    between = permute(odd_term, mate)
    befores = [rotate(term, 1) for term in next_terms]
    product, window = call(
        own_kernel,
        "own",
        (sds((rows, tile, width), F32), sds((rows, tile, 3 * width), F32)),
        (VMEM,) * 3,
        (pl.ANY, pl.ANY),
        [VMEM((tall, width), F32), pltpu.SemaphoreType.DMA((2, rows))],
        1024,
        1024,
    )(m_hi, m_lo, p)
    steps = [(2 * width, 1, over_x), (2 * width, 0, between)]
    steps += [(i * piece, None, term) for i, term in enumerate(befores)]
    for i, (at, parity, term) in enumerate(steps):
        window = call(
            functools.partial(arrived_kernel, at, parity),
            "arrived%d" % i,
            sds((rows, tile, 3 * width), F32),
            (VMEM, pl.ANY),
            pl.ANY,
            [pltpu.SemaphoreType.DMA((rows,))],
            1024,
            1024,
            {1: 0},
        )(term, window)
    return (product, window)


def solution(mesh):
    whole = P(AXES)
    return jax.shard_map(
        shards,
        mesh=mesh,
        in_specs=(whole,) * 7,
        out_specs=(whole, whole),
        check_vma=False,
    )
```

```python
import functools

import jax
import jax.numpy as jnp
from jax import lax
from jax.experimental import pallas as pl
from jax.experimental.pallas import tpu as pltpu
from jax.sharding import PartitionSpec as P

LANES = 128
F32 = jnp.float32
BF16 = jnp.bfloat16
VMEM = pltpu.VMEM
SMEM = pltpu.SMEM


AXES = ("parts", "line", "cross")


def permute(x, target):
    parts, line, cross = (lax.axis_size(axis) for axis in AXES)
    flat = lambda p, g, c: (p % parts * line + g % line) * cross + c
    places = [(p, g, c) for p in range(parts) for g in range(line) for c in range(cross)]
    return lax.ppermute(x, AXES, [(flat(*place), flat(*target(*place))) for place in places])


def rotate(x, by):
    return permute(x, lambda p, g, c: (p, g + by, c))


def ring_order(count):
    return list(range(0, count, 2))[:1] + list(range(1, count, 2)) + list(range(0, count, 2))[:0:-1]


def pass_on(x, by, parity=None):
    order = ring_order(lax.axis_size("cross"))
    after = {d: order[(i + by) % len(order)] for i, d in enumerate(order)}
    return permute(
        x,
        lambda p, g, c: (p, g, after[c]) if parity in (None, g % 2) else (p + 1, g, c),
    )


def parity_here():
    return lax.rem(lax.axis_index("line"), 2)


def shard_of(step):
    order = ring_order(lax.axis_size("cross"))
    me = lax.axis_index("cross")
    owner = jnp.int32(0)
    for i, d in enumerate(order):
        owner = jnp.where(me == d, order[i - step], owner)
    return owner


def fill_table(table, columns, counts):
    rows, width = table.shape
    for r in range(rows):
        for c in range(width):
            table[r, c] = 0
        for slot in range(columns.shape[1]):

            @pl.when(slot < counts[r])
            def _(r=r, slot=slot):
                table[r, columns[r, slot]] = slot + 1


def table_kernel(columns, counts, table):
    fill_table(table, columns, counts)


def split(v):
    hi = v.astype(BF16)
    return hi, (v - hi.astype(F32)).astype(BF16)


def low_lanes(rows):
    return lax.broadcasted_iota(jnp.int32, (rows, LANES), 1) < LANES // 2


def block_at(row_ref, code, upper):
    slot = jnp.maximum(code - 1, 0)
    v = row_ref[:, pl.ds(pl.multiple_of((slot >> 1) * LANES, LANES), LANES)]
    v = jnp.where((slot & 1) != upper, pltpu.roll(v, LANES // 2, 1), v)
    return jnp.where(code > 0, v, jnp.zeros_like(v))


def pair_at(row_ref, table, r, pair):
    v0 = block_at(row_ref, table[r, 2 * pair], 0)
    v1 = block_at(row_ref, table[r, 2 * pair + 1], 1)
    return jnp.where(low_lanes(v0.shape[0]), v0, v1)


def densify_half(chunk, table, half, b, first=0):
    tile = chunk.shape[1]
    for r in range(2):
        for pair in range(b.shape[1] // LANES):
            hi, lo = split(pair_at(chunk.at[r], table, 2 * half + r, first + pair))
            lanes = slice(pair * LANES, (pair + 1) * LANES)
            b[r * tile : (r + 1) * tile, lanes] = hi
            b[(2 + r) * tile : (3 + r) * tile, lanes] = lo


def times_half(a, b, lanes):
    depth = b.shape[0]
    return jnp.dot(a[:, :depth], b[:, lanes], preferred_element_type=F32) + jnp.dot(
        a[:, depth:], b[: depth // 2, lanes], preferred_element_type=F32
    )


def lane_blocks(width, step=256):
    return [slice(i, i + step) for i in range(0, width, step)]


def ham_kernel(ham_cols, ham_count, ham, a, ham_table, ham_here, sems):
    rows, tile, _ = ham.shape
    copies = [
        pltpu.make_async_copy(ham.at[q], ham_here.at[q], sems.at[q]) for q in range(rows)
    ]
    for copy in copies:
        copy.start()
    fill_table(ham_table, ham_cols, ham_count)
    for q in range(rows):
        copies[q].wait()
        for pair in range(ham_table.shape[1] // 2):
            hi, lo = split(pair_at(ham_here.at[q], ham_table, q, pair))
            a[pair, q * tile : (q + 1) * tile, 0:LANES] = hi
            a[pair, q * tile : (q + 1) * tile, LANES : 2 * LANES] = hi
            a[pair, q * tile : (q + 1) * tile, 2 * LANES : 3 * LANES] = lo


def add_shard(step, first, dens_table, a, acc_in, shard, out, b):
    per_shard = dens_table.shape[0] // 2
    for half in range(per_shard):
        densify_half(shard.at[pl.ds(2 * half, 2)], dens_table, half, b, first // LANES)
        pair = shard_of(step) * per_shard + half
        for lanes in lane_blocks(out.shape[1]):
            part = times_half(a[pair], b, lanes)
            if half > 0:
                part += out[:, lanes]
            elif acc_in is not None:
                part += acc_in[:, first + lanes.start : first + lanes.stop]
            out[:, lanes] = part


def own_shard_kernel(dens_table, a, dens, acc, b):
    add_shard(0, 0, dens_table, a, None, dens, acc, b)


def add_kernel(step, dens_table, a, acc_in, even, odd, acc, b):
    for parity, shard in enumerate((even, odd)):

        @pl.when(parity_here() == parity)
        def _(shard=shard):
            add_shard(step, 0, dens_table, a, acc_in, shard, acc, b)


def margin_kernel(over, hi_out, lo_out):
    rows, tile, _ = over.shape
    for s in range(3):
        for j in range(rows):
            for pair in range(rows // 2):
                at = (s * rows + j) * tile
                lanes = slice(at // LANES * LANES, at // LANES * LANES + LANES)
                v0, v1 = over[2 * pair, :, lanes], over[2 * pair + 1, :, lanes]
                if at % LANES == 0:
                    v1 = pltpu.roll(v1, LANES // 2, 1)
                else:
                    v0 = pltpu.roll(v0, LANES // 2, 1)
                hi, lo = split(jnp.where(low_lanes(tile), v0, v1))
                to = slice(pair * LANES, (pair + 1) * LANES)
                hi_out[s, j * tile : (j + 1) * tile, to] = hi
                lo_out[s, j * tile : (j + 1) * tile, to] = lo


def store_at(out):
    def weigh(m_hi, m_lo, s, p):
        for lanes in lane_blocks(p.shape[1]):
            hi, lo = split(p[:, lanes])
            out[:, lanes] = (
                jnp.dot(m_hi[s], hi, preferred_element_type=F32)
                + jnp.dot(m_hi[s], lo, preferred_element_type=F32)
                + jnp.dot(m_lo[s], hi, preferred_element_type=F32)
            )

    return weigh


def even_kernel(step, dens_table, a, acc_in, shard, m_hi, m_lo, p, prev_term, b):
    @pl.when(parity_here() == 0)
    def _():
        add_shard(step, 0, dens_table, a, acc_in, shard, p, b)
        store_at(prev_term)(m_hi, m_lo, 0, p)


def odd_kernel(step, dens_table, a, acc_in, shard, m_hi, m_lo, even_p, p, prev_term, *rest):
    next_terms, b = rest[:-1], rest[-1]

    @pl.when(parity_here() == 1)
    def _():
        add_shard(step, 0, dens_table, a, acc_in, shard, p, b)

    @pl.when(parity_here() == 0)
    def _():
        p[...] = even_p[...]

    piece = next_terms[0].shape[1]
    for i, out in enumerate(next_terms):
        store_at(out)(m_hi, m_lo, 2, p.at[:, pl.ds(i * piece, piece)])

    @pl.when(parity_here() == 1)
    def _():
        store_at(prev_term)(m_hi, m_lo, 0, p)


def own_kernel(m_hi, m_lo, p, product, window, term, sems):
    rows, tile, width = product.shape

    def start(ref, out, at, kind):
        for q in range(rows):
            copies.append(
                pltpu.make_async_copy(
                    ref.at[pl.ds(q * tile, tile)], out.at[q, :, pl.ds(at, width)], sems.at[kind, q]
                )
            )
            copies[-1].start()

    copies = []
    start(p, product, 0, 0)
    store_at(term)(m_hi, m_lo, 1, p)
    start(term, window, width, 1)
    for copy in copies:
        copy.wait()


def arrived_kernel(at, parity, term, window_in, window, sems):
    rows, tile, _ = window.shape

    def move():
        copies = [
            pltpu.make_async_copy(
                term.at[pl.ds(q * tile, tile)],
                window.at[q, :, pl.ds(at, term.shape[1])],
                sems.at[q],
            )
            for q in range(rows)
        ]
        for copy in copies:
            copy.start()
        for copy in copies:
            copy.wait()

    if parity is None:
        move()
    else:
        pl.when(parity_here() == parity)(move)


def call(kernel, name, out_shape, in_spaces, out_spaces, scratch, flops, moved, aliases=None):
    return pl.pallas_call(
        kernel,
        name=name,
        out_shape=out_shape,
        in_specs=[pl.BlockSpec(memory_space=s) for s in in_spaces],
        out_specs=jax.tree.map(lambda s: pl.BlockSpec(memory_space=s), out_spaces),
        scratch_shapes=scratch,
        input_output_aliases=aliases or {},
        cost_estimate=pl.CostEstimate(flops=flops, bytes_accessed=moved, transcendentals=0),
        compiler_params=pltpu.CompilerParams(vmem_limit_bytes=24 << 20),
    )


def shards(ham_tiles, ham_cols, ham_count, dens_tiles, dens_cols, dens_count, over_tiles):
    count = lax.axis_size("cross")
    rows, tile, _ = ham_tiles.shape
    blocks = rows * count
    width = blocks * tile
    tall = rows * tile
    per_shard = rows // 2
    sds = jax.ShapeDtypeStruct

    ham_cols, ham_count, dens_cols, dens_count, ham_tiles = (
        pltpu.with_memory_space_constraint(x, pltpu.HBM)
        for x in (ham_cols, ham_count, dens_cols, dens_count, ham_tiles)
    )
    even = pass_on(dens_tiles, 1, 0)
    m_hi, m_lo = call(
        margin_kernel,
        "margin",
        (sds((3, tall, tall), BF16),) * 2,
        (VMEM,),
        (VMEM, VMEM),
        [],
        1024,
        1024,
    )(over_tiles)
    table = call(
        table_kernel,
        "table",
        sds((rows, blocks), jnp.int32),
        (SMEM, SMEM),
        SMEM,
        [],
        1024,
        1024,
    )(dens_cols, dens_count)
    a = call(
        ham_kernel,
        "ham",
        sds((blocks // 2, tall, 3 * LANES), BF16),
        (SMEM, SMEM, pltpu.HBM),
        VMEM,
        [
            pltpu.SMEM((rows, blocks), jnp.int32),
            VMEM(ham_tiles.shape, F32),
            pltpu.SemaphoreType.DMA((rows,)),
        ],
        1024,
        1024,
    )(ham_cols, ham_count, ham_tiles)
    dens_late, table, a = lax.optimization_barrier((dens_tiles, table, a))
    odd = pass_on(dens_late, 1, 1)
    tables = [pass_on(table, 1)]
    b_scratch = [VMEM((4 * tile, width), BF16)]
    evens, odds = [even], [odd]
    acc = None
    for step in range(1, count):
        even, odd = evens[-1], odds[-1]
        if step == 1:
            even, table = lax.optimization_barrier((even, table))
            tables += [pass_on(table, ahead) for ahead in range(2, count)]
            odd, dens_own = lax.optimization_barrier((odd, dens_tiles))
            acc = call(
                own_shard_kernel,
                "own_shard",
                sds((tall, width), F32),
                (SMEM, VMEM, VMEM),
                VMEM,
                b_scratch,
                1024,
                1024,
            )(table, a, dens_own)
        else:
            if step < count - 1:
                even, acc, *tables = lax.optimization_barrier((even, acc, *tables))
            acc = call(
                functools.partial(add_kernel, step - 1),
                "add%d" % (step - 1),
                sds((tall, width), F32),
                (SMEM,) + (VMEM,) * 4,
                VMEM,
                b_scratch,
                1024,
                1024,
            )(tables[step - 2], a, acc, evens[-2], odds[-2])
            if step < count - 1:
                odd, acc = lax.optimization_barrier((odd, acc))
            if step == 2:
                odd, m_hi, m_lo = lax.optimization_barrier((odd, m_hi, m_lo))
        evens[-1], odds[-1] = even, odd
        if step < count - 1:
            evens.append(pass_on(even, 1, 0))
            odds.append(pass_on(odd, 1, 1))

    sides = 2
    piece = width // sides
    whole = sds((tall, width), F32)
    even_p, even_term = call(
        functools.partial(even_kernel, count - 1),
        "even",
        (whole, whole),
        (SMEM,) + (VMEM,) * 5,
        (VMEM, VMEM),
        b_scratch,
        1024,
        1024,
    )(tables[-1], a, acc, evens[-1], m_hi, m_lo)
    p, odd_term, *next_terms = call(
        functools.partial(odd_kernel, count - 1),
        "odd",
        [whole, whole] + [sds((tall, piece), F32)] * sides,
        (SMEM,) + (VMEM,) * 6,
        [VMEM] * (2 + sides),
        b_scratch,
        1024,
        1024,
    )(tables[-1], a, acc, odds[-1], m_hi, m_lo, even_p)
    mate = lambda p, g, c: (p, g + 1 - g % 2 * 2, c)
    over_x = permute(even_term, lambda p, g, c: mate(p, g, c) if g % 2 else (p, g - 1, c))
    between = permute(odd_term, mate)
    befores = [rotate(term, 1) for term in next_terms]
    product, window = call(
        own_kernel,
        "own",
        (sds((rows, tile, width), F32), sds((rows, tile, 3 * width), F32)),
        (VMEM,) * 3,
        (pl.ANY, pl.ANY),
        [VMEM((tall, width), F32), pltpu.SemaphoreType.DMA((2, rows))],
        1024,
        1024,
    )(m_hi, m_lo, p)
    steps = [(2 * width, 1, over_x), (2 * width, 0, between)]
    steps += [(i * piece, None, term) for i, term in enumerate(befores)]
    for i, (at, parity, term) in enumerate(steps):
        window = call(
            functools.partial(arrived_kernel, at, parity),
            "arrived%d" % i,
            sds((rows, tile, 3 * width), F32),
            (VMEM, pl.ANY),
            pl.ANY,
            [pltpu.SemaphoreType.DMA((rows,))],
            1024,
            1024,
            {1: 0},
        )(term, window)
    return (product, window)


def solution(mesh):
    whole = P(AXES)
    return jax.shard_map(
        shards,
        mesh=mesh,
        in_specs=(whole,) * 7,
        out_specs=(whole, whole),
        check_vma=False,
    )
```

```python
import functools

import jax
import jax.numpy as jnp
from jax import lax
from jax.experimental import pallas as pl
from jax.experimental.pallas import tpu as pltpu
from jax.sharding import PartitionSpec as P

LANES = 128
F32 = jnp.float32
BF16 = jnp.bfloat16
VMEM = pltpu.VMEM
SMEM = pltpu.SMEM


AXES = ("parts", "line", "cross")


def permute(x, target):
    parts, line, cross = (lax.axis_size(axis) for axis in AXES)
    flat = lambda p, g, c: (p % parts * line + g % line) * cross + c
    places = [(p, g, c) for p in range(parts) for g in range(line) for c in range(cross)]
    return lax.ppermute(x, AXES, [(flat(*place), flat(*target(*place))) for place in places])


def rotate(x, by):
    return permute(x, lambda p, g, c: (p, g + by, c))


def ring_order(count):
    return list(range(0, count, 2))[:1] + list(range(1, count, 2)) + list(range(0, count, 2))[:0:-1]


def pass_on(x, by):
    order = ring_order(lax.axis_size("cross"))
    after = {d: order[(i + by) % len(order)] for i, d in enumerate(order)}
    return permute(x, lambda p, g, c: (p, g, after[c]))


def shard_of(step):
    order = ring_order(lax.axis_size("cross"))
    me = lax.axis_index("cross")
    owner = jnp.int32(0)
    for i, d in enumerate(order):
        owner = jnp.where(me == d, order[i - step], owner)
    return owner


def fill_table(table, columns, counts):
    rows, width = table.shape
    for r in range(rows):
        for c in range(width):
            table[r, c] = 0
        for slot in range(columns.shape[1]):

            @pl.when(slot < counts[r])
            def _(r=r, slot=slot):
                table[r, columns[r, slot]] = slot + 1


def table_kernel(columns, counts, table):
    fill_table(table, columns, counts)


def split(v):
    hi = v.astype(BF16)
    return hi, (v - hi.astype(F32)).astype(BF16)


def low_lanes(rows):
    return lax.broadcasted_iota(jnp.int32, (rows, LANES), 1) < LANES // 2


def block_at(row_ref, code, upper):
    slot = jnp.maximum(code - 1, 0)
    v = row_ref[:, pl.ds(pl.multiple_of((slot >> 1) * LANES, LANES), LANES)]
    v = jnp.where((slot & 1) != upper, pltpu.roll(v, LANES // 2, 1), v)
    return jnp.where(code > 0, v, jnp.zeros_like(v))


def pair_at(row_ref, table, r, pair):
    v0 = block_at(row_ref, table[r, 2 * pair], 0)
    v1 = block_at(row_ref, table[r, 2 * pair + 1], 1)
    return jnp.where(low_lanes(v0.shape[0]), v0, v1)


def densify_half(chunk, table, half, b, first=0):
    tile = chunk.shape[1]
    for r in range(2):
        for pair in range(b.shape[1] // LANES):
            hi, lo = split(pair_at(chunk.at[r], table, 2 * half + r, first + pair))
            lanes = slice(pair * LANES, (pair + 1) * LANES)
            b[r * tile : (r + 1) * tile, lanes] = hi
            b[(2 + r) * tile : (3 + r) * tile, lanes] = lo


def times_half(a, b, lanes):
    depth = b.shape[0]
    return jnp.dot(a[:, :depth], b[:, lanes], preferred_element_type=F32) + jnp.dot(
        a[:, depth:], b[: depth // 2, lanes], preferred_element_type=F32
    )


def lane_blocks(width, step=256):
    return [slice(i, i + step) for i in range(0, width, step)]


def ham_kernel(ham_cols, ham_count, ham, a, ham_table, ham_here, sems):
    rows, tile, _ = ham.shape
    copies = [
        pltpu.make_async_copy(ham.at[q], ham_here.at[q], sems.at[q]) for q in range(rows)
    ]
    for copy in copies:
        copy.start()
    fill_table(ham_table, ham_cols, ham_count)
    for q in range(rows):
        copies[q].wait()
        for pair in range(ham_table.shape[1] // 2):
            hi, lo = split(pair_at(ham_here.at[q], ham_table, q, pair))
            a[pair, q * tile : (q + 1) * tile, 0:LANES] = hi
            a[pair, q * tile : (q + 1) * tile, LANES : 2 * LANES] = hi
            a[pair, q * tile : (q + 1) * tile, 2 * LANES : 3 * LANES] = lo


def add_half(step, half, first, dens_table, a, acc_in, chunk, out, b):
    densify_half(chunk, dens_table, half, b, first // LANES)
    pair = shard_of(step) * (dens_table.shape[0] // 2) + half
    for lanes in lane_blocks(out.shape[1]):
        part = times_half(a[pair], b, lanes)
        if acc_in is not None:
            part += acc_in[:, first + lanes.start : first + lanes.stop]
        out[:, lanes] = part


def add_kernel(step, halves, dens_table, a, *rest):
    (acc, b), chunks = rest[-2:], rest[-2 - len(halves) : -2]
    before = rest[0] if step > 0 else None
    for half, chunk in zip(halves, chunks):
        add_half(step, half, 0, dens_table, a, before, chunk, acc, b)
        before = acc


def last_kernel(step, half, first, dens_table, a, acc_in, chunk, m_hi, m_lo, p, above, below, b):
    add_half(step, half, first, dens_table, a, acc_in, chunk, p, b)
    weigh(below, m_hi, m_lo, 2, p)
    weigh(above, m_hi, m_lo, 0, p)


def margin_kernel(over, hi_out, lo_out):
    rows, tile, _ = over.shape
    for s in range(3):
        for j in range(rows):
            for pair in range(rows // 2):
                at = (s * rows + j) * tile
                lanes = slice(at // LANES * LANES, at // LANES * LANES + LANES)
                v0, v1 = over[2 * pair, :, lanes], over[2 * pair + 1, :, lanes]
                if at % LANES == 0:
                    v1 = pltpu.roll(v1, LANES // 2, 1)
                else:
                    v0 = pltpu.roll(v0, LANES // 2, 1)
                hi, lo = split(jnp.where(low_lanes(tile), v0, v1))
                to = slice(pair * LANES, (pair + 1) * LANES)
                hi_out[s, j * tile : (j + 1) * tile, to] = hi
                lo_out[s, j * tile : (j + 1) * tile, to] = lo


def weigh(out, m_hi, m_lo, s, p):
    for lanes in lane_blocks(p.shape[1]):
        hi, lo = split(p[:, lanes])
        out[:, lanes] = (
            jnp.dot(m_hi[s], hi, preferred_element_type=F32)
            + jnp.dot(m_hi[s], lo, preferred_element_type=F32)
            + jnp.dot(m_lo[s], hi, preferred_element_type=F32)
        )


def own_kernel(m_hi, m_lo, *rest):
    parts, (product, window, term, sems) = rest[:-4], rest[-4:]
    rows, tile, width = product.shape
    step = width // len(parts)
    copies = []

    def start(ref, out, at):
        for q in range(rows):
            copies.append(
                pltpu.make_async_copy(
                    ref.at[pl.ds(q * tile, tile)],
                    out.at[q, :, pl.ds(at, step)],
                    sems.at[len(copies)],
                )
            )
            copies[-1].start()

    for i, part in enumerate(parts):
        start(part, product, i * step)
    for i, part in enumerate(parts):
        weigh(term.at[i], m_hi, m_lo, 1, part)
        start(term.at[i], window, width + i * step)
    for copy in copies:
        copy.wait()


def arrived_kernel(at, above, below, window_in, window, sems):
    rows, tile, triple = window.shape
    copies = [
        pltpu.make_async_copy(
            term.at[pl.ds(q * tile, tile)],
            window.at[q, :, pl.ds(start + at, term.shape[1])],
            sems.at[i, q],
        )
        for i, (term, start) in enumerate(((above, 0), (below, triple // 3 * 2)))
        for q in range(rows)
    ]
    for copy in copies:
        copy.start()
    for copy in copies:
        copy.wait()


def call(kernel, name, out_shape, in_spaces, out_spaces, scratch, aliases=None):
    return pl.pallas_call(
        kernel,
        name=name,
        out_shape=out_shape,
        in_specs=[pl.BlockSpec(memory_space=s) for s in in_spaces],
        out_specs=jax.tree.map(lambda s: pl.BlockSpec(memory_space=s), out_spaces),
        scratch_shapes=scratch,
        input_output_aliases=aliases or {},
        cost_estimate=pl.CostEstimate(flops=1024, bytes_accessed=1024, transcendentals=0),
        compiler_params=pltpu.CompilerParams(vmem_limit_bytes=24 << 20),
    )


def shards(ham_tiles, ham_cols, ham_count, dens_tiles, dens_cols, dens_count, over_tiles):
    count = lax.axis_size("cross")
    rows, tile, _ = ham_tiles.shape
    blocks = rows * count
    width = blocks * tile
    tall = rows * tile
    per_shard = rows // 2
    sds = jax.ShapeDtypeStruct

    halves = [dens_tiles[2 * h : 2 * h + 2] for h in range(per_shard)]
    *halves, dens_cols = lax.optimization_barrier((*halves, dens_cols))
    arrivals = [halves, [pass_on(h, 1) for h in halves]]
    ham_cols, ham_count, dens_cols, dens_count, ham_tiles = (
        pltpu.with_memory_space_constraint(x, pltpu.HBM)
        for x in (ham_cols, ham_count, dens_cols, dens_count, ham_tiles)
    )
    table = call(
        table_kernel,
        "table",
        sds((rows, blocks), jnp.int32),
        (SMEM, SMEM),
        SMEM,
        [],
    )(dens_cols, dens_count)
    tables = [table] + [pass_on(table, step) for step in range(1, count)]
    m_hi, m_lo = call(
        margin_kernel,
        "margin",
        (sds((3, tall, tall), BF16),) * 2,
        (VMEM,),
        (VMEM, VMEM),
        [],
    )(over_tiles)
    a = call(
        ham_kernel,
        "ham",
        sds((blocks // 2, tall, 3 * LANES), BF16),
        (SMEM, SMEM, pltpu.HBM),
        VMEM,
        [
            pltpu.SMEM((rows, blocks), jnp.int32),
            VMEM(ham_tiles.shape, F32),
            pltpu.SemaphoreType.DMA((rows,)),
        ],
    )(ham_cols, ham_count, ham_tiles)

    def add(step, chunks, acc):
        return call(
            functools.partial(add_kernel, step, list(range(len(chunks)))),
            "add%d" % step,
            sds((tall, width), F32),
            (SMEM,) + (VMEM,) * (1 + len(chunks) + (step > 0)),
            VMEM,
            [VMEM((4 * tile, width), BF16)],
        )(tables[step], a, *([acc] if step > 0 else []), *chunks)

    acc = None
    for step in range(1, count - 1):
        now = arrivals[-1]
        if step == 1:
            now[0], a = lax.optimization_barrier((now[0], a))
            now[-1], *tables = lax.optimization_barrier((now[-1], *tables))
        else:
            now[0], acc = lax.optimization_barrier((now[0], acc))
        if step == 2:
            now[-1], m_hi, m_lo = lax.optimization_barrier((now[-1], m_hi, m_lo))
        acc = add(step - 1, arrivals[-2], acc)
        arrivals.append([pass_on(h, 1) for h in now])
    acc = add(count - 2, arrivals[-2], acc)
    acc = add(count - 1, arrivals[-1][:-1], acc)

    sides = 2
    piece = width // sides
    parts, befores, afters = [], [], []
    for side in range(sides):
        part, above, below = call(
            functools.partial(last_kernel, count - 1, per_shard - 1, side * piece),
            "last%d" % side,
            [sds((tall, piece), F32)] * 3,
            (SMEM,) + (VMEM,) * 5,
            [VMEM] * 3,
            [VMEM((4 * tile, piece), BF16)],
        )(tables[-1], a, acc, arrivals[-1][-1], m_hi, m_lo)
        if side + 1 < sides:
            part, acc = lax.optimization_barrier((part, acc))
        parts.append(part)
        befores.append(rotate(below, 1))
        afters.append(rotate(above, -1))
    product, window = call(
        own_kernel,
        "own",
        (sds((rows, tile, width), F32), sds((rows, tile, 3 * width), F32)),
        (VMEM,) * (2 + sides),
        (pl.ANY, pl.ANY),
        [VMEM((sides, tall, piece), F32), pltpu.SemaphoreType.DMA((2 * sides * rows,))],
    )(m_hi, m_lo, *parts)
    for side in range(sides):
        window = call(
            functools.partial(arrived_kernel, side * piece),
            "arrived%d" % side,
            sds((rows, tile, 3 * width), F32),
            (VMEM, VMEM, pl.ANY),
            pl.ANY,
            [pltpu.SemaphoreType.DMA((2, rows))],
            {2: 0},
        )(befores[side], afters[side], window)
    return (product, window)


def solution(mesh):
    whole = P(AXES)
    return jax.shard_map(
        shards,
        mesh=mesh,
        in_specs=(whole,) * 7,
        out_specs=(whole, whole),
        check_vma=False,
    )
```

```python
import functools

import jax
import jax.numpy as jnp
from jax import lax
from jax.experimental import pallas as pl
from jax.experimental.pallas import tpu as pltpu
from jax.sharding import PartitionSpec as P

LANES = 128
F32 = jnp.float32
BF16 = jnp.bfloat16
VMEM = pltpu.VMEM
SMEM = pltpu.SMEM


AXES = ("parts", "line", "cross")


def permute(x, target):
    parts, line, cross = (lax.axis_size(axis) for axis in AXES)
    flat = lambda p, g, c: (p % parts * line + g % line) * cross + c
    places = [(p, g, c) for p in range(parts) for g in range(line) for c in range(cross)]
    return lax.ppermute(x, AXES, [(flat(*place), flat(*target(*place))) for place in places])


def rotate(x, by):
    return permute(x, lambda p, g, c: (p, g + by, c))


def ring_order(count):
    return list(range(0, count, 2))[:1] + list(range(1, count, 2)) + list(range(0, count, 2))[:0:-1]


def pass_on(x, by):
    order = ring_order(lax.axis_size("cross"))
    after = {d: order[(i + by) % len(order)] for i, d in enumerate(order)}
    return permute(x, lambda p, g, c: (p, g, after[c]))


def shard_of(step):
    order = ring_order(lax.axis_size("cross"))
    me = lax.axis_index("cross")
    owner = jnp.int32(0)
    for i, d in enumerate(order):
        owner = jnp.where(me == d, order[i - step], owner)
    return owner


def fill_table(table, columns, counts):
    rows, width = table.shape
    for r in range(rows):
        for c in range(width):
            table[r, c] = 0
        for slot in range(columns.shape[1]):

            @pl.when(slot < counts[r])
            def _(r=r, slot=slot):
                table[r, columns[r, slot]] = slot + 1


def table_kernel(columns, counts, table):
    fill_table(table, columns, counts)


def split(v):
    hi = v.astype(BF16)
    return hi, (v - hi.astype(F32)).astype(BF16)


def low_lanes(rows):
    return lax.broadcasted_iota(jnp.int32, (rows, LANES), 1) < LANES // 2


def block_at(row_ref, code, upper):
    slot = jnp.maximum(code - 1, 0)
    v = row_ref[:, pl.ds(pl.multiple_of((slot >> 1) * LANES, LANES), LANES)]
    v = jnp.where((slot & 1) != upper, pltpu.roll(v, LANES // 2, 1), v)
    return jnp.where(code > 0, v, jnp.zeros_like(v))


def pair_at(row_ref, table, r, pair):
    v0 = block_at(row_ref, table[r, 2 * pair], 0)
    v1 = block_at(row_ref, table[r, 2 * pair + 1], 1)
    return jnp.where(low_lanes(v0.shape[0]), v0, v1)


def densify_half(chunk, table, half, b, first=0):
    tile = chunk.shape[1]
    for r in range(2):
        for pair in range(b.shape[1] // LANES):
            hi, lo = split(pair_at(chunk.at[r], table, 2 * half + r, first + pair))
            lanes = slice(pair * LANES, (pair + 1) * LANES)
            b[r * tile : (r + 1) * tile, lanes] = hi
            b[(2 + r) * tile : (3 + r) * tile, lanes] = lo


def times_half(a, b, lanes):
    depth = b.shape[0]
    return jnp.dot(a[:, :depth], b[:, lanes], preferred_element_type=F32) + jnp.dot(
        a[:, depth:], b[: depth // 2, lanes], preferred_element_type=F32
    )


def lane_blocks(width, step=256):
    return [slice(i, i + step) for i in range(0, width, step)]


def ham_kernel(ham_cols, ham_count, ham, a, ham_table, ham_here, sems):
    rows, tile, _ = ham.shape
    copies = [
        pltpu.make_async_copy(ham.at[q], ham_here.at[q], sems.at[q]) for q in range(rows)
    ]
    for copy in copies:
        copy.start()
    fill_table(ham_table, ham_cols, ham_count)
    for q in range(rows):
        copies[q].wait()
        for pair in range(ham_table.shape[1] // 2):
            hi, lo = split(pair_at(ham_here.at[q], ham_table, q, pair))
            a[pair, q * tile : (q + 1) * tile, 0:LANES] = hi
            a[pair, q * tile : (q + 1) * tile, LANES : 2 * LANES] = hi
            a[pair, q * tile : (q + 1) * tile, 2 * LANES : 3 * LANES] = lo


def add_half(step, half, first, dens_table, a, acc_in, chunk, out, b):
    densify_half(chunk, dens_table, half, b, first // LANES)
    pair = shard_of(step) * (dens_table.shape[0] // 2) + half
    for lanes in lane_blocks(out.shape[1]):
        part = times_half(a[pair], b, lanes)
        if acc_in is not None:
            part += acc_in[:, first + lanes.start : first + lanes.stop]
        out[:, lanes] = part


def add_kernel(step, halves, dens_table, a, *rest):
    (acc, b), chunks = rest[-2:], rest[-2 - len(halves) : -2]
    before = rest[0] if step > 0 else None
    for half, chunk in zip(halves, chunks):
        add_half(step, half, 0, dens_table, a, before, chunk, acc, b)
        before = acc


def pick_kernel(half, dens_table, pick):
    rows, deep, width = pick.shape
    here = lax.broadcasted_iota(jnp.int32, (deep, LANES), 0)
    lane = lax.broadcasted_iota(jnp.int32, (deep, LANES), 1)
    block = LANES // 2
    for r in range(rows):
        for pair in range(width // LANES):
            codes = [dens_table[2 * half + r, 2 * pair + side] for side in range(2)]
            wanted = jnp.where(
                lane < block, codes[0] * block - block, codes[1] * block - LANES
            )
            pick[r, :, pair * LANES : (pair + 1) * LANES] = jnp.where(
                here == lane + wanted, 1.0, 0.0
            ).astype(BF16)


def last_kernel(step, half, first, a, acc_in, chunk, pick, m_hi, m_lo, p, above, below, b):
    rows, tile, _ = chunk.shape
    width = p.shape[1]
    for r in range(rows):
        hi, lo = split(chunk[r])
        placed = jnp.dot(
            jnp.concatenate([hi, lo], axis=0),
            pick[r, :, first : first + width],
            preferred_element_type=F32,
        ).astype(BF16)
        b[r * tile : (r + 1) * tile, :] = placed[:tile]
        b[(rows + r) * tile : (rows + r + 1) * tile, :] = placed[tile:]
    pair = shard_of(step) * (a.shape[0] // lax.axis_size("cross")) + half
    tall = p.shape[0]
    both_hi = m_hi[0:2].reshape(2 * tall, tall)
    both_lo = m_lo[0:2].reshape(2 * tall, tall)
    for lanes in lane_blocks(width):
        part = acc_in[:, first + lanes.start : first + lanes.stop] + times_half(a[pair], b, lanes)
        p[:, lanes] = part
        hi, lo = split(part)
        terms = (
            jnp.dot(both_hi, hi, preferred_element_type=F32)
            + jnp.dot(both_hi, lo, preferred_element_type=F32)
            + jnp.dot(both_lo, hi, preferred_element_type=F32)
        )
        above[:, lanes] = terms[:tall]
        below[:, lanes] = terms[tall:]


def margin_kernel(over, hi_out, lo_out):
    rows, tile, _ = over.shape
    for place, s in enumerate((0, 2, 1)):
        for j in range(rows):
            for pair in range(rows // 2):
                at = (s * rows + j) * tile
                lanes = slice(at // LANES * LANES, at // LANES * LANES + LANES)
                v0, v1 = over[2 * pair, :, lanes], over[2 * pair + 1, :, lanes]
                if at % LANES == 0:
                    v1 = pltpu.roll(v1, LANES // 2, 1)
                else:
                    v0 = pltpu.roll(v0, LANES // 2, 1)
                hi, lo = split(jnp.where(low_lanes(tile), v0, v1))
                to = slice(pair * LANES, (pair + 1) * LANES)
                hi_out[place, j * tile : (j + 1) * tile, to] = hi
                lo_out[place, j * tile : (j + 1) * tile, to] = lo


def weigh(out, m_hi, m_lo, s, p):
    for lanes in lane_blocks(p.shape[1]):
        hi, lo = split(p[:, lanes])
        out[:, lanes] = (
            jnp.dot(m_hi[s], hi, preferred_element_type=F32)
            + jnp.dot(m_hi[s], lo, preferred_element_type=F32)
            + jnp.dot(m_lo[s], hi, preferred_element_type=F32)
        )


def own_kernel(m_hi, m_lo, *rest):
    parts, (product, window, term, sems) = rest[:-4], rest[-4:]
    rows, tile, width = product.shape
    copies = []

    def start(ref, out, at):
        for q in range(rows):
            copies.append(
                pltpu.make_async_copy(
                    ref.at[pl.ds(q * tile, tile)],
                    out.at[q, :, pl.ds(at, ref.shape[1])],
                    sems.at[len(copies)],
                )
            )
            copies[-1].start()

    at = 0
    for part in parts:
        start(part, product, at)
        at += part.shape[1]
    at = 0
    for part in parts:
        here = term.at[:, pl.ds(at, part.shape[1])]
        weigh(here, m_hi, m_lo, 2, part)
        start(here, window, width + at)
        at += part.shape[1]
    for copy in copies:
        copy.wait()


def arrived_kernel(at, above, below, window_in, window, sems):
    rows, tile, triple = window.shape
    copies = [
        pltpu.make_async_copy(
            term.at[pl.ds(q * tile, tile)],
            window.at[q, :, pl.ds(start + at, term.shape[1])],
            sems.at[i, q],
        )
        for i, (term, start) in enumerate(((above, 0), (below, triple // 3 * 2)))
        for q in range(rows)
    ]
    for copy in copies:
        copy.start()
    for copy in copies:
        copy.wait()


def call(kernel, name, out_shape, in_spaces, out_spaces, scratch, aliases=None):
    return pl.pallas_call(
        kernel,
        name=name,
        out_shape=out_shape,
        in_specs=[pl.BlockSpec(memory_space=s) for s in in_spaces],
        out_specs=jax.tree.map(lambda s: pl.BlockSpec(memory_space=s), out_spaces),
        scratch_shapes=scratch,
        input_output_aliases=aliases or {},
        cost_estimate=pl.CostEstimate(flops=1024, bytes_accessed=1024, transcendentals=0),
        compiler_params=pltpu.CompilerParams(vmem_limit_bytes=24 << 20),
    )


def shards(ham_tiles, ham_cols, ham_count, dens_tiles, dens_cols, dens_count, over_tiles):
    count = lax.axis_size("cross")
    rows, tile, _ = ham_tiles.shape
    blocks = rows * count
    width = blocks * tile
    tall = rows * tile
    per_shard = rows // 2
    sds = jax.ShapeDtypeStruct

    halves = [dens_tiles[2 * h : 2 * h + 2] for h in range(per_shard)]
    *halves, dens_cols = lax.optimization_barrier((*halves, dens_cols))
    arrivals = [halves, [pass_on(h, 1) for h in halves]]
    ham_cols, ham_count, dens_cols, dens_count, ham_tiles = (
        pltpu.with_memory_space_constraint(x, pltpu.HBM)
        for x in (ham_cols, ham_count, dens_cols, dens_count, ham_tiles)
    )
    table = call(
        table_kernel,
        "table",
        sds((rows, blocks), jnp.int32),
        (SMEM, SMEM),
        SMEM,
        [],
    )(dens_cols, dens_count)
    tables = [table] + [pass_on(table, step) for step in range(1, count)]
    m_hi, m_lo = call(
        margin_kernel,
        "margin",
        (sds((3, tall, tall), BF16),) * 2,
        (VMEM,),
        (VMEM, VMEM),
        [],
    )(over_tiles)
    a = call(
        ham_kernel,
        "ham",
        sds((blocks // 2, tall, 3 * LANES), BF16),
        (SMEM, SMEM, pltpu.HBM),
        VMEM,
        [
            pltpu.SMEM((rows, blocks), jnp.int32),
            VMEM(ham_tiles.shape, F32),
            pltpu.SemaphoreType.DMA((rows,)),
        ],
    )(ham_cols, ham_count, ham_tiles)

    def add(step, chunks, acc):
        return call(
            functools.partial(add_kernel, step, list(range(len(chunks)))),
            "add%d" % step,
            sds((tall, width), F32),
            (SMEM,) + (VMEM,) * (1 + len(chunks) + (step > 0)),
            VMEM,
            [VMEM((4 * tile, width), BF16)],
        )(tables[step], a, *([acc] if step > 0 else []), *chunks)

    pieces = (width // 2, width // 2)
    acc = None
    for step in range(1, count - 1):
        now = arrivals[-1]
        if step == 1:
            now[0], a = lax.optimization_barrier((now[0], a))
            now[-1], *tables = lax.optimization_barrier((now[-1], *tables))
        else:
            now[0], acc = lax.optimization_barrier((now[0], acc))
        if step == 2:
            pick = call(
                functools.partial(pick_kernel, per_shard - 1),
                "pick",
                sds((2, dens_tiles.shape[2], width), BF16),
                (SMEM,),
                VMEM,
                [],
            )(tables[-1])
            now[-1], m_hi, m_lo, pick = lax.optimization_barrier((now[-1], m_hi, m_lo, pick))
        acc = add(step - 1, arrivals[-2], acc)
        arrivals.append([pass_on(h, 1) for h in now])
    acc = add(count - 2, arrivals[-2], acc)
    acc = add(count - 1, arrivals[-1][:-1], acc)

    parts, befores, afters = [], [], []
    for i, piece in enumerate(pieces):
        part, above, below = call(
            functools.partial(last_kernel, count - 1, per_shard - 1, sum(pieces[:i])),
            "last%d" % i,
            [sds((tall, piece), F32)] * 3,
            (VMEM,) * 6,
            [VMEM] * 3,
            [VMEM((4 * tile, piece), BF16)],
        )(a, acc, arrivals[-1][-1], pick, m_hi, m_lo)
        if i + 1 < len(pieces):
            part, acc = lax.optimization_barrier((part, acc))
        parts.append(part)
        befores.append(rotate(below, 1))
        afters.append(rotate(above, -1))
    product, window = call(
        own_kernel,
        "own",
        (sds((rows, tile, width), F32), sds((rows, tile, 3 * width), F32)),
        (VMEM,) * (2 + len(pieces)),
        (pl.ANY, pl.ANY),
        [VMEM((tall, width), F32), pltpu.SemaphoreType.DMA((2 * len(pieces) * rows,))],
    )(m_hi, m_lo, *parts)
    for i in range(len(pieces)):
        window = call(
            functools.partial(arrived_kernel, sum(pieces[:i])),
            "arrived%d" % i,
            sds((rows, tile, 3 * width), F32),
            (VMEM, VMEM, pl.ANY),
            pl.ANY,
            [pltpu.SemaphoreType.DMA((2, rows))],
            {2: 0},
        )(befores[i], afters[i], window)
    return (product, window)


def solution(mesh):
    whole = P(AXES)
    return jax.shard_map(
        shards,
        mesh=mesh,
        in_specs=(whole,) * 7,
        out_specs=(whole, whole),
        check_vma=False,
    )
```

```python
import functools

import jax
import jax.numpy as jnp
from jax import lax
from jax.experimental import pallas as pl
from jax.experimental.pallas import tpu as pltpu
from jax.sharding import PartitionSpec as P

LANES = 128
F32 = jnp.float32
BF16 = jnp.bfloat16
VMEM = pltpu.VMEM
SMEM = pltpu.SMEM


AXES = ("parts", "line", "cross")


def permute(x, target):
    parts, line, cross = (lax.axis_size(axis) for axis in AXES)
    flat = lambda p, g, c: (p % parts * line + g % line) * cross + c
    places = [(p, g, c) for p in range(parts) for g in range(line) for c in range(cross)]
    return lax.ppermute(x, AXES, [(flat(*place), flat(*target(*place))) for place in places])


def rotate(x, by):
    return permute(x, lambda p, g, c: (p, g + by, c))


def ring_order(count):
    return list(range(0, count, 2))[:1] + list(range(1, count, 2)) + list(range(0, count, 2))[:0:-1]


def pass_on(x, by):
    order = ring_order(lax.axis_size("cross"))
    after = {d: order[(i + by) % len(order)] for i, d in enumerate(order)}
    return permute(x, lambda p, g, c: (p, g, after[c]))


def shard_of(step):
    order = ring_order(lax.axis_size("cross"))
    me = lax.axis_index("cross")
    owner = jnp.int32(0)
    for i, d in enumerate(order):
        owner = jnp.where(me == d, order[i - step], owner)
    return owner


def fill_table(table, columns, counts):
    rows, width = table.shape
    for r in range(rows):
        for c in range(width):
            table[r, c] = 0
        for slot in range(columns.shape[1]):

            @pl.when(slot < counts[r])
            def _(r=r, slot=slot):
                table[r, columns[r, slot]] = slot + 1


def cut_kernel(dens, *rest):
    halves, sems = rest[:-1], rest[-1]
    copies = [
        pltpu.make_async_copy(dens.at[pl.ds(2 * h, 2)], half, sems.at[h])
        for h, half in enumerate(halves)
    ]
    for copy in copies:
        copy.start()
    for copy in copies:
        copy.wait()


def table_kernel(columns, counts, table):
    fill_table(table, columns, counts)


def split(v):
    hi = v.astype(BF16)
    return hi, (v - hi.astype(F32)).astype(BF16)


def low_lanes(rows):
    return lax.broadcasted_iota(jnp.int32, (rows, LANES), 1) < LANES // 2


def block_at(row_ref, code, upper):
    slot = jnp.maximum(code - 1, 0)
    v = row_ref[:, pl.ds(pl.multiple_of((slot >> 1) * LANES, LANES), LANES)]
    v = jnp.where((slot & 1) != upper, pltpu.roll(v, LANES // 2, 1), v)
    return jnp.where(code > 0, v, jnp.zeros_like(v))


def pair_at(row_ref, table, r, pair):
    v0 = block_at(row_ref, table[r, 2 * pair], 0)
    v1 = block_at(row_ref, table[r, 2 * pair + 1], 1)
    return jnp.where(low_lanes(v0.shape[0]), v0, v1)


def densify_half(chunk, table, half, b, first=0):
    tile = chunk.shape[1]
    for r in range(2):
        for pair in range(b.shape[1] // LANES):
            hi, lo = split(pair_at(chunk.at[r], table, 2 * half + r, first + pair))
            lanes = slice(pair * LANES, (pair + 1) * LANES)
            b[r * tile : (r + 1) * tile, lanes] = hi
            b[(2 + r) * tile : (3 + r) * tile, lanes] = lo


def times_half(a, b, lanes):
    depth = b.shape[0]
    return jnp.dot(a[:, :depth], b[:, lanes], preferred_element_type=F32) + jnp.dot(
        a[:, depth:], b[: depth // 2, lanes], preferred_element_type=F32
    )


def lane_blocks(width, step=256):
    return [slice(i, i + step) for i in range(0, width, step)]


def ham_kernel(ham_cols, ham_count, ham, a, ham_table, ham_here, sems):
    rows, tile, _ = ham.shape
    copies = [
        pltpu.make_async_copy(ham.at[q], ham_here.at[q], sems.at[q]) for q in range(rows)
    ]
    for copy in copies:
        copy.start()
    fill_table(ham_table, ham_cols, ham_count)
    for q in range(rows):
        copies[q].wait()
        for pair in range(ham_table.shape[1] // 2):
            hi, lo = split(pair_at(ham_here.at[q], ham_table, q, pair))
            a[pair, q * tile : (q + 1) * tile, 0:LANES] = hi
            a[pair, q * tile : (q + 1) * tile, LANES : 2 * LANES] = hi
            a[pair, q * tile : (q + 1) * tile, 2 * LANES : 3 * LANES] = lo


def add_half(step, half, first, dens_table, a, acc_in, chunk, out, b):
    densify_half(chunk, dens_table, half, b, first // LANES)
    pair = shard_of(step) * (dens_table.shape[0] // 2) + half
    for lanes in lane_blocks(out.shape[1]):
        part = times_half(a[pair], b, lanes)
        if acc_in is not None:
            part += acc_in[:, first + lanes.start : first + lanes.stop]
        out[:, lanes] = part


def add_kernel(step, halves, dens_table, a, *rest):
    (acc, b), chunks = rest[-2:], rest[-2 - len(halves) : -2]
    before = rest[0] if step > 0 else None
    for half, chunk in zip(halves, chunks):
        add_half(step, half, 0, dens_table, a, before, chunk, acc, b)
        before = acc


def pick_kernel(half, dens_table, pick):
    rows, deep, width = pick.shape
    here = lax.broadcasted_iota(jnp.int32, (deep, LANES), 0)
    lane = lax.broadcasted_iota(jnp.int32, (deep, LANES), 1)
    block = LANES // 2
    for r in range(rows):
        for pair in range(width // LANES):
            codes = [dens_table[2 * half + r, 2 * pair + side] for side in range(2)]
            wanted = jnp.where(
                lane < block, codes[0] * block - block, codes[1] * block - LANES
            )
            pick[r, :, pair * LANES : (pair + 1) * LANES] = jnp.where(
                here == lane + wanted, 1.0, 0.0
            ).astype(BF16)


def last_kernel(step, half, first, a, acc_in, chunk, pick, m_hi, m_lo, p, above, below, b):
    rows, tile, _ = chunk.shape
    width = p.shape[1]
    for r in range(rows):
        hi, lo = split(chunk[r])
        placed = jnp.dot(
            jnp.concatenate([hi, lo], axis=0),
            pick[r, :, first : first + width],
            preferred_element_type=F32,
        ).astype(BF16)
        b[r * tile : (r + 1) * tile, :] = placed[:tile]
        b[(rows + r) * tile : (rows + r + 1) * tile, :] = placed[tile:]
    pair = shard_of(step) * (a.shape[0] // lax.axis_size("cross")) + half
    tall = p.shape[0]
    both_hi = m_hi[0:2].reshape(2 * tall, tall)
    both_lo = m_lo[0:2].reshape(2 * tall, tall)
    for lanes in lane_blocks(width):
        part = acc_in[:, first + lanes.start : first + lanes.stop] + times_half(a[pair], b, lanes)
        p[:, lanes] = part
        hi, lo = split(part)
        terms = (
            jnp.dot(both_hi, hi, preferred_element_type=F32)
            + jnp.dot(both_hi, lo, preferred_element_type=F32)
            + jnp.dot(both_lo, hi, preferred_element_type=F32)
        )
        above[:, lanes] = terms[:tall]
        below[:, lanes] = terms[tall:]


def margin_kernel(over, hi_out, lo_out):
    rows, tile, _ = over.shape
    for place, s in enumerate((0, 2, 1)):
        for j in range(rows):
            for pair in range(rows // 2):
                at = (s * rows + j) * tile
                lanes = slice(at // LANES * LANES, at // LANES * LANES + LANES)
                v0, v1 = over[2 * pair, :, lanes], over[2 * pair + 1, :, lanes]
                if at % LANES == 0:
                    v1 = pltpu.roll(v1, LANES // 2, 1)
                else:
                    v0 = pltpu.roll(v0, LANES // 2, 1)
                hi, lo = split(jnp.where(low_lanes(tile), v0, v1))
                to = slice(pair * LANES, (pair + 1) * LANES)
                hi_out[place, j * tile : (j + 1) * tile, to] = hi
                lo_out[place, j * tile : (j + 1) * tile, to] = lo


def weigh(out, m_hi, m_lo, s, p):
    for lanes in lane_blocks(p.shape[1]):
        hi, lo = split(p[:, lanes])
        out[:, lanes] = (
            jnp.dot(m_hi[s], hi, preferred_element_type=F32)
            + jnp.dot(m_hi[s], lo, preferred_element_type=F32)
            + jnp.dot(m_lo[s], hi, preferred_element_type=F32)
        )


def own_kernel(m_hi, m_lo, *rest):
    parts, (product, window, term, sems) = rest[:-4], rest[-4:]
    rows, tile, width = product.shape
    copies = []

    def start(ref, out, at):
        for q in range(rows):
            copies.append(
                pltpu.make_async_copy(
                    ref.at[pl.ds(q * tile, tile)],
                    out.at[q, :, pl.ds(at, ref.shape[1])],
                    sems.at[len(copies)],
                )
            )
            copies[-1].start()

    at = 0
    for part in parts:
        start(part, product, at)
        at += part.shape[1]
    at = 0
    for part in parts:
        here = term.at[:, pl.ds(at, part.shape[1])]
        weigh(here, m_hi, m_lo, 2, part)
        start(here, window, width + at)
        at += part.shape[1]
    for copy in copies:
        copy.wait()


def arrived_kernel(at, above, below, window_in, window, sems):
    rows, tile, triple = window.shape
    copies = [
        pltpu.make_async_copy(
            term.at[pl.ds(q * tile, tile)],
            window.at[q, :, pl.ds(start + at, term.shape[1])],
            sems.at[i, q],
        )
        for i, (term, start) in enumerate(((above, 0), (below, triple // 3 * 2)))
        for q in range(rows)
    ]
    for copy in copies:
        copy.start()
    for copy in copies:
        copy.wait()


def call(kernel, name, out_shape, in_spaces, out_spaces, scratch, aliases=None):
    return pl.pallas_call(
        kernel,
        name=name,
        out_shape=out_shape,
        in_specs=[pl.BlockSpec(memory_space=s) for s in in_spaces],
        out_specs=jax.tree.map(lambda s: pl.BlockSpec(memory_space=s), out_spaces),
        scratch_shapes=scratch,
        input_output_aliases=aliases or {},
        cost_estimate=pl.CostEstimate(flops=1024, bytes_accessed=1024, transcendentals=0),
        compiler_params=pltpu.CompilerParams(vmem_limit_bytes=24 << 20),
    )


def shards(ham_tiles, ham_cols, ham_count, dens_tiles, dens_cols, dens_count, over_tiles):
    count = lax.axis_size("cross")
    rows, tile, _ = ham_tiles.shape
    blocks = rows * count
    width = blocks * tile
    tall = rows * tile
    per_shard = rows // 2
    sds = jax.ShapeDtypeStruct

    halves = call(
        cut_kernel,
        "cut",
        [sds((2, tile, dens_tiles.shape[2]), F32)] * per_shard,
        (pltpu.HBM,),
        [VMEM] * per_shard,
        [pltpu.SemaphoreType.DMA((per_shard,))],
    )(pltpu.with_memory_space_constraint(dens_tiles, pltpu.HBM))
    *halves, dens_cols = lax.optimization_barrier((*halves, dens_cols))
    arrivals = [halves, [pass_on(h, 1) for h in halves]]
    ham_cols, ham_count, dens_cols, dens_count, ham_tiles = (
        pltpu.with_memory_space_constraint(x, pltpu.HBM)
        for x in (ham_cols, ham_count, dens_cols, dens_count, ham_tiles)
    )
    table = call(
        table_kernel,
        "table",
        sds((rows, blocks), jnp.int32),
        (SMEM, SMEM),
        SMEM,
        [],
    )(dens_cols, dens_count)
    tables = [table] + [pass_on(table, step) for step in range(1, count)]
    m_hi, m_lo = call(
        margin_kernel,
        "margin",
        (sds((3, tall, tall), BF16),) * 2,
        (VMEM,),
        (VMEM, VMEM),
        [],
    )(over_tiles)
    a = call(
        ham_kernel,
        "ham",
        sds((blocks // 2, tall, 3 * LANES), BF16),
        (SMEM, SMEM, pltpu.HBM),
        VMEM,
        [
            pltpu.SMEM((rows, blocks), jnp.int32),
            VMEM(ham_tiles.shape, F32),
            pltpu.SemaphoreType.DMA((rows,)),
        ],
    )(ham_cols, ham_count, ham_tiles)

    def add(step, chunks, acc):
        return call(
            functools.partial(add_kernel, step, list(range(len(chunks)))),
            "add%d" % step,
            sds((tall, width), F32),
            (SMEM,) + (VMEM,) * (1 + len(chunks) + (step > 0)),
            VMEM,
            [VMEM((4 * tile, width), BF16)],
        )(tables[step], a, *([acc] if step > 0 else []), *chunks)

    pieces = (width // 4,) * 4
    acc = None
    for step in range(1, count - 1):
        now = arrivals[-1]
        if step == 1:
            now[0], a = lax.optimization_barrier((now[0], a))
            now[-1], *tables = lax.optimization_barrier((now[-1], *tables))
        else:
            now[0], acc = lax.optimization_barrier((now[0], acc))
        if step == 2:
            pick = call(
                functools.partial(pick_kernel, per_shard - 1),
                "pick",
                sds((2, dens_tiles.shape[2], width), BF16),
                (SMEM,),
                VMEM,
                [],
            )(tables[-1])
            now[-1], m_hi, m_lo, pick = lax.optimization_barrier((now[-1], m_hi, m_lo, pick))
        acc = add(step - 1, arrivals[-2], acc)
        arrivals.append([pass_on(h, 1) for h in now])
    acc = add(count - 2, arrivals[-2], acc)
    acc = add(count - 1, arrivals[-1][:-1], acc)

    parts, befores, afters = [], [], []
    for i, piece in enumerate(pieces):
        part, above, below = call(
            functools.partial(last_kernel, count - 1, per_shard - 1, sum(pieces[:i])),
            "last%d" % i,
            [sds((tall, piece), F32)] * 3,
            (VMEM,) * 6,
            [VMEM] * 3,
            [VMEM((4 * tile, piece), BF16)],
        )(a, acc, arrivals[-1][-1], pick, m_hi, m_lo)
        if i + 1 < len(pieces):
            part, acc = lax.optimization_barrier((part, acc))
        parts.append(part)
        befores.append(rotate(below, 1))
        afters.append(rotate(above, -1))
    product, window = call(
        own_kernel,
        "own",
        (sds((rows, tile, width), F32), sds((rows, tile, 3 * width), F32)),
        (VMEM,) * (2 + len(pieces)),
        (pl.ANY, pl.ANY),
        [VMEM((tall, width), F32), pltpu.SemaphoreType.DMA((2 * len(pieces) * rows,))],
    )(m_hi, m_lo, *parts)
    for i in range(len(pieces)):
        window = call(
            functools.partial(arrived_kernel, sum(pieces[:i])),
            "arrived%d" % i,
            sds((rows, tile, 3 * width), F32),
            (VMEM, VMEM, pl.ANY),
            pl.ANY,
            [pltpu.SemaphoreType.DMA((2, rows))],
            {2: 0},
        )(befores[i], afters[i], window)
    return (product, window)


def solution(mesh):
    whole = P(AXES)
    return jax.shard_map(
        shards,
        mesh=mesh,
        in_specs=(whole,) * 7,
        out_specs=(whole, whole),
        check_vma=False,
    )
```

```python
import functools

import jax
import jax.numpy as jnp
from jax import lax
from jax.experimental import pallas as pl
from jax.experimental.pallas import tpu as pltpu
from jax.sharding import PartitionSpec as P

LANES = 128
F32 = jnp.float32
BF16 = jnp.bfloat16
VMEM = pltpu.VMEM
SMEM = pltpu.SMEM


AXES = ("parts", "line", "cross")


def permute(x, target):
    parts, line, cross = (lax.axis_size(axis) for axis in AXES)
    flat = lambda p, g, c: (p % parts * line + g % line) * cross + c
    places = [(p, g, c) for p in range(parts) for g in range(line) for c in range(cross)]
    return lax.ppermute(x, AXES, [(flat(*place), flat(*target(*place))) for place in places])


def rotate(x, by):
    return permute(x, lambda p, g, c: (p, g + by, c))


def ring_order(count):
    return list(range(0, count, 2))[:1] + list(range(1, count, 2)) + list(range(0, count, 2))[:0:-1]


def pass_on(x, by):
    order = ring_order(lax.axis_size("cross"))
    after = {d: order[(i + by) % len(order)] for i, d in enumerate(order)}
    return permute(x, lambda p, g, c: (p, g, after[c]))


def shard_of(step):
    order = ring_order(lax.axis_size("cross"))
    me = lax.axis_index("cross")
    owner = jnp.int32(0)
    for i, d in enumerate(order):
        owner = jnp.where(me == d, order[i - step], owner)
    return owner


def fill_table(table, columns, counts):
    rows, width = table.shape
    for r in range(rows):
        for c in range(width):
            table[r, c] = 0
        for slot in range(columns.shape[1]):

            @pl.when(slot < counts[r])
            def _(r=r, slot=slot):
                table[r, columns[r, slot]] = slot + 1


def cut_kernel(dens, *rest):
    halves, sems = rest[:-1], rest[-1]
    copies = [
        pltpu.make_async_copy(dens.at[pl.ds(2 * h, 2)], half, sems.at[h])
        for h, half in enumerate(halves)
    ]
    for copy in copies:
        copy.start()
    for copy in copies:
        copy.wait()


def table_kernel(columns, counts, table):
    fill_table(table, columns, counts)


def split(v):
    hi = v.astype(BF16)
    return hi, (v - hi.astype(F32)).astype(BF16)


def low_lanes(rows):
    return lax.broadcasted_iota(jnp.int32, (rows, LANES), 1) < LANES // 2


def block_at(row_ref, code, upper):
    slot = jnp.maximum(code - 1, 0)
    v = row_ref[:, pl.ds(pl.multiple_of((slot >> 1) * LANES, LANES), LANES)]
    v = jnp.where((slot & 1) != upper, pltpu.roll(v, LANES // 2, 1), v)
    return jnp.where(code > 0, v, jnp.zeros_like(v))


def pair_at(row_ref, table, r, pair):
    v0 = block_at(row_ref, table[r, 2 * pair], 0)
    v1 = block_at(row_ref, table[r, 2 * pair + 1], 1)
    return jnp.where(low_lanes(v0.shape[0]), v0, v1)


def densify_half(chunk, table, half, b, first=0):
    tile = chunk.shape[1]
    for r in range(2):
        for pair in range(b.shape[1] // LANES):
            hi, lo = split(pair_at(chunk.at[r], table, 2 * half + r, first + pair))
            lanes = slice(pair * LANES, (pair + 1) * LANES)
            b[r * tile : (r + 1) * tile, lanes] = hi
            b[(2 + r) * tile : (3 + r) * tile, lanes] = lo


def times_half(a, b, lanes):
    depth = b.shape[0]
    return jnp.dot(a[:, :depth], b[:, lanes], preferred_element_type=F32) + jnp.dot(
        a[:, depth:], b[: depth // 2, lanes], preferred_element_type=F32
    )


def lane_blocks(width, step=256):
    return [slice(i, i + step) for i in range(0, width, step)]


def ham_kernel(ham_cols, ham_count, ham, a, ham_table, ham_here, sems):
    rows, tile, _ = ham.shape
    copies = [
        pltpu.make_async_copy(ham.at[q], ham_here.at[q], sems.at[q]) for q in range(rows)
    ]
    for copy in copies:
        copy.start()
    fill_table(ham_table, ham_cols, ham_count)
    for q in range(rows):
        copies[q].wait()
        for pair in range(ham_table.shape[1] // 2):
            hi, lo = split(pair_at(ham_here.at[q], ham_table, q, pair))
            a[pair, q * tile : (q + 1) * tile, 0:LANES] = hi
            a[pair, q * tile : (q + 1) * tile, LANES : 2 * LANES] = hi
            a[pair, q * tile : (q + 1) * tile, 2 * LANES : 3 * LANES] = lo


def add_half(step, half, first, dens_table, a, acc_in, chunk, out, b):
    densify_half(chunk, dens_table, half, b, first // LANES)
    pair = shard_of(step) * (dens_table.shape[0] // 2) + half
    for lanes in lane_blocks(out.shape[1]):
        part = times_half(a[pair], b, lanes)
        if acc_in is not None:
            part += acc_in[:, first + lanes.start : first + lanes.stop]
        out[:, lanes] = part


def add_kernel(step, halves, dens_table, a, *rest):
    (acc, b), chunks = rest[-2:], rest[-2 - len(halves) : -2]
    before = rest[0] if step > 0 else None
    for half, chunk in zip(halves, chunks):
        add_half(step, half, 0, dens_table, a, before, chunk, acc, b)
        before = acc


def pick_kernel(half, dens_table, pick):
    rows, deep, width = pick.shape
    here = lax.broadcasted_iota(jnp.int32, (deep, LANES), 0)
    lane = lax.broadcasted_iota(jnp.int32, (deep, LANES), 1)
    block = LANES // 2
    for r in range(rows):
        for pair in range(width // LANES):
            codes = [dens_table[2 * half + r, 2 * pair + side] for side in range(2)]
            wanted = jnp.where(
                lane < block, codes[0] * block - block, codes[1] * block - LANES
            )
            pick[r, :, pair * LANES : (pair + 1) * LANES] = jnp.where(
                here == lane + wanted, 1.0, 0.0
            ).astype(BF16)


def last_kernel(step, half, first, a, acc_in, chunk, pick, m_hi, m_lo, p, below, b):
    rows, tile, _ = chunk.shape
    width = p.shape[1]
    for r in range(rows):
        hi, lo = split(chunk[r])
        placed = jnp.dot(
            jnp.concatenate([hi, lo], axis=0),
            pick[r, :, first : first + width],
            preferred_element_type=F32,
        ).astype(BF16)
        b[r * tile : (r + 1) * tile, :] = placed[:tile]
        b[(rows + r) * tile : (rows + r + 1) * tile, :] = placed[tile:]
    pair = shard_of(step) * (a.shape[0] // lax.axis_size("cross")) + half
    for lanes in lane_blocks(width):
        part = acc_in[:, first + lanes.start : first + lanes.stop] + times_half(a[pair], b, lanes)
        p[:, lanes] = part
        weigh(below.at[:, lanes], m_hi, m_lo, 2, part)


def above_kernel(count, m_hi, m_lo, *rest):
    parts, outs = rest[:count], rest[count:]
    step = parts[0].shape[1]
    per_out = outs[0].shape[1] // step
    for i, part in enumerate(parts):
        lanes = pl.ds(i % per_out * step, step)
        weigh(outs[i // per_out].at[:, lanes], m_hi, m_lo, 0, part[...])


def margin_kernel(over, hi_out, lo_out):
    rows, tile, _ = over.shape
    for s in range(3):
        for j in range(rows):
            for pair in range(rows // 2):
                at = (s * rows + j) * tile
                lanes = slice(at // LANES * LANES, at // LANES * LANES + LANES)
                v0, v1 = over[2 * pair, :, lanes], over[2 * pair + 1, :, lanes]
                if at % LANES == 0:
                    v1 = pltpu.roll(v1, LANES // 2, 1)
                else:
                    v0 = pltpu.roll(v0, LANES // 2, 1)
                hi, lo = split(jnp.where(low_lanes(tile), v0, v1))
                to = slice(pair * LANES, (pair + 1) * LANES)
                hi_out[s, j * tile : (j + 1) * tile, to] = hi
                lo_out[s, j * tile : (j + 1) * tile, to] = lo


def weigh(out, m_hi, m_lo, s, p):
    hi, lo = split(p)
    out[...] = (
        jnp.dot(m_hi[s], hi, preferred_element_type=F32)
        + jnp.dot(m_hi[s], lo, preferred_element_type=F32)
        + jnp.dot(m_lo[s], hi, preferred_element_type=F32)
    )


def own_kernel(m_hi, m_lo, *rest):
    parts, (product, window, term, sems) = rest[:-4], rest[-4:]
    rows, tile, width = product.shape
    copies = []

    def start(ref, out, at):
        for q in range(rows):
            copies.append(
                pltpu.make_async_copy(
                    ref.at[pl.ds(q * tile, tile)],
                    out.at[q, :, pl.ds(at, ref.shape[1])],
                    sems.at[len(copies)],
                )
            )
            copies[-1].start()

    at = 0
    for part in parts:
        start(part, product, at)
        at += part.shape[1]
    at = 0
    for part in parts:
        here = term.at[:, pl.ds(at, part.shape[1])]
        weigh(here, m_hi, m_lo, 1, part[...])
        start(here, window, width + at)
        at += part.shape[1]
    for copy in copies:
        copy.wait()


def arrived_kernel(at, count, *rest):
    terms, (window_in, window, sems) = rest[:count], rest[count:]
    rows, tile, _ = window.shape
    copies = []
    for term in terms:
        for q in range(rows):
            copies.append(
                pltpu.make_async_copy(
                    term.at[pl.ds(q * tile, tile)],
                    window.at[q, :, pl.ds(at, term.shape[1])],
                    sems.at[len(copies)],
                )
            )
            copies[-1].start()
        at += term.shape[1]
    for copy in copies:
        copy.wait()


def call(kernel, name, out_shape, in_spaces, out_spaces, scratch, aliases=None):
    return pl.pallas_call(
        kernel,
        name=name,
        out_shape=out_shape,
        in_specs=[pl.BlockSpec(memory_space=s) for s in in_spaces],
        out_specs=jax.tree.map(lambda s: pl.BlockSpec(memory_space=s), out_spaces),
        scratch_shapes=scratch,
        input_output_aliases=aliases or {},
        cost_estimate=pl.CostEstimate(flops=1024, bytes_accessed=1024, transcendentals=0),
        compiler_params=pltpu.CompilerParams(vmem_limit_bytes=24 << 20),
    )


def shards(ham_tiles, ham_cols, ham_count, dens_tiles, dens_cols, dens_count, over_tiles):
    count = lax.axis_size("cross")
    rows, tile, _ = ham_tiles.shape
    blocks = rows * count
    width = blocks * tile
    tall = rows * tile
    per_shard = rows // 2
    sds = jax.ShapeDtypeStruct

    halves = call(
        cut_kernel,
        "cut",
        [sds((2, tile, dens_tiles.shape[2]), F32)] * per_shard,
        (pltpu.HBM,),
        [VMEM] * per_shard,
        [pltpu.SemaphoreType.DMA((per_shard,))],
    )(pltpu.with_memory_space_constraint(dens_tiles, pltpu.HBM))
    *halves, dens_cols = lax.optimization_barrier((*halves, dens_cols))
    arrivals = [halves, [pass_on(h, 1) for h in halves]]
    ham_cols, ham_count, dens_cols, dens_count, ham_tiles = (
        pltpu.with_memory_space_constraint(x, pltpu.HBM)
        for x in (ham_cols, ham_count, dens_cols, dens_count, ham_tiles)
    )
    table = call(
        table_kernel,
        "table",
        sds((rows, blocks), jnp.int32),
        (SMEM, SMEM),
        SMEM,
        [],
    )(dens_cols, dens_count)
    tables = [table] + [pass_on(table, step) for step in range(1, count)]
    m_hi, m_lo = call(
        margin_kernel,
        "margin",
        (sds((3, tall, tall), BF16),) * 2,
        (VMEM,),
        (VMEM, VMEM),
        [],
    )(over_tiles)
    a = call(
        ham_kernel,
        "ham",
        sds((blocks // 2, tall, 3 * LANES), BF16),
        (SMEM, SMEM, pltpu.HBM),
        VMEM,
        [
            pltpu.SMEM((rows, blocks), jnp.int32),
            VMEM(ham_tiles.shape, F32),
            pltpu.SemaphoreType.DMA((rows,)),
        ],
    )(ham_cols, ham_count, ham_tiles)

    def add(step, chunks, acc):
        return call(
            functools.partial(add_kernel, step, list(range(len(chunks)))),
            "add%d" % step,
            sds((tall, width), F32),
            (SMEM,) + (VMEM,) * (1 + len(chunks) + (step > 0)),
            VMEM,
            [VMEM((4 * tile, width), BF16)],
        )(tables[step], a, *([acc] if step > 0 else []), *chunks)

    pieces = (width // 2,) * 2
    acc = None
    for step in range(1, count - 1):
        now = arrivals[-1]
        if step == 1:
            now[0], a = lax.optimization_barrier((now[0], a))
            now[-1], *tables = lax.optimization_barrier((now[-1], *tables))
        else:
            now[0], acc = lax.optimization_barrier((now[0], acc))
        if step == 2:
            pick = call(
                functools.partial(pick_kernel, per_shard - 1),
                "pick",
                sds((2, dens_tiles.shape[2], width), BF16),
                (SMEM,),
                VMEM,
                [],
            )(tables[-1])
            now[-1], m_hi, m_lo, pick = lax.optimization_barrier((now[-1], m_hi, m_lo, pick))
        acc = add(step - 1, arrivals[-2], acc)
        arrivals.append([pass_on(h, 1) for h in now])
    acc = add(count - 2, arrivals[-2], acc)
    acc = add(count - 1, arrivals[-1][:-1], acc)

    parts, befores = [], []
    for i, piece in enumerate(pieces):
        part, below = call(
            functools.partial(last_kernel, count - 1, per_shard - 1, sum(pieces[:i])),
            "last%d" % i,
            [sds((tall, piece), F32)] * 2,
            (VMEM,) * 6,
            [VMEM] * 2,
            [VMEM((4 * tile, piece), BF16)],
        )(a, acc, arrivals[-1][-1], pick, m_hi, m_lo)
        if i + 1 < len(pieces):
            part, acc = lax.optimization_barrier((part, acc))
        parts.append(part)
        befores.append(rotate(below, 1))
    outs = 2
    above = call(
        functools.partial(above_kernel, len(parts)),
        "above",
        [sds((tall, width // outs), F32)] * outs,
        (VMEM,) * (2 + len(parts)),
        [VMEM] * outs,
        [],
    )(m_hi, m_lo, *parts)
    above = list(above)
    above[0], *befores[:-1] = lax.optimization_barrier((above[0], *befores[:-1]))
    afters = [rotate(term, -1) for term in above]
    product, window = call(
        own_kernel,
        "own",
        (sds((rows, tile, width), F32), sds((rows, tile, 3 * width), F32)),
        (VMEM,) * (2 + len(pieces)),
        (pl.ANY, pl.ANY),
        [VMEM((tall, width), F32), pltpu.SemaphoreType.DMA((2 * len(pieces) * rows,))],
    )(m_hi, m_lo, *parts)
    arrived = [(0, befores)]
    arrived += [(2 * width + i * (width // outs), [term]) for i, term in enumerate(afters)]
    for i, (at, terms) in enumerate(arrived):
        window = call(
            functools.partial(arrived_kernel, at, len(terms)),
            "arrived%d" % i,
            sds((rows, tile, 3 * width), F32),
            (VMEM,) * len(terms) + (pl.ANY,),
            pl.ANY,
            [pltpu.SemaphoreType.DMA((len(terms) * rows,))],
            {len(terms): 0},
        )(*terms, window)
    return (product, window)


def solution(mesh):
    whole = P(AXES)
    return jax.shard_map(
        shards,
        mesh=mesh,
        in_specs=(whole,) * 7,
        out_specs=(whole, whole),
        check_vma=False,
    )
```

```python
import functools

import jax
import jax.numpy as jnp
from jax import lax
from jax.experimental import pallas as pl
from jax.experimental.pallas import tpu as pltpu
from jax.sharding import PartitionSpec as P

LANES = 128
F32 = jnp.float32
BF16 = jnp.bfloat16
VMEM = pltpu.VMEM
SMEM = pltpu.SMEM


AXES = ("parts", "line", "cross")


def permute(x, target):
    parts, line, cross = (lax.axis_size(axis) for axis in AXES)
    flat = lambda p, g, c: (p % parts * line + g % line) * cross + c
    places = [(p, g, c) for p in range(parts) for g in range(line) for c in range(cross)]
    return lax.ppermute(x, AXES, [(flat(*place), flat(*target(*place))) for place in places])


def rotate(x, by):
    return permute(x, lambda p, g, c: (p, g + by, c))


def ring_order(count):
    return list(range(0, count, 2))[:1] + list(range(1, count, 2)) + list(range(0, count, 2))[:0:-1]


def pass_on(x, by):
    order = ring_order(lax.axis_size("cross"))
    after = {d: order[(i + by) % len(order)] for i, d in enumerate(order)}
    return permute(x, lambda p, g, c: (p, g, after[c]))


def shard_of(step):
    order = ring_order(lax.axis_size("cross"))
    me = lax.axis_index("cross")
    owner = jnp.int32(0)
    for i, d in enumerate(order):
        owner = jnp.where(me == d, order[i - step], owner)
    return owner


def fill_table(table, columns, counts):
    rows, width = table.shape
    for r in range(rows):
        for c in range(width):
            table[r, c] = 0
        for slot in range(columns.shape[1]):

            @pl.when(slot < counts[r])
            def _(r=r, slot=slot):
                table[r, columns[r, slot]] = slot + 1


def cut_kernel(half, dens, out, sem):
    copy = pltpu.make_async_copy(dens.at[pl.ds(2 * half, 2)], out, sem)
    copy.start()
    copy.wait()


def table_kernel(columns, counts, table):
    fill_table(table, columns, counts)


def split(v):
    hi = v.astype(BF16)
    return hi, (v - hi.astype(F32)).astype(BF16)


def low_lanes(rows):
    return lax.broadcasted_iota(jnp.int32, (rows, LANES), 1) < LANES // 2


def block_at(row_ref, code, upper):
    slot = jnp.maximum(code - 1, 0)
    v = row_ref[:, pl.ds(pl.multiple_of((slot >> 1) * LANES, LANES), LANES)]
    v = jnp.where((slot & 1) != upper, pltpu.roll(v, LANES // 2, 1), v)
    return jnp.where(code > 0, v, jnp.zeros_like(v))


def pair_at(row_ref, table, r, pair):
    v0 = block_at(row_ref, table[r, 2 * pair], 0)
    v1 = block_at(row_ref, table[r, 2 * pair + 1], 1)
    return jnp.where(low_lanes(v0.shape[0]), v0, v1)


def densify_half(chunk, table, half, b, first=0):
    tile = chunk.shape[1]
    for r in range(2):
        for pair in range(b.shape[1] // LANES):
            hi, lo = split(pair_at(chunk.at[r], table, 2 * half + r, first + pair))
            lanes = slice(pair * LANES, (pair + 1) * LANES)
            b[r * tile : (r + 1) * tile, lanes] = hi
            b[(2 + r) * tile : (3 + r) * tile, lanes] = lo


def times_half(a, b, lanes):
    depth = b.shape[0]
    return jnp.dot(a[:, :depth], b[:, lanes], preferred_element_type=F32) + jnp.dot(
        a[:, depth:], b[: depth // 2, lanes], preferred_element_type=F32
    )


def lane_blocks(width, step=256):
    return [slice(i, i + step) for i in range(0, width, step)]


def ham_kernel(ham_cols, ham_count, ham, a, ham_table, ham_here, sems):
    rows, tile, _ = ham.shape
    copies = [
        pltpu.make_async_copy(ham.at[q], ham_here.at[q], sems.at[q]) for q in range(rows)
    ]
    for copy in copies:
        copy.start()
    fill_table(ham_table, ham_cols, ham_count)
    for q in range(rows):
        copies[q].wait()
        for pair in range(ham_table.shape[1] // 2):
            hi, lo = split(pair_at(ham_here.at[q], ham_table, q, pair))
            a[pair, q * tile : (q + 1) * tile, 0:LANES] = hi
            a[pair, q * tile : (q + 1) * tile, LANES : 2 * LANES] = hi
            a[pair, q * tile : (q + 1) * tile, 2 * LANES : 3 * LANES] = lo


def add_half(step, half, first, dens_table, a, acc_in, chunk, out, b):
    densify_half(chunk, dens_table, half, b, first // LANES)
    pair = shard_of(step) * (dens_table.shape[0] // 2) + half
    for lanes in lane_blocks(out.shape[1]):
        part = times_half(a[pair], b, lanes)
        if acc_in is not None:
            part += acc_in[:, first + lanes.start : first + lanes.stop]
        out[:, lanes] = part


def add_kernel(step, halves, dens_table, a, *rest):
    (acc, b), chunks = rest[-2:], rest[-2 - len(halves) : -2]
    before = rest[0] if step > 0 else None
    for half, chunk in zip(halves, chunks):
        add_half(step, half, 0, dens_table, a, before, chunk, acc, b)
        before = acc


def pick_kernel(half, dens_table, pick):
    rows, deep, width = pick.shape
    here = lax.broadcasted_iota(jnp.int32, (deep, LANES), 0)
    lane = lax.broadcasted_iota(jnp.int32, (deep, LANES), 1)
    block = LANES // 2
    for r in range(rows):
        for pair in range(width // LANES):
            codes = [dens_table[2 * half + r, 2 * pair + side] for side in range(2)]
            wanted = jnp.where(
                lane < block, codes[0] * block - block, codes[1] * block - LANES
            )
            pick[r, :, pair * LANES : (pair + 1) * LANES] = jnp.where(
                here == lane + wanted, 1.0, 0.0
            ).astype(BF16)


def last_kernel(step, half, first, a, acc_in, chunk, pick, m_hi, m_lo, p, above, below, b):
    rows, tile, _ = chunk.shape
    width = p.shape[1]
    for r in range(rows):
        hi, lo = split(chunk[r])
        placed = jnp.dot(
            jnp.concatenate([hi, lo], axis=0),
            pick[r, :, first : first + width],
            preferred_element_type=F32,
        ).astype(BF16)
        b[r * tile : (r + 1) * tile, :] = placed[:tile]
        b[(rows + r) * tile : (rows + r + 1) * tile, :] = placed[tile:]
    pair = shard_of(step) * (a.shape[0] // lax.axis_size("cross")) + half
    tall = p.shape[0]
    both_hi = m_hi[0:2].reshape(2 * tall, tall)
    both_lo = m_lo[0:2].reshape(2 * tall, tall)
    for lanes in lane_blocks(width):
        part = acc_in[:, first + lanes.start : first + lanes.stop] + times_half(a[pair], b, lanes)
        p[:, lanes] = part
        hi, lo = split(part)
        terms = (
            jnp.dot(both_hi, hi, preferred_element_type=F32)
            + jnp.dot(both_hi, lo, preferred_element_type=F32)
            + jnp.dot(both_lo, hi, preferred_element_type=F32)
        )
        above[:, lanes] = terms[:tall]
        below[:, lanes] = terms[tall:]


def margin_kernel(over, hi_out, lo_out):
    rows, tile, _ = over.shape
    for place, s in enumerate((0, 2, 1)):
        for j in range(rows):
            for pair in range(rows // 2):
                at = (s * rows + j) * tile
                lanes = slice(at // LANES * LANES, at // LANES * LANES + LANES)
                v0, v1 = over[2 * pair, :, lanes], over[2 * pair + 1, :, lanes]
                if at % LANES == 0:
                    v1 = pltpu.roll(v1, LANES // 2, 1)
                else:
                    v0 = pltpu.roll(v0, LANES // 2, 1)
                hi, lo = split(jnp.where(low_lanes(tile), v0, v1))
                to = slice(pair * LANES, (pair + 1) * LANES)
                hi_out[place, j * tile : (j + 1) * tile, to] = hi
                lo_out[place, j * tile : (j + 1) * tile, to] = lo


def weigh(out, m_hi, m_lo, s, p):
    for lanes in lane_blocks(p.shape[1]):
        hi, lo = split(p[:, lanes])
        out[:, lanes] = (
            jnp.dot(m_hi[s], hi, preferred_element_type=F32)
            + jnp.dot(m_hi[s], lo, preferred_element_type=F32)
            + jnp.dot(m_lo[s], hi, preferred_element_type=F32)
        )


def own_kernel(m_hi, m_lo, *rest):
    parts, (product, window, term, sems) = rest[:-4], rest[-4:]
    rows, tile, width = product.shape
    copies = []

    def start(ref, out, at):
        for q in range(rows):
            copies.append(
                pltpu.make_async_copy(
                    ref.at[pl.ds(q * tile, tile)],
                    out.at[q, :, pl.ds(at, ref.shape[1])],
                    sems.at[len(copies)],
                )
            )
            copies[-1].start()

    at = 0
    for part in parts:
        start(part, product, at)
        at += part.shape[1]
    at = 0
    for part in parts:
        here = term.at[:, pl.ds(at, part.shape[1])]
        weigh(here, m_hi, m_lo, 2, part)
        start(here, window, width + at)
        at += part.shape[1]
    for copy in copies:
        copy.wait()


def arrived_kernel(at, below, above, window_in, window, sems):
    rows, tile, triple = window.shape
    copies = [
        pltpu.make_async_copy(
            term.at[pl.ds(q * tile, tile)],
            window.at[q, :, pl.ds(start + at, term.shape[1])],
            sems.at[i, q],
        )
        for i, (term, start) in enumerate(((above, 0), (below, triple // 3 * 2)))
        for q in range(rows)
    ]
    for copy in copies:
        copy.start()
    for copy in copies:
        copy.wait()


def call(kernel, name, out_shape, in_spaces, out_spaces, scratch, aliases=None):
    return pl.pallas_call(
        kernel,
        name=name,
        out_shape=out_shape,
        in_specs=[pl.BlockSpec(memory_space=s) for s in in_spaces],
        out_specs=jax.tree.map(lambda s: pl.BlockSpec(memory_space=s), out_spaces),
        scratch_shapes=scratch,
        input_output_aliases=aliases or {},
        cost_estimate=pl.CostEstimate(flops=1024, bytes_accessed=1024, transcendentals=0),
        compiler_params=pltpu.CompilerParams(vmem_limit_bytes=24 << 20),
    )


def shards(ham_tiles, ham_cols, ham_count, dens_tiles, dens_cols, dens_count, over_tiles):
    count = lax.axis_size("cross")
    rows, tile, _ = ham_tiles.shape
    blocks = rows * count
    width = blocks * tile
    tall = rows * tile
    per_shard = rows // 2
    sds = jax.ShapeDtypeStruct

    dens_here = pltpu.with_memory_space_constraint(dens_tiles, pltpu.HBM)
    halves = []
    for h in range(per_shard):
        half = call(
            functools.partial(cut_kernel, h),
            "cut%d" % h,
            sds((2, tile, dens_tiles.shape[2]), F32),
            (pltpu.HBM,),
            VMEM,
            [pltpu.SemaphoreType.DMA],
        )(dens_here)
        half, dens_here = lax.optimization_barrier((half, dens_here))
        halves.append(half)
    halves[0], dens_cols = lax.optimization_barrier((halves[0], dens_cols))
    arrivals = [halves, [pass_on(h, 1) for h in halves]]
    ham_cols, ham_count, dens_cols, dens_count, ham_tiles = (
        pltpu.with_memory_space_constraint(x, pltpu.HBM)
        for x in (ham_cols, ham_count, dens_cols, dens_count, ham_tiles)
    )
    table = call(
        table_kernel,
        "table",
        sds((rows, blocks), jnp.int32),
        (SMEM, SMEM),
        SMEM,
        [],
    )(dens_cols, dens_count)
    tables = [table] + [pass_on(table, step) for step in range(1, count)]
    m_hi, m_lo = call(
        margin_kernel,
        "margin",
        (sds((3, tall, tall), BF16),) * 2,
        (VMEM,),
        (VMEM, VMEM),
        [],
    )(over_tiles)
    a = call(
        ham_kernel,
        "ham",
        sds((blocks // 2, tall, 3 * LANES), BF16),
        (SMEM, SMEM, pltpu.HBM),
        VMEM,
        [
            pltpu.SMEM((rows, blocks), jnp.int32),
            VMEM(ham_tiles.shape, F32),
            pltpu.SemaphoreType.DMA((rows,)),
        ],
    )(ham_cols, ham_count, ham_tiles)

    def add(step, chunks, acc):
        return call(
            functools.partial(add_kernel, step, list(range(len(chunks)))),
            "add%d" % step,
            sds((tall, width), F32),
            (SMEM,) + (VMEM,) * (1 + len(chunks) + (step > 0)),
            VMEM,
            [VMEM((4 * tile, width), BF16)],
        )(tables[step], a, *([acc] if step > 0 else []), *chunks)

    pieces = (width // 4,) * 4
    acc = None
    for step in range(1, count - 1):
        now = arrivals[-1]
        if step == 1:
            now[0], a = lax.optimization_barrier((now[0], a))
            now[-1], *tables = lax.optimization_barrier((now[-1], *tables))
        else:
            now[0], acc = lax.optimization_barrier((now[0], acc))
        if step == 2:
            pick = call(
                functools.partial(pick_kernel, per_shard - 1),
                "pick",
                sds((2, dens_tiles.shape[2], width), BF16),
                (SMEM,),
                VMEM,
                [],
            )(tables[-1])
            now[-1], m_hi, m_lo, pick = lax.optimization_barrier((now[-1], m_hi, m_lo, pick))
        acc = add(step - 1, arrivals[-2], acc)
        arrivals.append([pass_on(h, 1) for h in now])
    acc = add(count - 2, arrivals[-2], acc)
    acc = add(count - 1, arrivals[-1][:-1], acc)

    parts, befores, afters = [], [], []
    for i, piece in enumerate(pieces):
        part, above, below = call(
            functools.partial(last_kernel, count - 1, per_shard - 1, sum(pieces[:i])),
            "last%d" % i,
            [sds((tall, piece), F32)] * 3,
            (VMEM,) * 6,
            [VMEM] * 3,
            [VMEM((4 * tile, piece), BF16)],
        )(a, acc, arrivals[-1][-1], pick, m_hi, m_lo)
        if i + 1 < len(pieces):
            part, acc = lax.optimization_barrier((part, acc))
        parts.append(part)
        afters.append(rotate(above, -1))
        befores.append(rotate(below, 1))
    product, window = call(
        own_kernel,
        "own",
        (sds((rows, tile, width), F32), sds((rows, tile, 3 * width), F32)),
        (VMEM,) * (2 + len(pieces)),
        (pl.ANY, pl.ANY),
        [VMEM((tall, width), F32), pltpu.SemaphoreType.DMA((2 * len(pieces) * rows,))],
    )(m_hi, m_lo, *parts)
    for i in range(len(pieces)):
        window = call(
            functools.partial(arrived_kernel, sum(pieces[:i])),
            "arrived%d" % i,
            sds((rows, tile, 3 * width), F32),
            (VMEM, VMEM, pl.ANY),
            pl.ANY,
            [pltpu.SemaphoreType.DMA((2, rows))],
            {2: 0},
        )(afters[i], befores[i], window)
    return (product, window)


def solution(mesh):
    whole = P(AXES)
    return jax.shard_map(
        shards,
        mesh=mesh,
        in_specs=(whole,) * 7,
        out_specs=(whole, whole),
        check_vma=False,
    )
```

```python
import functools

import jax
import jax.numpy as jnp
from jax import lax
from jax.experimental import pallas as pl
from jax.experimental.pallas import tpu as pltpu
from jax.sharding import PartitionSpec as P

LANES = 128
F32 = jnp.float32
BF16 = jnp.bfloat16
VMEM = pltpu.VMEM
SMEM = pltpu.SMEM


AXES = ("parts", "line", "cross")


def permute(x, target):
    parts, line, cross = (lax.axis_size(axis) for axis in AXES)
    flat = lambda p, g, c: (p % parts * line + g % line) * cross + c
    places = [(p, g, c) for p in range(parts) for g in range(line) for c in range(cross)]
    return lax.ppermute(x, AXES, [(flat(*place), flat(*target(*place))) for place in places])


def rotate(x, by):
    return permute(x, lambda p, g, c: (p, g + by, c))


def ring_order(count):
    return list(range(0, count, 2))[:1] + list(range(1, count, 2)) + list(range(0, count, 2))[:0:-1]


def pass_on(x, by):
    order = ring_order(lax.axis_size("cross"))
    after = {d: order[(i + by) % len(order)] for i, d in enumerate(order)}
    return permute(x, lambda p, g, c: (p, g, after[c]))


def shard_of(step):
    order = ring_order(lax.axis_size("cross"))
    me = lax.axis_index("cross")
    owner = jnp.int32(0)
    for i, d in enumerate(order):
        owner = jnp.where(me == d, order[i - step], owner)
    return owner


def fill_table(table, columns, counts):
    rows, width = table.shape
    for r in range(rows):
        for c in range(width):
            table[r, c] = 0
        for slot in range(columns.shape[1]):

            @pl.when(slot < counts[r])
            def _(r=r, slot=slot):
                table[r, columns[r, slot]] = slot + 1


def cut_kernel(half, dens, out, sem):
    copy = pltpu.make_async_copy(dens.at[pl.ds(2 * half, 2)], out, sem)
    copy.start()
    copy.wait()


def table_kernel(columns, counts, table):
    fill_table(table, columns, counts)


def split(v):
    hi = v.astype(BF16)
    return hi, (v - hi.astype(F32)).astype(BF16)


def low_lanes(rows):
    return lax.broadcasted_iota(jnp.int32, (rows, LANES), 1) < LANES // 2


def block_at(row_ref, code, upper):
    slot = jnp.maximum(code - 1, 0)
    v = row_ref[:, pl.ds(pl.multiple_of((slot >> 1) * LANES, LANES), LANES)]
    v = jnp.where((slot & 1) != upper, pltpu.roll(v, LANES // 2, 1), v)
    return jnp.where(code > 0, v, jnp.zeros_like(v))


def pair_at(row_ref, table, r, pair):
    v0 = block_at(row_ref, table[r, 2 * pair], 0)
    v1 = block_at(row_ref, table[r, 2 * pair + 1], 1)
    return jnp.where(low_lanes(v0.shape[0]), v0, v1)


def densify_half(chunk, table, half, b, first=0):
    tile = chunk.shape[1]
    for r in range(2):
        for pair in range(b.shape[1] // LANES):
            hi, lo = split(pair_at(chunk.at[r], table, 2 * half + r, first + pair))
            lanes = slice(pair * LANES, (pair + 1) * LANES)
            b[r * tile : (r + 1) * tile, lanes] = hi
            b[(2 + r) * tile : (3 + r) * tile, lanes] = lo


def times_half(a, b, lanes):
    depth = b.shape[0]
    return jnp.dot(a[:, :depth], b[:, lanes], preferred_element_type=F32) + jnp.dot(
        a[:, depth:], b[: depth // 2, lanes], preferred_element_type=F32
    )


def lane_blocks(width, step=256):
    return [slice(i, i + step) for i in range(0, width, step)]


def ham_kernel(ham_cols, ham_count, ham, a, ham_table, ham_here, sems):
    rows, tile, _ = ham.shape
    copies = [
        pltpu.make_async_copy(ham.at[q], ham_here.at[q], sems.at[q]) for q in range(rows)
    ]
    for copy in copies:
        copy.start()
    fill_table(ham_table, ham_cols, ham_count)
    for q in range(rows):
        copies[q].wait()
        for pair in range(ham_table.shape[1] // 2):
            hi, lo = split(pair_at(ham_here.at[q], ham_table, q, pair))
            a[pair, q * tile : (q + 1) * tile, 0:LANES] = hi
            a[pair, q * tile : (q + 1) * tile, LANES : 2 * LANES] = hi
            a[pair, q * tile : (q + 1) * tile, 2 * LANES : 3 * LANES] = lo


def add_half(step, half, first, dens_table, a, acc_in, chunk, out, b):
    densify_half(chunk, dens_table, half, b, first // LANES)
    pair = shard_of(step) * (dens_table.shape[0] // 2) + half
    for lanes in lane_blocks(out.shape[1]):
        part = times_half(a[pair], b, lanes)
        if acc_in is not None:
            part += acc_in[:, first + lanes.start : first + lanes.stop]
        out[:, lanes] = part


def add_kernel(step, halves, dens_table, a, *rest):
    (acc, b), chunks = rest[-2:], rest[-2 - len(halves) : -2]
    before = rest[0] if step > 0 else None
    for half, chunk in zip(halves, chunks):
        add_half(step, half, 0, dens_table, a, before, chunk, acc, b)
        before = acc


def pick_kernel(half, dens_table, pick):
    rows, deep, width = pick.shape
    here = lax.broadcasted_iota(jnp.int32, (deep, LANES), 0)
    lane = lax.broadcasted_iota(jnp.int32, (deep, LANES), 1)
    block = LANES // 2
    for r in range(rows):
        for pair in range(width // LANES):
            codes = [dens_table[2 * half + r, 2 * pair + side] for side in range(2)]
            wanted = jnp.where(
                lane < block, codes[0] * block - block, codes[1] * block - LANES
            )
            pick[r, :, pair * LANES : (pair + 1) * LANES] = jnp.where(
                here == lane + wanted, 1.0, 0.0
            ).astype(BF16)


def last_kernel(step, half, first, a, acc_in, chunk, pick, m_hi, m_lo, p, above, below, b):
    rows, tile, _ = chunk.shape
    width = p.shape[1]
    for r in range(rows):
        hi, lo = split(chunk[r])
        placed = jnp.dot(
            jnp.concatenate([hi, lo], axis=0),
            pick[r, :, first : first + width],
            preferred_element_type=F32,
        ).astype(BF16)
        b[r * tile : (r + 1) * tile, :] = placed[:tile]
        b[(rows + r) * tile : (rows + r + 1) * tile, :] = placed[tile:]
    pair = shard_of(step) * (a.shape[0] // lax.axis_size("cross")) + half
    tall = p.shape[0]
    both_hi = m_hi[0:2].reshape(2 * tall, tall)
    both_lo = m_lo[0:2].reshape(2 * tall, tall)
    for lanes in lane_blocks(width):
        part = acc_in[:, first + lanes.start : first + lanes.stop] + times_half(a[pair], b, lanes)
        p[:, lanes] = part
        hi, lo = split(part)
        terms = (
            jnp.dot(both_hi, hi, preferred_element_type=F32)
            + jnp.dot(both_hi, lo, preferred_element_type=F32)
            + jnp.dot(both_lo, hi, preferred_element_type=F32)
        )
        above[:, lanes] = terms[:tall]
        below[:, lanes] = terms[tall:]


def margin_kernel(over, hi_out, lo_out):
    rows, tile, _ = over.shape
    for place, s in enumerate((0, 2, 1)):
        for j in range(rows):
            for pair in range(rows // 2):
                at = (s * rows + j) * tile
                lanes = slice(at // LANES * LANES, at // LANES * LANES + LANES)
                v0, v1 = over[2 * pair, :, lanes], over[2 * pair + 1, :, lanes]
                if at % LANES == 0:
                    v1 = pltpu.roll(v1, LANES // 2, 1)
                else:
                    v0 = pltpu.roll(v0, LANES // 2, 1)
                hi, lo = split(jnp.where(low_lanes(tile), v0, v1))
                to = slice(pair * LANES, (pair + 1) * LANES)
                hi_out[place, j * tile : (j + 1) * tile, to] = hi
                lo_out[place, j * tile : (j + 1) * tile, to] = lo


def weigh(out, m_hi, m_lo, s, p):
    for lanes in lane_blocks(p.shape[1]):
        hi, lo = split(p[:, lanes])
        out[:, lanes] = (
            jnp.dot(m_hi[s], hi, preferred_element_type=F32)
            + jnp.dot(m_hi[s], lo, preferred_element_type=F32)
            + jnp.dot(m_lo[s], hi, preferred_element_type=F32)
        )


def own_kernel(m_hi, m_lo, *rest):
    parts, (product, window, term, sems) = rest[:-4], rest[-4:]
    rows, tile, width = product.shape
    copies = []

    def start(ref, out, at):
        for q in range(rows):
            copies.append(
                pltpu.make_async_copy(
                    ref.at[pl.ds(q * tile, tile)],
                    out.at[q, :, pl.ds(at, ref.shape[1])],
                    sems.at[len(copies)],
                )
            )
            copies[-1].start()

    at = 0
    for part in parts:
        start(part, product, at)
        at += part.shape[1]
    at = 0
    for part in parts:
        here = term.at[:, pl.ds(at, part.shape[1])]
        weigh(here, m_hi, m_lo, 2, part)
        start(here, window, width + at)
        at += part.shape[1]
    for copy in copies:
        copy.wait()


def arrived_kernel(at, below, above, window_in, window, sems):
    rows, tile, triple = window.shape
    copies = [
        pltpu.make_async_copy(
            term.at[pl.ds(q * tile, tile)],
            window.at[q, :, pl.ds(start + at, term.shape[1])],
            sems.at[i, q],
        )
        for i, (term, start) in enumerate(((above, 0), (below, triple // 3 * 2)))
        for q in range(rows)
    ]
    for copy in copies:
        copy.start()
    for copy in copies:
        copy.wait()


def call(kernel, name, out_shape, in_spaces, out_spaces, scratch, aliases=None):
    return pl.pallas_call(
        kernel,
        name=name,
        out_shape=out_shape,
        in_specs=[pl.BlockSpec(memory_space=s) for s in in_spaces],
        out_specs=jax.tree.map(lambda s: pl.BlockSpec(memory_space=s), out_spaces),
        scratch_shapes=scratch,
        input_output_aliases=aliases or {},
        cost_estimate=pl.CostEstimate(flops=1024, bytes_accessed=1024, transcendentals=0),
        compiler_params=pltpu.CompilerParams(vmem_limit_bytes=24 << 20),
    )


def shards(ham_tiles, ham_cols, ham_count, dens_tiles, dens_cols, dens_count, over_tiles):
    count = lax.axis_size("cross")
    rows, tile, _ = ham_tiles.shape
    blocks = rows * count
    width = blocks * tile
    tall = rows * tile
    per_shard = rows // 2
    sds = jax.ShapeDtypeStruct

    dens_here = pltpu.with_memory_space_constraint(dens_tiles, pltpu.HBM)
    halves = []
    for h in range(per_shard):
        half = call(
            functools.partial(cut_kernel, h),
            "cut%d" % h,
            sds((2, tile, dens_tiles.shape[2]), F32),
            (pltpu.HBM,),
            VMEM,
            [pltpu.SemaphoreType.DMA],
        )(dens_here)
        half, dens_here = lax.optimization_barrier((half, dens_here))
        halves.append(half)
    halves[0], dens_cols = lax.optimization_barrier((halves[0], dens_cols))
    arrivals = [halves, [pass_on(h, 1) for h in halves]]
    ham_cols, ham_count, dens_cols, dens_count, ham_tiles = (
        pltpu.with_memory_space_constraint(x, pltpu.HBM)
        for x in (ham_cols, ham_count, dens_cols, dens_count, ham_tiles)
    )
    table = call(
        table_kernel,
        "table",
        sds((rows, blocks), jnp.int32),
        (SMEM, SMEM),
        SMEM,
        [],
    )(dens_cols, dens_count)
    tables = [table] + [pass_on(table, step) for step in range(1, count)]
    m_hi, m_lo = call(
        margin_kernel,
        "margin",
        (sds((3, tall, tall), BF16),) * 2,
        (VMEM,),
        (VMEM, VMEM),
        [],
    )(over_tiles)
    a = call(
        ham_kernel,
        "ham",
        sds((blocks // 2, tall, 3 * LANES), BF16),
        (SMEM, SMEM, pltpu.HBM),
        VMEM,
        [
            pltpu.SMEM((rows, blocks), jnp.int32),
            VMEM(ham_tiles.shape, F32),
            pltpu.SemaphoreType.DMA((rows,)),
        ],
    )(ham_cols, ham_count, ham_tiles)

    def add(step, chunks, acc):
        return call(
            functools.partial(add_kernel, step, list(range(len(chunks)))),
            "add%d" % step,
            sds((tall, width), F32),
            (SMEM,) + (VMEM,) * (1 + len(chunks) + (step > 0)),
            VMEM,
            [VMEM((4 * tile, width), BF16)],
        )(tables[step], a, *([acc] if step > 0 else []), *chunks)

    pieces = (width // 2, width // 2)
    acc = None
    for step in range(1, count - 1):
        now = arrivals[-1]
        if step == 1:
            now[0], a = lax.optimization_barrier((now[0], a))
            now[-1], *tables = lax.optimization_barrier((now[-1], *tables))
        else:
            now[0], acc = lax.optimization_barrier((now[0], acc))
        if step == 2:
            pick = call(
                functools.partial(pick_kernel, per_shard - 1),
                "pick",
                sds((2, dens_tiles.shape[2], width), BF16),
                (SMEM,),
                VMEM,
                [],
            )(tables[-1])
            now[-1], m_hi, m_lo, pick = lax.optimization_barrier((now[-1], m_hi, m_lo, pick))
        acc = add(step - 1, arrivals[-2], acc)
        arrivals.append([pass_on(h, 1) for h in now])
    acc = add(count - 2, arrivals[-2], acc)
    acc = add(count - 1, arrivals[-1][:-1], acc)

    parts, befores, afters = [], [], []
    for i, piece in enumerate(pieces):
        part, above, below = call(
            functools.partial(last_kernel, count - 1, per_shard - 1, sum(pieces[:i])),
            "last%d" % i,
            [sds((tall, piece), F32)] * 3,
            (VMEM,) * 6,
            [VMEM] * 3,
            [VMEM((4 * tile, piece), BF16)],
        )(a, acc, arrivals[-1][-1], pick, m_hi, m_lo)
        if i + 1 < len(pieces):
            part, acc = lax.optimization_barrier((part, acc))
        parts.append(part)
        afters.append(rotate(above, -1))
        befores.append(rotate(below, 1))
    product, window = call(
        own_kernel,
        "own",
        (sds((rows, tile, width), F32), sds((rows, tile, 3 * width), F32)),
        (VMEM,) * (2 + len(pieces)),
        (pl.ANY, pl.ANY),
        [VMEM((tall, width), F32), pltpu.SemaphoreType.DMA((2 * len(pieces) * rows,))],
    )(m_hi, m_lo, *parts)
    for i in range(len(pieces)):
        window = call(
            functools.partial(arrived_kernel, sum(pieces[:i])),
            "arrived%d" % i,
            sds((rows, tile, 3 * width), F32),
            (VMEM, VMEM, pl.ANY),
            pl.ANY,
            [pltpu.SemaphoreType.DMA((2, rows))],
            {2: 0},
        )(afters[i], befores[i], window)
    return (product, window)


def solution(mesh):
    whole = P(AXES)
    return jax.shard_map(
        shards,
        mesh=mesh,
        in_specs=(whole,) * 7,
        out_specs=(whole, whole),
        check_vma=False,
    )
```

```python
import functools

import jax
import jax.numpy as jnp
from jax import lax
from jax.experimental import pallas as pl
from jax.experimental.pallas import tpu as pltpu
from jax.sharding import PartitionSpec as P

LANES = 128
F32 = jnp.float32
BF16 = jnp.bfloat16
VMEM = pltpu.VMEM
SMEM = pltpu.SMEM


AXES = ("parts", "line", "cross")


def permute(x, target):
    parts, line, cross = (lax.axis_size(axis) for axis in AXES)
    flat = lambda p, g, c: (p % parts * line + g % line) * cross + c
    places = [(p, g, c) for p in range(parts) for g in range(line) for c in range(cross)]
    return lax.ppermute(x, AXES, [(flat(*place), flat(*target(*place))) for place in places])


def rotate(x, by):
    return permute(x, lambda p, g, c: (p, g + by, c))


def ring_order(count):
    return list(range(0, count, 2))[:1] + list(range(1, count, 2)) + list(range(0, count, 2))[:0:-1]


def pass_on(x, by):
    order = ring_order(lax.axis_size("cross"))
    after = {d: order[(i + by) % len(order)] for i, d in enumerate(order)}
    return permute(x, lambda p, g, c: (p, g, after[c]))


def shard_of(step):
    order = ring_order(lax.axis_size("cross"))
    me = lax.axis_index("cross")
    owner = jnp.int32(0)
    for i, d in enumerate(order):
        owner = jnp.where(me == d, order[i - step], owner)
    return owner


def fill_table(table, columns, counts):
    rows, width = table.shape
    for r in range(rows):
        for c in range(width):
            table[r, c] = 0
        for slot in range(columns.shape[1]):

            @pl.when(slot < counts[r])
            def _(r=r, slot=slot):
                table[r, columns[r, slot]] = slot + 1


def cut_kernel(half, dens, out, sem):
    copy = pltpu.make_async_copy(dens.at[pl.ds(2 * half, 2)], out, sem)
    copy.start()
    copy.wait()


def table_kernel(columns, counts, table):
    fill_table(table, columns, counts)


def split(v):
    hi = v.astype(BF16)
    return hi, (v - hi.astype(F32)).astype(BF16)


def low_lanes(rows):
    return lax.broadcasted_iota(jnp.int32, (rows, LANES), 1) < LANES // 2


def block_at(row_ref, code, upper):
    slot = jnp.maximum(code - 1, 0)
    v = row_ref[:, pl.ds(pl.multiple_of((slot >> 1) * LANES, LANES), LANES)]
    v = jnp.where((slot & 1) != upper, pltpu.roll(v, LANES // 2, 1), v)
    return jnp.where(code > 0, v, jnp.zeros_like(v))


def pair_at(row_ref, table, r, pair):
    v0 = block_at(row_ref, table[r, 2 * pair], 0)
    v1 = block_at(row_ref, table[r, 2 * pair + 1], 1)
    return jnp.where(low_lanes(v0.shape[0]), v0, v1)


def densify_half(chunk, table, half, b, first=0):
    tile = chunk.shape[1]
    for r in range(2):
        for pair in range(b.shape[1] // LANES):
            hi, lo = split(pair_at(chunk.at[r], table, 2 * half + r, first + pair))
            lanes = slice(pair * LANES, (pair + 1) * LANES)
            b[r * tile : (r + 1) * tile, lanes] = hi
            b[(2 + r) * tile : (3 + r) * tile, lanes] = lo


def times_half(a, b, lanes):
    depth = b.shape[0]
    return jnp.dot(a[:, :depth], b[:, lanes], preferred_element_type=F32) + jnp.dot(
        a[:, depth:], b[: depth // 2, lanes], preferred_element_type=F32
    )


def lane_blocks(width, step=256):
    return [slice(i, min(i + step, width)) for i in range(0, width, step)]


def ham_kernel(ham_cols, ham_count, ham, a, ham_table, ham_here, sems):
    rows, tile, _ = ham.shape
    copies = [
        pltpu.make_async_copy(ham.at[q], ham_here.at[q], sems.at[q]) for q in range(rows)
    ]
    for copy in copies:
        copy.start()
    fill_table(ham_table, ham_cols, ham_count)
    for q in range(rows):
        copies[q].wait()
        for pair in range(ham_table.shape[1] // 2):
            hi, lo = split(pair_at(ham_here.at[q], ham_table, q, pair))
            a[pair, q * tile : (q + 1) * tile, 0:LANES] = hi
            a[pair, q * tile : (q + 1) * tile, LANES : 2 * LANES] = hi
            a[pair, q * tile : (q + 1) * tile, 2 * LANES : 3 * LANES] = lo


def add_half(step, half, first, dens_table, a, acc_in, chunk, out, b):
    densify_half(chunk, dens_table, half, b, first // LANES)
    pair = shard_of(step) * (dens_table.shape[0] // 2) + half
    for lanes in lane_blocks(out.shape[1]):
        part = times_half(a[pair], b, lanes)
        if acc_in is not None:
            part += acc_in[:, first + lanes.start : first + lanes.stop]
        out[:, lanes] = part


def add_kernel(step, halves, dens_table, a, *rest):
    (acc, b), chunks = rest[-2:], rest[-2 - len(halves) : -2]
    before = rest[0] if step > 0 else None
    for half, chunk in zip(halves, chunks):
        add_half(step, half, 0, dens_table, a, before, chunk, acc, b)
        before = acc


def pick_kernel(half, dens_table, pick):
    rows, deep, width = pick.shape
    here = lax.broadcasted_iota(jnp.int32, (deep, LANES), 0)
    lane = lax.broadcasted_iota(jnp.int32, (deep, LANES), 1)
    block = LANES // 2
    for r in range(rows):
        for pair in range(width // LANES):
            codes = [dens_table[2 * half + r, 2 * pair + side] for side in range(2)]
            wanted = jnp.where(
                lane < block, codes[0] * block - block, codes[1] * block - LANES
            )
            pick[r, :, pair * LANES : (pair + 1) * LANES] = jnp.where(
                here == lane + wanted, 1.0, 0.0
            ).astype(BF16)


def last_kernel(step, half, first, a, acc_in, chunk, pick, m_hi, m_lo, p, above, below, b):
    rows, tile, _ = chunk.shape
    width = p.shape[1]
    for r in range(rows):
        hi, lo = split(chunk[r])
        placed = jnp.dot(
            jnp.concatenate([hi, lo], axis=0),
            pick[r, :, first : first + width],
            preferred_element_type=F32,
        ).astype(BF16)
        b[r * tile : (r + 1) * tile, :] = placed[:tile]
        b[(rows + r) * tile : (rows + r + 1) * tile, :] = placed[tile:]
    pair = shard_of(step) * (a.shape[0] // lax.axis_size("cross")) + half
    tall = p.shape[0]
    both_hi = m_hi[0:2].reshape(2 * tall, tall)
    both_lo = m_lo[0:2].reshape(2 * tall, tall)
    for lanes in lane_blocks(width):
        part = acc_in[:, first + lanes.start : first + lanes.stop] + times_half(a[pair], b, lanes)
        p[:, lanes] = part
        hi, lo = split(part)
        terms = (
            jnp.dot(both_hi, hi, preferred_element_type=F32)
            + jnp.dot(both_hi, lo, preferred_element_type=F32)
            + jnp.dot(both_lo, hi, preferred_element_type=F32)
        )
        above[:, lanes] = terms[:tall]
        below[:, lanes] = terms[tall:]


def margin_kernel(over, hi_out, lo_out):
    rows, tile, _ = over.shape
    for place, s in enumerate((0, 2, 1)):
        for j in range(rows):
            for pair in range(rows // 2):
                at = (s * rows + j) * tile
                lanes = slice(at // LANES * LANES, at // LANES * LANES + LANES)
                v0, v1 = over[2 * pair, :, lanes], over[2 * pair + 1, :, lanes]
                if at % LANES == 0:
                    v1 = pltpu.roll(v1, LANES // 2, 1)
                else:
                    v0 = pltpu.roll(v0, LANES // 2, 1)
                hi, lo = split(jnp.where(low_lanes(tile), v0, v1))
                to = slice(pair * LANES, (pair + 1) * LANES)
                hi_out[place, j * tile : (j + 1) * tile, to] = hi
                lo_out[place, j * tile : (j + 1) * tile, to] = lo


def weigh(out, m_hi, m_lo, s, p):
    for lanes in lane_blocks(p.shape[1]):
        hi, lo = split(p[:, lanes])
        out[:, lanes] = (
            jnp.dot(m_hi[s], hi, preferred_element_type=F32)
            + jnp.dot(m_hi[s], lo, preferred_element_type=F32)
            + jnp.dot(m_lo[s], hi, preferred_element_type=F32)
        )


def own_kernel(m_hi, m_lo, *rest):
    parts, (product, window, term, sems) = rest[:-4], rest[-4:]
    rows, tile, width = product.shape
    copies = []

    def start(ref, out, at):
        for q in range(rows):
            copies.append(
                pltpu.make_async_copy(
                    ref.at[pl.ds(q * tile, tile)],
                    out.at[q, :, pl.ds(at, ref.shape[1])],
                    sems.at[len(copies)],
                )
            )
            copies[-1].start()

    at = 0
    for part in parts:
        start(part, product, at)
        at += part.shape[1]
    at = 0
    for part in parts:
        here = term.at[:, pl.ds(at, part.shape[1])]
        weigh(here, m_hi, m_lo, 2, part)
        start(here, window, width + at)
        at += part.shape[1]
    for copy in copies:
        copy.wait()


def arrived_kernel(at, above, below, window_in, window, sems):
    rows, tile, triple = window.shape
    copies = [
        pltpu.make_async_copy(
            term.at[pl.ds(q * tile, tile)],
            window.at[q, :, pl.ds(start + at, term.shape[1])],
            sems.at[i, q],
        )
        for i, (term, start) in enumerate(((above, 0), (below, triple // 3 * 2)))
        for q in range(rows)
    ]
    for copy in copies:
        copy.start()
    for copy in copies:
        copy.wait()


def call(kernel, name, out_shape, in_spaces, out_spaces, scratch, aliases=None):
    return pl.pallas_call(
        kernel,
        name=name,
        out_shape=out_shape,
        in_specs=[pl.BlockSpec(memory_space=s) for s in in_spaces],
        out_specs=jax.tree.map(lambda s: pl.BlockSpec(memory_space=s), out_spaces),
        scratch_shapes=scratch,
        input_output_aliases=aliases or {},
        cost_estimate=pl.CostEstimate(flops=1024, bytes_accessed=1024, transcendentals=0),
        compiler_params=pltpu.CompilerParams(vmem_limit_bytes=24 << 20),
    )


def shards(ham_tiles, ham_cols, ham_count, dens_tiles, dens_cols, dens_count, over_tiles):
    count = lax.axis_size("cross")
    rows, tile, _ = ham_tiles.shape
    blocks = rows * count
    width = blocks * tile
    tall = rows * tile
    per_shard = rows // 2
    sds = jax.ShapeDtypeStruct

    dens_here = pltpu.with_memory_space_constraint(dens_tiles, pltpu.HBM)
    halves = []
    for h in range(per_shard):
        half = call(
            functools.partial(cut_kernel, h),
            "cut%d" % h,
            sds((2, tile, dens_tiles.shape[2]), F32),
            (pltpu.HBM,),
            VMEM,
            [pltpu.SemaphoreType.DMA],
        )(dens_here)
        half, dens_here = lax.optimization_barrier((half, dens_here))
        halves.append(half)
    halves[0], dens_cols = lax.optimization_barrier((halves[0], dens_cols))
    arrivals = [halves, [pass_on(h, 1) for h in halves]]
    ham_cols, ham_count, dens_cols, dens_count, ham_tiles = (
        pltpu.with_memory_space_constraint(x, pltpu.HBM)
        for x in (ham_cols, ham_count, dens_cols, dens_count, ham_tiles)
    )
    table = call(
        table_kernel,
        "table",
        sds((rows, blocks), jnp.int32),
        (SMEM, SMEM),
        SMEM,
        [],
    )(dens_cols, dens_count)
    tables = [table] + [pass_on(table, step) for step in range(1, count)]
    m_hi, m_lo = call(
        margin_kernel,
        "margin",
        (sds((3, tall, tall), BF16),) * 2,
        (VMEM,),
        (VMEM, VMEM),
        [],
    )(over_tiles)
    a = call(
        ham_kernel,
        "ham",
        sds((blocks // 2, tall, 3 * LANES), BF16),
        (SMEM, SMEM, pltpu.HBM),
        VMEM,
        [
            pltpu.SMEM((rows, blocks), jnp.int32),
            VMEM(ham_tiles.shape, F32),
            pltpu.SemaphoreType.DMA((rows,)),
        ],
    )(ham_cols, ham_count, ham_tiles)

    def add(step, chunks, acc):
        return call(
            functools.partial(add_kernel, step, list(range(len(chunks)))),
            "add%d" % step,
            sds((tall, width), F32),
            (SMEM,) + (VMEM,) * (1 + len(chunks) + (step > 0)),
            VMEM,
            [VMEM((4 * tile, width), BF16)],
        )(tables[step], a, *([acc] if step > 0 else []), *chunks)

    pieces = (width * 3 // 8, width * 3 // 8, width // 4)
    acc = None
    for step in range(1, count - 1):
        now = arrivals[-1]
        if step == 1:
            now[0], a = lax.optimization_barrier((now[0], a))
            now[-1], *tables = lax.optimization_barrier((now[-1], *tables))
        else:
            now[0], acc = lax.optimization_barrier((now[0], acc))
        if step == 2:
            pick = call(
                functools.partial(pick_kernel, per_shard - 1),
                "pick",
                sds((2, dens_tiles.shape[2], width), BF16),
                (SMEM,),
                VMEM,
                [],
            )(tables[-1])
            now[-1], m_hi, m_lo, pick = lax.optimization_barrier((now[-1], m_hi, m_lo, pick))
        acc = add(step - 1, arrivals[-2], acc)
        arrivals.append([pass_on(h, 1) for h in now])
    acc = add(count - 2, arrivals[-2], acc)
    acc = add(count - 1, arrivals[-1][:-1], acc)

    parts, befores, afters = [], [], []
    for i, piece in enumerate(pieces):
        part, above, below = call(
            functools.partial(last_kernel, count - 1, per_shard - 1, sum(pieces[:i])),
            "last%d" % i,
            [sds((tall, piece), F32)] * 3,
            (VMEM,) * 6,
            [VMEM] * 3,
            [VMEM((4 * tile, piece), BF16)],
        )(a, acc, arrivals[-1][-1], pick, m_hi, m_lo)
        if i + 1 < len(pieces):
            part, acc = lax.optimization_barrier((part, acc))
        parts.append(part)
        befores.append(rotate(below, 1))
        afters.append(rotate(above, -1))
    product, window = call(
        own_kernel,
        "own",
        (sds((rows, tile, width), F32), sds((rows, tile, 3 * width), F32)),
        (VMEM,) * (2 + len(pieces)),
        (pl.ANY, pl.ANY),
        [VMEM((tall, width), F32), pltpu.SemaphoreType.DMA((2 * len(pieces) * rows,))],
    )(m_hi, m_lo, *parts)
    for i in range(len(pieces)):
        window = call(
            functools.partial(arrived_kernel, sum(pieces[:i])),
            "arrived%d" % i,
            sds((rows, tile, 3 * width), F32),
            (VMEM, VMEM, pl.ANY),
            pl.ANY,
            [pltpu.SemaphoreType.DMA((2, rows))],
            {2: 0},
        )(befores[i], afters[i], window)
    return (product, window)


def solution(mesh):
    whole = P(AXES)
    return jax.shard_map(
        shards,
        mesh=mesh,
        in_specs=(whole,) * 7,
        out_specs=(whole, whole),
        check_vma=False,
    )
```

```python
import functools

import jax
import jax.numpy as jnp
from jax import lax
from jax.experimental import pallas as pl
from jax.experimental.pallas import tpu as pltpu
from jax.sharding import PartitionSpec as P

LANES = 128
F32 = jnp.float32
BF16 = jnp.bfloat16
VMEM = pltpu.VMEM
SMEM = pltpu.SMEM


AXES = ("parts", "line", "cross")


def permute(x, target):
    parts, line, cross = (lax.axis_size(axis) for axis in AXES)
    flat = lambda p, g, c: (p % parts * line + g % line) * cross + c
    places = [(p, g, c) for p in range(parts) for g in range(line) for c in range(cross)]
    return lax.ppermute(x, AXES, [(flat(*place), flat(*target(*place))) for place in places])


def rotate(x, by):
    return permute(x, lambda p, g, c: (p, g + by, c))


def ring_order(count):
    return list(range(0, count, 2))[:1] + list(range(1, count, 2)) + list(range(0, count, 2))[:0:-1]


def pass_on(x, by):
    order = ring_order(lax.axis_size("cross"))
    after = {d: order[(i + by) % len(order)] for i, d in enumerate(order)}
    return permute(x, lambda p, g, c: (p, g, after[c]))


def shard_of(step):
    order = ring_order(lax.axis_size("cross"))
    me = lax.axis_index("cross")
    owner = jnp.int32(0)
    for i, d in enumerate(order):
        owner = jnp.where(me == d, order[i - step], owner)
    return owner


def fill_table(table, columns, counts):
    rows, width = table.shape
    for r in range(rows):
        for c in range(width):
            table[r, c] = 0
        for slot in range(columns.shape[1]):

            @pl.when(slot < counts[r])
            def _(r=r, slot=slot):
                table[r, columns[r, slot]] = slot + 1


def cut_kernel(half, dens, out, sem):
    copy = pltpu.make_async_copy(dens.at[pl.ds(2 * half, 2)], out, sem)
    copy.start()
    copy.wait()


def table_kernel(columns, counts, table):
    fill_table(table, columns, counts)


def split(v):
    hi = v.astype(BF16)
    return hi, (v - hi.astype(F32)).astype(BF16)


def low_lanes(rows):
    return lax.broadcasted_iota(jnp.int32, (rows, LANES), 1) < LANES // 2


def block_at(row_ref, code, upper):
    slot = jnp.maximum(code - 1, 0)
    v = row_ref[:, pl.ds(pl.multiple_of((slot >> 1) * LANES, LANES), LANES)]
    v = jnp.where((slot & 1) != upper, pltpu.roll(v, LANES // 2, 1), v)
    return jnp.where(code > 0, v, jnp.zeros_like(v))


def pair_at(row_ref, table, r, pair):
    v0 = block_at(row_ref, table[r, 2 * pair], 0)
    v1 = block_at(row_ref, table[r, 2 * pair + 1], 1)
    return jnp.where(low_lanes(v0.shape[0]), v0, v1)


def densify_half(chunk, table, half, b, first=0):
    tile = chunk.shape[1]
    for r in range(2):
        for pair in range(b.shape[1] // LANES):
            hi, lo = split(pair_at(chunk.at[r], table, 2 * half + r, first + pair))
            lanes = slice(pair * LANES, (pair + 1) * LANES)
            b[r * tile : (r + 1) * tile, lanes] = hi
            b[(2 + r) * tile : (3 + r) * tile, lanes] = lo


def times_half(a, b, lanes):
    depth = b.shape[0]
    return jnp.dot(a[:, :depth], b[:, lanes], preferred_element_type=F32) + jnp.dot(
        a[:, depth:], b[: depth // 2, lanes], preferred_element_type=F32
    )


def lane_blocks(width, step=256):
    return [slice(i, min(i + step, width)) for i in range(0, width, step)]


def ham_kernel(ham_cols, ham_count, ham, a, ham_table, ham_here, sems):
    rows, tile, _ = ham.shape
    copies = [
        pltpu.make_async_copy(ham.at[q], ham_here.at[q], sems.at[q]) for q in range(rows)
    ]
    for copy in copies:
        copy.start()
    fill_table(ham_table, ham_cols, ham_count)
    for q in range(rows):
        copies[q].wait()
        for pair in range(ham_table.shape[1] // 2):
            hi, lo = split(pair_at(ham_here.at[q], ham_table, q, pair))
            a[pair, q * tile : (q + 1) * tile, 0:LANES] = hi
            a[pair, q * tile : (q + 1) * tile, LANES : 2 * LANES] = hi
            a[pair, q * tile : (q + 1) * tile, 2 * LANES : 3 * LANES] = lo


def add_half(step, half, first, dens_table, a, acc_in, chunk, out, b):
    densify_half(chunk, dens_table, half, b, first // LANES)
    pair = shard_of(step) * (dens_table.shape[0] // 2) + half
    for lanes in lane_blocks(out.shape[1]):
        part = times_half(a[pair], b, lanes)
        if acc_in is not None:
            part += acc_in[:, first + lanes.start : first + lanes.stop]
        out[:, lanes] = part


def add_kernel(step, halves, dens_table, a, *rest):
    (acc, b), chunks = rest[-2:], rest[-2 - len(halves) : -2]
    before = rest[0] if step > 0 else None
    for half, chunk in zip(halves, chunks):
        add_half(step, half, 0, dens_table, a, before, chunk, acc, b)
        before = acc


def pick_kernel(half, dens_table, pick):
    rows, deep, width = pick.shape
    here = lax.broadcasted_iota(jnp.int32, (deep, LANES), 0)
    lane = lax.broadcasted_iota(jnp.int32, (deep, LANES), 1)
    block = LANES // 2
    for r in range(rows):
        for pair in range(width // LANES):
            codes = [dens_table[2 * half + r, 2 * pair + side] for side in range(2)]
            wanted = jnp.where(
                lane < block, codes[0] * block - block, codes[1] * block - LANES
            )
            pick[r, :, pair * LANES : (pair + 1) * LANES] = jnp.where(
                here == lane + wanted, 1.0, 0.0
            ).astype(BF16)


def last_kernel(step, half, first, a, acc_in, chunk, pick, m_hi, m_lo, p, above, below, b):
    rows, tile, _ = chunk.shape
    width = p.shape[1]
    for r in range(rows):
        hi, lo = split(chunk[r])
        placed = jnp.dot(
            jnp.concatenate([hi, lo], axis=0),
            pick[r, :, first : first + width],
            preferred_element_type=F32,
        ).astype(BF16)
        b[r * tile : (r + 1) * tile, :] = placed[:tile]
        b[(rows + r) * tile : (rows + r + 1) * tile, :] = placed[tile:]
    pair = shard_of(step) * (a.shape[0] // lax.axis_size("cross")) + half
    tall = p.shape[0]
    both_hi = m_hi[0:2].reshape(2 * tall, tall)
    both_lo = m_lo[0:2].reshape(2 * tall, tall)
    for lanes in lane_blocks(width):
        part = acc_in[:, first + lanes.start : first + lanes.stop] + times_half(a[pair], b, lanes)
        p[:, lanes] = part
        hi, lo = split(part)
        terms = (
            jnp.dot(both_hi, hi, preferred_element_type=F32)
            + jnp.dot(both_hi, lo, preferred_element_type=F32)
            + jnp.dot(both_lo, hi, preferred_element_type=F32)
        )
        above[:, lanes] = terms[:tall]
        below[:, lanes] = terms[tall:]


def margin_kernel(over, hi_out, lo_out):
    rows, tile, _ = over.shape
    for place, s in enumerate((0, 2, 1)):
        for j in range(rows):
            for pair in range(rows // 2):
                at = (s * rows + j) * tile
                lanes = slice(at // LANES * LANES, at // LANES * LANES + LANES)
                v0, v1 = over[2 * pair, :, lanes], over[2 * pair + 1, :, lanes]
                if at % LANES == 0:
                    v1 = pltpu.roll(v1, LANES // 2, 1)
                else:
                    v0 = pltpu.roll(v0, LANES // 2, 1)
                hi, lo = split(jnp.where(low_lanes(tile), v0, v1))
                to = slice(pair * LANES, (pair + 1) * LANES)
                hi_out[place, j * tile : (j + 1) * tile, to] = hi
                lo_out[place, j * tile : (j + 1) * tile, to] = lo


def weigh(out, m_hi, m_lo, s, p):
    for lanes in lane_blocks(p.shape[1]):
        hi, lo = split(p[:, lanes])
        out[:, lanes] = (
            jnp.dot(m_hi[s], hi, preferred_element_type=F32)
            + jnp.dot(m_hi[s], lo, preferred_element_type=F32)
            + jnp.dot(m_lo[s], hi, preferred_element_type=F32)
        )


def own_kernel(m_hi, m_lo, *rest):
    parts, (product, window, term, sems) = rest[:-4], rest[-4:]
    rows, tile, width = product.shape
    copies = []

    def start(ref, out, at):
        for q in range(rows):
            copies.append(
                pltpu.make_async_copy(
                    ref.at[pl.ds(q * tile, tile)],
                    out.at[q, :, pl.ds(at, ref.shape[1])],
                    sems.at[len(copies)],
                )
            )
            copies[-1].start()

    at = 0
    for part in parts:
        start(part, product, at)
        at += part.shape[1]
    at = 0
    for part in parts:
        here = term.at[:, pl.ds(at, part.shape[1])]
        weigh(here, m_hi, m_lo, 2, part)
        start(here, window, width + at)
        at += part.shape[1]
    for copy in copies:
        copy.wait()


def arrived_kernel(at, above, below, window_in, window, sems):
    rows, tile, triple = window.shape
    copies = [
        pltpu.make_async_copy(
            term.at[pl.ds(q * tile, tile)],
            window.at[q, :, pl.ds(start + at, term.shape[1])],
            sems.at[i, q],
        )
        for i, (term, start) in enumerate(((above, 0), (below, triple // 3 * 2)))
        for q in range(rows)
    ]
    for copy in copies:
        copy.start()
    for copy in copies:
        copy.wait()


def call(kernel, name, out_shape, in_spaces, out_spaces, scratch, aliases=None):
    return pl.pallas_call(
        kernel,
        name=name,
        out_shape=out_shape,
        in_specs=[pl.BlockSpec(memory_space=s) for s in in_spaces],
        out_specs=jax.tree.map(lambda s: pl.BlockSpec(memory_space=s), out_spaces),
        scratch_shapes=scratch,
        input_output_aliases=aliases or {},
        cost_estimate=pl.CostEstimate(flops=1024, bytes_accessed=1024, transcendentals=0),
        compiler_params=pltpu.CompilerParams(vmem_limit_bytes=24 << 20),
    )


def shards(ham_tiles, ham_cols, ham_count, dens_tiles, dens_cols, dens_count, over_tiles):
    count = lax.axis_size("cross")
    rows, tile, _ = ham_tiles.shape
    blocks = rows * count
    width = blocks * tile
    tall = rows * tile
    per_shard = rows // 2
    sds = jax.ShapeDtypeStruct

    dens_here = pltpu.with_memory_space_constraint(dens_tiles, pltpu.HBM)
    halves = []
    for h in range(per_shard):
        half = call(
            functools.partial(cut_kernel, h),
            "cut%d" % h,
            sds((2, tile, dens_tiles.shape[2]), F32),
            (pltpu.HBM,),
            VMEM,
            [pltpu.SemaphoreType.DMA],
        )(dens_here)
        half, dens_here = lax.optimization_barrier((half, dens_here))
        halves.append(half)
    halves[0], dens_cols = lax.optimization_barrier((halves[0], dens_cols))
    arrivals = [halves, [pass_on(h, 1) for h in halves]]
    ham_cols, ham_count, dens_cols, dens_count, ham_tiles = (
        pltpu.with_memory_space_constraint(x, pltpu.HBM)
        for x in (ham_cols, ham_count, dens_cols, dens_count, ham_tiles)
    )
    table = call(
        table_kernel,
        "table",
        sds((rows, blocks), jnp.int32),
        (SMEM, SMEM),
        SMEM,
        [],
    )(dens_cols, dens_count)
    tables = [table] + [pass_on(table, step) for step in range(1, count)]
    m_hi, m_lo = call(
        margin_kernel,
        "margin",
        (sds((3, tall, tall), BF16),) * 2,
        (VMEM,),
        (VMEM, VMEM),
        [],
    )(over_tiles)
    a = call(
        ham_kernel,
        "ham",
        sds((blocks // 2, tall, 3 * LANES), BF16),
        (SMEM, SMEM, pltpu.HBM),
        VMEM,
        [
            pltpu.SMEM((rows, blocks), jnp.int32),
            VMEM(ham_tiles.shape, F32),
            pltpu.SemaphoreType.DMA((rows,)),
        ],
    )(ham_cols, ham_count, ham_tiles)

    def add(step, chunks, acc):
        return call(
            functools.partial(add_kernel, step, list(range(len(chunks)))),
            "add%d" % step,
            sds((tall, width), F32),
            (SMEM,) + (VMEM,) * (1 + len(chunks) + (step > 0)),
            VMEM,
            [VMEM((4 * tile, width), BF16)],
        )(tables[step], a, *([acc] if step > 0 else []), *chunks)

    pieces = (width // 4,) * 4
    acc = None
    for step in range(1, count - 1):
        now = arrivals[-1]
        if step == 1:
            now[0], a = lax.optimization_barrier((now[0], a))
            now[-1], *tables = lax.optimization_barrier((now[-1], *tables))
        else:
            now[0], acc = lax.optimization_barrier((now[0], acc))
        if step == 2:
            pick = call(
                functools.partial(pick_kernel, per_shard - 1),
                "pick",
                sds((2, dens_tiles.shape[2], width), BF16),
                (SMEM,),
                VMEM,
                [],
            )(tables[-1])
            now[-1], m_hi, m_lo, pick = lax.optimization_barrier((now[-1], m_hi, m_lo, pick))
        acc = add(step - 1, arrivals[-2], acc)
        arrivals.append([pass_on(h, 1) for h in now])
    acc = add(count - 2, arrivals[-2], acc)
    acc = add(count - 1, arrivals[-1][:-1], acc)

    parts, befores, afters = [], [], []
    for i, piece in enumerate(pieces):
        part, above, below = call(
            functools.partial(last_kernel, count - 1, per_shard - 1, sum(pieces[:i])),
            "last%d" % i,
            [sds((tall, piece), F32)] * 3,
            (VMEM,) * 6,
            [VMEM] * 3,
            [VMEM((4 * tile, piece), BF16)],
        )(a, acc, arrivals[-1][-1], pick, m_hi, m_lo)
        if i + 1 < len(pieces):
            part, acc = lax.optimization_barrier((part, acc))
        parts.append(part)
        befores.append(rotate(below, 1))
        afters.append(rotate(above, -1))
    product, window = call(
        own_kernel,
        "own",
        (sds((rows, tile, width), F32), sds((rows, tile, 3 * width), F32)),
        (VMEM,) * (2 + len(pieces)),
        (pl.ANY, pl.ANY),
        [VMEM((tall, width), F32), pltpu.SemaphoreType.DMA((2 * len(pieces) * rows,))],
    )(m_hi, m_lo, *parts)
    for i in range(len(pieces)):
        window = call(
            functools.partial(arrived_kernel, sum(pieces[:i])),
            "arrived%d" % i,
            sds((rows, tile, 3 * width), F32),
            (VMEM, VMEM, pl.ANY),
            pl.ANY,
            [pltpu.SemaphoreType.DMA((2, rows))],
            {2: 0},
        )(befores[i], afters[i], window)
    return (product, window)


def solution(mesh):
    whole = P(AXES)
    return jax.shard_map(
        shards,
        mesh=mesh,
        in_specs=(whole,) * 7,
        out_specs=(whole, whole),
        check_vma=False,
    )
```

```python
import functools

import jax
import jax.numpy as jnp
from jax import lax
from jax.experimental import pallas as pl
from jax.experimental.pallas import tpu as pltpu
from jax.sharding import PartitionSpec as P

LANES = 128
F32 = jnp.float32
BF16 = jnp.bfloat16
VMEM = pltpu.VMEM
SMEM = pltpu.SMEM


AXES = ("parts", "line", "cross")


def permute(x, target):
    parts, line, cross = (lax.axis_size(axis) for axis in AXES)
    flat = lambda p, g, c: (p % parts * line + g % line) * cross + c
    places = [(p, g, c) for p in range(parts) for g in range(line) for c in range(cross)]
    return lax.ppermute(x, AXES, [(flat(*place), flat(*target(*place))) for place in places])


def rotate(x, by):
    return permute(x, lambda p, g, c: (p, g + by, c))


def ring_order(count):
    return list(range(0, count, 2))[:1] + list(range(1, count, 2)) + list(range(0, count, 2))[:0:-1]


def pass_on(x, by):
    order = ring_order(lax.axis_size("cross"))
    after = {d: order[(i + by) % len(order)] for i, d in enumerate(order)}
    return permute(x, lambda p, g, c: (p, g, after[c]))


def shard_of(step):
    order = ring_order(lax.axis_size("cross"))
    me = lax.axis_index("cross")
    owner = jnp.int32(0)
    for i, d in enumerate(order):
        owner = jnp.where(me == d, order[i - step], owner)
    return owner


def fill_table(table, columns, counts):
    rows, width = table.shape
    for r in range(rows):
        for c in range(width):
            table[r, c] = 0
        for slot in range(columns.shape[1]):

            @pl.when(slot < counts[r])
            def _(r=r, slot=slot):
                table[r, columns[r, slot]] = slot + 1


def cut_kernel(half, dens, out, sem):
    copy = pltpu.make_async_copy(dens.at[pl.ds(2 * half, 2)], out, sem)
    copy.start()
    copy.wait()


def table_kernel(columns, counts, table):
    fill_table(table, columns, counts)


def split(v):
    hi = v.astype(BF16)
    return hi, (v - hi.astype(F32)).astype(BF16)


def low_lanes(rows):
    return lax.broadcasted_iota(jnp.int32, (rows, LANES), 1) < LANES // 2


def block_at(row_ref, code, upper):
    slot = jnp.maximum(code - 1, 0)
    v = row_ref[:, pl.ds(pl.multiple_of((slot >> 1) * LANES, LANES), LANES)]
    v = jnp.where((slot & 1) != upper, pltpu.roll(v, LANES // 2, 1), v)
    return jnp.where(code > 0, v, jnp.zeros_like(v))


def pair_at(row_ref, table, r, pair):
    v0 = block_at(row_ref, table[r, 2 * pair], 0)
    v1 = block_at(row_ref, table[r, 2 * pair + 1], 1)
    return jnp.where(low_lanes(v0.shape[0]), v0, v1)


def densify_half(chunk, table, half, b, first=0):
    tile = chunk.shape[1]
    for r in range(2):
        for pair in range(b.shape[1] // LANES):
            hi, lo = split(pair_at(chunk.at[r], table, 2 * half + r, first + pair))
            lanes = slice(pair * LANES, (pair + 1) * LANES)
            b[r * tile : (r + 1) * tile, lanes] = hi
            b[(2 + r) * tile : (3 + r) * tile, lanes] = lo


def times_half(a, b, lanes):
    depth = b.shape[0]
    return jnp.dot(a[:, :depth], b[:, lanes], preferred_element_type=F32) + jnp.dot(
        a[:, depth:], b[: depth // 2, lanes], preferred_element_type=F32
    )


def lane_blocks(width, step=256):
    return [slice(i, min(i + step, width)) for i in range(0, width, step)]


def ham_kernel(ham_cols, ham_count, ham, a, ham_table, ham_here, sems):
    rows, tile, _ = ham.shape
    copies = [
        pltpu.make_async_copy(ham.at[q], ham_here.at[q], sems.at[q]) for q in range(rows)
    ]
    for copy in copies:
        copy.start()
    fill_table(ham_table, ham_cols, ham_count)
    for q in range(rows):
        copies[q].wait()
        for pair in range(ham_table.shape[1] // 2):
            hi, lo = split(pair_at(ham_here.at[q], ham_table, q, pair))
            a[pair, q * tile : (q + 1) * tile, 0:LANES] = hi
            a[pair, q * tile : (q + 1) * tile, LANES : 2 * LANES] = hi
            a[pair, q * tile : (q + 1) * tile, 2 * LANES : 3 * LANES] = lo


def add_half(step, half, first, dens_table, a, acc_in, chunk, out, b):
    densify_half(chunk, dens_table, half, b, first // LANES)
    pair = shard_of(step) * (dens_table.shape[0] // 2) + half
    for lanes in lane_blocks(out.shape[1]):
        part = times_half(a[pair], b, lanes)
        if acc_in is not None:
            part += acc_in[:, first + lanes.start : first + lanes.stop]
        out[:, lanes] = part


def add_kernel(step, halves, dens_table, a, *rest):
    (acc, b), chunks = rest[-2:], rest[-2 - len(halves) : -2]
    before = rest[0] if step > 0 else None
    for half, chunk in zip(halves, chunks):
        add_half(step, half, 0, dens_table, a, before, chunk, acc, b)
        before = acc


def pick_kernel(half, dens_table, pick):
    rows, deep, width = pick.shape
    here = lax.broadcasted_iota(jnp.int32, (deep, LANES), 0)
    lane = lax.broadcasted_iota(jnp.int32, (deep, LANES), 1)
    block = LANES // 2
    for r in range(rows):
        for pair in range(width // LANES):
            codes = [dens_table[2 * half + r, 2 * pair + side] for side in range(2)]
            wanted = jnp.where(
                lane < block, codes[0] * block - block, codes[1] * block - LANES
            )
            pick[r, :, pair * LANES : (pair + 1) * LANES] = jnp.where(
                here == lane + wanted, 1.0, 0.0
            ).astype(BF16)


def last_kernel(step, half, first, a, acc_in, chunk, pick, m_hi, m_lo, p, above, below, b):
    rows, tile, _ = chunk.shape
    width = p.shape[1]
    for r in range(rows):
        hi, lo = split(chunk[r])
        placed = jnp.dot(
            jnp.concatenate([hi, lo], axis=0),
            pick[r, :, first : first + width],
            preferred_element_type=F32,
        ).astype(BF16)
        b[r * tile : (r + 1) * tile, :] = placed[:tile]
        b[(rows + r) * tile : (rows + r + 1) * tile, :] = placed[tile:]
    pair = shard_of(step) * (a.shape[0] // lax.axis_size("cross")) + half
    tall = p.shape[0]
    both_hi = m_hi[0:2].reshape(2 * tall, tall)
    both_lo = m_lo[0:2].reshape(2 * tall, tall)
    for lanes in lane_blocks(width):
        part = acc_in[:, first + lanes.start : first + lanes.stop] + times_half(a[pair], b, lanes)
        p[:, lanes] = part
        hi, lo = split(part)
        terms = (
            jnp.dot(both_hi, hi, preferred_element_type=F32)
            + jnp.dot(both_hi, lo, preferred_element_type=F32)
            + jnp.dot(both_lo, hi, preferred_element_type=F32)
        )
        above[:, lanes] = terms[:tall]
        below[:, lanes] = terms[tall:]


def margin_kernel(over, hi_out, lo_out):
    rows, tile, _ = over.shape
    for place, s in enumerate((0, 2, 1)):
        for j in range(rows):
            for pair in range(rows // 2):
                at = (s * rows + j) * tile
                lanes = slice(at // LANES * LANES, at // LANES * LANES + LANES)
                v0, v1 = over[2 * pair, :, lanes], over[2 * pair + 1, :, lanes]
                if at % LANES == 0:
                    v1 = pltpu.roll(v1, LANES // 2, 1)
                else:
                    v0 = pltpu.roll(v0, LANES // 2, 1)
                hi, lo = split(jnp.where(low_lanes(tile), v0, v1))
                to = slice(pair * LANES, (pair + 1) * LANES)
                hi_out[place, j * tile : (j + 1) * tile, to] = hi
                lo_out[place, j * tile : (j + 1) * tile, to] = lo


def weigh(out, m_hi, m_lo, s, p):
    for lanes in lane_blocks(p.shape[1]):
        hi, lo = split(p[:, lanes])
        out[:, lanes] = (
            jnp.dot(m_hi[s], hi, preferred_element_type=F32)
            + jnp.dot(m_hi[s], lo, preferred_element_type=F32)
            + jnp.dot(m_lo[s], hi, preferred_element_type=F32)
        )


def own_kernel(m_hi, m_lo, *rest):
    parts, (product, window, term, sems) = rest[:-4], rest[-4:]
    rows, tile, width = product.shape
    copies = []

    def start(ref, out, at):
        for q in range(rows):
            copies.append(
                pltpu.make_async_copy(
                    ref.at[pl.ds(q * tile, tile)],
                    out.at[q, :, pl.ds(at, ref.shape[1])],
                    sems.at[len(copies)],
                )
            )
            copies[-1].start()

    at = 0
    for part in parts:
        start(part, product, at)
        at += part.shape[1]
    at = 0
    for part in parts:
        here = term.at[:, pl.ds(at, part.shape[1])]
        weigh(here, m_hi, m_lo, 2, part)
        start(here, window, width + at)
        at += part.shape[1]
    for copy in copies:
        copy.wait()


def arrived_kernel(at, before_first, one, other, window_in, window, sems):
    rows, tile, triple = window.shape
    above, below = (one, other) if before_first else (other, one)
    copies = [
        pltpu.make_async_copy(
            term.at[pl.ds(q * tile, tile)],
            window.at[q, :, pl.ds(start + at, term.shape[1])],
            sems.at[i, q],
        )
        for i, (term, start) in enumerate(((above, 0), (below, triple // 3 * 2)))
        for q in range(rows)
    ]
    for copy in copies:
        copy.start()
    for copy in copies:
        copy.wait()


def call(kernel, name, out_shape, in_spaces, out_spaces, scratch, aliases=None):
    return pl.pallas_call(
        kernel,
        name=name,
        out_shape=out_shape,
        in_specs=[pl.BlockSpec(memory_space=s) for s in in_spaces],
        out_specs=jax.tree.map(lambda s: pl.BlockSpec(memory_space=s), out_spaces),
        scratch_shapes=scratch,
        input_output_aliases=aliases or {},
        cost_estimate=pl.CostEstimate(flops=1024, bytes_accessed=1024, transcendentals=0),
        compiler_params=pltpu.CompilerParams(vmem_limit_bytes=24 << 20),
    )


def shards(ham_tiles, ham_cols, ham_count, dens_tiles, dens_cols, dens_count, over_tiles):
    count = lax.axis_size("cross")
    rows, tile, _ = ham_tiles.shape
    blocks = rows * count
    width = blocks * tile
    tall = rows * tile
    per_shard = rows // 2
    sds = jax.ShapeDtypeStruct

    dens_here = pltpu.with_memory_space_constraint(dens_tiles, pltpu.HBM)
    halves = []
    for h in range(per_shard):
        half = call(
            functools.partial(cut_kernel, h),
            "cut%d" % h,
            sds((2, tile, dens_tiles.shape[2]), F32),
            (pltpu.HBM,),
            VMEM,
            [pltpu.SemaphoreType.DMA],
        )(dens_here)
        half, dens_here = lax.optimization_barrier((half, dens_here))
        halves.append(half)
    halves[0], dens_cols = lax.optimization_barrier((halves[0], dens_cols))
    arrivals = [halves, [pass_on(h, 1) for h in halves]]
    ham_cols, ham_count, dens_cols, dens_count, ham_tiles = (
        pltpu.with_memory_space_constraint(x, pltpu.HBM)
        for x in (ham_cols, ham_count, dens_cols, dens_count, ham_tiles)
    )
    table = call(
        table_kernel,
        "table",
        sds((rows, blocks), jnp.int32),
        (SMEM, SMEM),
        SMEM,
        [],
    )(dens_cols, dens_count)
    tables = [table] + [pass_on(table, step) for step in range(1, count)]
    m_hi, m_lo = call(
        margin_kernel,
        "margin",
        (sds((3, tall, tall), BF16),) * 2,
        (VMEM,),
        (VMEM, VMEM),
        [],
    )(over_tiles)
    a = call(
        ham_kernel,
        "ham",
        sds((blocks // 2, tall, 3 * LANES), BF16),
        (SMEM, SMEM, pltpu.HBM),
        VMEM,
        [
            pltpu.SMEM((rows, blocks), jnp.int32),
            VMEM(ham_tiles.shape, F32),
            pltpu.SemaphoreType.DMA((rows,)),
        ],
    )(ham_cols, ham_count, ham_tiles)

    def add(step, chunks, acc):
        return call(
            functools.partial(add_kernel, step, list(range(len(chunks)))),
            "add%d" % step,
            sds((tall, width), F32),
            (SMEM,) + (VMEM,) * (1 + len(chunks) + (step > 0)),
            VMEM,
            [VMEM((4 * tile, width), BF16)],
        )(tables[step], a, *([acc] if step > 0 else []), *chunks)

    pieces = (width // 4,) * 4
    acc = None
    for step in range(1, count - 1):
        now = arrivals[-1]
        if step == 1:
            now[0], a = lax.optimization_barrier((now[0], a))
            now[-1], *tables = lax.optimization_barrier((now[-1], *tables))
        else:
            now[0], acc = lax.optimization_barrier((now[0], acc))
        if step == 2:
            pick = call(
                functools.partial(pick_kernel, per_shard - 1),
                "pick",
                sds((2, dens_tiles.shape[2], width), BF16),
                (SMEM,),
                VMEM,
                [],
            )(tables[-1])
            now[-1], m_hi, m_lo, pick = lax.optimization_barrier((now[-1], m_hi, m_lo, pick))
        acc = add(step - 1, arrivals[-2], acc)
        arrivals.append([pass_on(h, 1) for h in now])
    acc = add(count - 2, arrivals[-2], acc)
    acc = add(count - 1, arrivals[-1][:-1], acc)

    parts, befores, afters = [], [], []
    for i, piece in enumerate(pieces):
        part, above, below = call(
            functools.partial(last_kernel, count - 1, per_shard - 1, sum(pieces[:i])),
            "last%d" % i,
            [sds((tall, piece), F32)] * 3,
            (VMEM,) * 6,
            [VMEM] * 3,
            [VMEM((4 * tile, piece), BF16)],
        )(a, acc, arrivals[-1][-1], pick, m_hi, m_lo)
        if i + 1 < len(pieces):
            part, acc = lax.optimization_barrier((part, acc))
        parts.append(part)
        if i == 0:
            afters.append(rotate(above, -1))
        befores.append(rotate(below, 1))
        if i > 0:
            afters.append(rotate(above, -1))
    product, window = call(
        own_kernel,
        "own",
        (sds((rows, tile, width), F32), sds((rows, tile, 3 * width), F32)),
        (VMEM,) * (2 + len(pieces)),
        (pl.ANY, pl.ANY),
        [VMEM((tall, width), F32), pltpu.SemaphoreType.DMA((2 * len(pieces) * rows,))],
    )(m_hi, m_lo, *parts)
    for i in range(len(pieces)):
        window = call(
            functools.partial(arrived_kernel, sum(pieces[:i]), i > 0),
            "arrived%d" % i,
            sds((rows, tile, 3 * width), F32),
            (VMEM, VMEM, pl.ANY),
            pl.ANY,
            [pltpu.SemaphoreType.DMA((2, rows))],
            {2: 0},
        )(*((befores[i], afters[i]) if i > 0 else (afters[i], befores[i])), window)
    return (product, window)


def solution(mesh):
    whole = P(AXES)
    return jax.shard_map(
        shards,
        mesh=mesh,
        in_specs=(whole,) * 7,
        out_specs=(whole, whole),
        check_vma=False,
    )
```

```python
import functools

import jax
import jax.numpy as jnp
from jax import lax
from jax.experimental import pallas as pl
from jax.experimental.pallas import tpu as pltpu
from jax.sharding import PartitionSpec as P

LANES = 128
F32 = jnp.float32
BF16 = jnp.bfloat16
VMEM = pltpu.VMEM
SMEM = pltpu.SMEM


AXES = ("parts", "line", "cross")


def permute(x, target):
    parts, line, cross = (lax.axis_size(axis) for axis in AXES)
    flat = lambda p, g, c: (p % parts * line + g % line) * cross + c
    places = [(p, g, c) for p in range(parts) for g in range(line) for c in range(cross)]
    return lax.ppermute(x, AXES, [(flat(*place), flat(*target(*place))) for place in places])


def rotate(x, by):
    return permute(x, lambda p, g, c: (p, g + by, c))


def ring_order(count):
    return list(range(0, count, 2))[:1] + list(range(1, count, 2)) + list(range(0, count, 2))[:0:-1]


def pass_on(x, by):
    order = ring_order(lax.axis_size("cross"))
    after = {d: order[(i + by) % len(order)] for i, d in enumerate(order)}
    return permute(x, lambda p, g, c: (p, g, after[c]))


def shard_of(step):
    order = ring_order(lax.axis_size("cross"))
    me = lax.axis_index("cross")
    owner = jnp.int32(0)
    for i, d in enumerate(order):
        owner = jnp.where(me == d, order[i - step], owner)
    return owner


def fill_table(table, columns, counts):
    rows, width = table.shape
    for r in range(rows):
        for c in range(width):
            table[r, c] = 0
        for slot in range(columns.shape[1]):

            @pl.when(slot < counts[r])
            def _(r=r, slot=slot):
                table[r, columns[r, slot]] = slot + 1


def cut_kernel(dens, *rest):
    halves, sems = rest[:-1], rest[-1]
    copies = [
        pltpu.make_async_copy(dens.at[pl.ds(2 * h, 2)], half, sems.at[h])
        for h, half in enumerate(halves)
    ]
    for copy in copies:
        copy.start()
    for copy in copies:
        copy.wait()


def table_kernel(columns, counts, table):
    fill_table(table, columns, counts)


def split(v):
    hi = v.astype(BF16)
    return hi, (v - hi.astype(F32)).astype(BF16)


def low_lanes(rows):
    return lax.broadcasted_iota(jnp.int32, (rows, LANES), 1) < LANES // 2


def block_at(row_ref, code, upper):
    slot = jnp.maximum(code - 1, 0)
    v = row_ref[:, pl.ds(pl.multiple_of((slot >> 1) * LANES, LANES), LANES)]
    v = jnp.where((slot & 1) != upper, pltpu.roll(v, LANES // 2, 1), v)
    return jnp.where(code > 0, v, jnp.zeros_like(v))


def pair_at(row_ref, table, r, pair):
    v0 = block_at(row_ref, table[r, 2 * pair], 0)
    v1 = block_at(row_ref, table[r, 2 * pair + 1], 1)
    return jnp.where(low_lanes(v0.shape[0]), v0, v1)


def densify_half(chunk, table, half, b, first=0):
    tile = chunk.shape[1]
    for r in range(2):
        for pair in range(b.shape[1] // LANES):
            hi, lo = split(pair_at(chunk.at[r], table, 2 * half + r, first + pair))
            lanes = slice(pair * LANES, (pair + 1) * LANES)
            b[r * tile : (r + 1) * tile, lanes] = hi
            b[(2 + r) * tile : (3 + r) * tile, lanes] = lo


def times_half(a, b, lanes):
    depth = b.shape[0]
    return jnp.dot(a[:, :depth], b[:, lanes], preferred_element_type=F32) + jnp.dot(
        a[:, depth:], b[: depth // 2, lanes], preferred_element_type=F32
    )


def lane_blocks(width, step=256):
    return [slice(i, i + step) for i in range(0, width, step)]


def ham_kernel(ham_cols, ham_count, ham, a, ham_table, ham_here, sems):
    rows, tile, _ = ham.shape
    copies = [
        pltpu.make_async_copy(ham.at[q], ham_here.at[q], sems.at[q]) for q in range(rows)
    ]
    for copy in copies:
        copy.start()
    fill_table(ham_table, ham_cols, ham_count)
    for q in range(rows):
        copies[q].wait()
        for pair in range(ham_table.shape[1] // 2):
            hi, lo = split(pair_at(ham_here.at[q], ham_table, q, pair))
            a[pair, q * tile : (q + 1) * tile, 0:LANES] = hi
            a[pair, q * tile : (q + 1) * tile, LANES : 2 * LANES] = hi
            a[pair, q * tile : (q + 1) * tile, 2 * LANES : 3 * LANES] = lo


def add_half(step, half, first, dens_table, a, acc_in, chunk, out, b):
    densify_half(chunk, dens_table, half, b, first // LANES)
    pair = shard_of(step) * (dens_table.shape[0] // 2) + half
    for lanes in lane_blocks(out.shape[1]):
        part = times_half(a[pair], b, lanes)
        if acc_in is not None:
            part += acc_in[:, first + lanes.start : first + lanes.stop]
        out[:, lanes] = part


def add_kernel(step, halves, dens_table, a, *rest):
    (acc, b), chunks = rest[-2:], rest[-2 - len(halves) : -2]
    before = rest[0] if step > 0 else None
    for half, chunk in zip(halves, chunks):
        add_half(step, half, 0, dens_table, a, before, chunk, acc, b)
        before = acc


def pick_kernel(half, dens_table, pick):
    rows, deep, width = pick.shape
    here = lax.broadcasted_iota(jnp.int32, (deep, LANES), 0)
    lane = lax.broadcasted_iota(jnp.int32, (deep, LANES), 1)
    block = LANES // 2
    for r in range(rows):
        for pair in range(width // LANES):
            codes = [dens_table[2 * half + r, 2 * pair + side] for side in range(2)]
            wanted = jnp.where(
                lane < block, codes[0] * block - block, codes[1] * block - LANES
            )
            pick[r, :, pair * LANES : (pair + 1) * LANES] = jnp.where(
                here == lane + wanted, 1.0, 0.0
            ).astype(BF16)


def last_kernel(step, half, first, a, acc_in, chunk, pick, m_hi, m_lo, p, above, below, b):
    rows, tile, _ = chunk.shape
    width = p.shape[1]
    for r in range(rows):
        hi, lo = split(chunk[r])
        placed = jnp.dot(
            jnp.concatenate([hi, lo], axis=0),
            pick[r, :, first : first + width],
            preferred_element_type=F32,
        ).astype(BF16)
        b[r * tile : (r + 1) * tile, :] = placed[:tile]
        b[(rows + r) * tile : (rows + r + 1) * tile, :] = placed[tile:]
    pair = shard_of(step) * (a.shape[0] // lax.axis_size("cross")) + half
    tall = p.shape[0]
    both_hi = m_hi[0:2].reshape(2 * tall, tall)
    both_lo = m_lo[0:2].reshape(2 * tall, tall)
    for lanes in lane_blocks(width):
        part = acc_in[:, first + lanes.start : first + lanes.stop] + times_half(a[pair], b, lanes)
        p[:, lanes] = part
        hi, lo = split(part)
        terms = (
            jnp.dot(both_hi, hi, preferred_element_type=F32)
            + jnp.dot(both_hi, lo, preferred_element_type=F32)
            + jnp.dot(both_lo, hi, preferred_element_type=F32)
        )
        above[:, lanes] = terms[:tall]
        below[:, lanes] = terms[tall:]


def margin_kernel(over, hi_out, lo_out):
    rows, tile, _ = over.shape
    for place, s in enumerate((0, 2, 1)):
        for j in range(rows):
            for pair in range(rows // 2):
                at = (s * rows + j) * tile
                lanes = slice(at // LANES * LANES, at // LANES * LANES + LANES)
                v0, v1 = over[2 * pair, :, lanes], over[2 * pair + 1, :, lanes]
                if at % LANES == 0:
                    v1 = pltpu.roll(v1, LANES // 2, 1)
                else:
                    v0 = pltpu.roll(v0, LANES // 2, 1)
                hi, lo = split(jnp.where(low_lanes(tile), v0, v1))
                to = slice(pair * LANES, (pair + 1) * LANES)
                hi_out[place, j * tile : (j + 1) * tile, to] = hi
                lo_out[place, j * tile : (j + 1) * tile, to] = lo


def weigh(out, m_hi, m_lo, s, p):
    for lanes in lane_blocks(p.shape[1]):
        hi, lo = split(p[:, lanes])
        out[:, lanes] = (
            jnp.dot(m_hi[s], hi, preferred_element_type=F32)
            + jnp.dot(m_hi[s], lo, preferred_element_type=F32)
            + jnp.dot(m_lo[s], hi, preferred_element_type=F32)
        )


def own_kernel(m_hi, m_lo, *rest):
    parts, (product, window, term, sems) = rest[:-4], rest[-4:]
    rows, tile, width = product.shape
    copies = []

    def start(ref, out, at):
        for q in range(rows):
            copies.append(
                pltpu.make_async_copy(
                    ref.at[pl.ds(q * tile, tile)],
                    out.at[q, :, pl.ds(at, ref.shape[1])],
                    sems.at[len(copies)],
                )
            )
            copies[-1].start()

    at = 0
    for part in parts:
        start(part, product, at)
        at += part.shape[1]
    at = 0
    for part in parts:
        here = term.at[:, pl.ds(at, part.shape[1])]
        weigh(here, m_hi, m_lo, 2, part)
        start(here, window, width + at)
        at += part.shape[1]
    for copy in copies:
        copy.wait()


def arrived_kernel(at, above, below, window_in, window, sems):
    rows, tile, triple = window.shape
    copies = [
        pltpu.make_async_copy(
            term.at[pl.ds(q * tile, tile)],
            window.at[q, :, pl.ds(start + at, term.shape[1])],
            sems.at[i, q],
        )
        for i, (term, start) in enumerate(((above, 0), (below, triple // 3 * 2)))
        for q in range(rows)
    ]
    for copy in copies:
        copy.start()
    for copy in copies:
        copy.wait()


def call(kernel, name, out_shape, in_spaces, out_spaces, scratch, aliases=None):
    return pl.pallas_call(
        kernel,
        name=name,
        out_shape=out_shape,
        in_specs=[pl.BlockSpec(memory_space=s) for s in in_spaces],
        out_specs=jax.tree.map(lambda s: pl.BlockSpec(memory_space=s), out_spaces),
        scratch_shapes=scratch,
        input_output_aliases=aliases or {},
        cost_estimate=pl.CostEstimate(flops=1024, bytes_accessed=1024, transcendentals=0),
        compiler_params=pltpu.CompilerParams(vmem_limit_bytes=24 << 20),
    )


def shards(ham_tiles, ham_cols, ham_count, dens_tiles, dens_cols, dens_count, over_tiles):
    count = lax.axis_size("cross")
    rows, tile, _ = ham_tiles.shape
    blocks = rows * count
    width = blocks * tile
    tall = rows * tile
    per_shard = rows // 2
    sds = jax.ShapeDtypeStruct

    halves = call(
        cut_kernel,
        "cut",
        [sds((2, tile, dens_tiles.shape[2]), F32)] * per_shard,
        (pltpu.HBM,),
        [VMEM] * per_shard,
        [pltpu.SemaphoreType.DMA((per_shard,))],
    )(pltpu.with_memory_space_constraint(dens_tiles, pltpu.HBM))
    *halves, dens_cols = lax.optimization_barrier((*halves, dens_cols))
    arrivals = [halves, [pass_on(h, 1) for h in halves]]
    ham_cols, ham_count, dens_cols, dens_count, ham_tiles = (
        pltpu.with_memory_space_constraint(x, pltpu.HBM)
        for x in (ham_cols, ham_count, dens_cols, dens_count, ham_tiles)
    )
    table = call(
        table_kernel,
        "table",
        sds((rows, blocks), jnp.int32),
        (SMEM, SMEM),
        SMEM,
        [],
    )(dens_cols, dens_count)
    tables = [table] + [pass_on(table, step) for step in range(1, count)]
    m_hi, m_lo = call(
        margin_kernel,
        "margin",
        (sds((3, tall, tall), BF16),) * 2,
        (VMEM,),
        (VMEM, VMEM),
        [],
    )(over_tiles)
    a = None

    def add(step, chunks, acc):
        return call(
            functools.partial(add_kernel, step, list(range(len(chunks)))),
            "add%d" % step,
            sds((tall, width), F32),
            (SMEM,) + (VMEM,) * (1 + len(chunks) + (step > 0)),
            VMEM,
            [VMEM((4 * tile, width), BF16)],
        )(tables[step], a, *([acc] if step > 0 else []), *chunks)

    pieces = (width // 4,) * 4
    acc = None
    for step in range(1, count - 1):
        now = arrivals[-1]
        if step == 1:
            now[0], ham_tiles = lax.optimization_barrier((now[0], ham_tiles))
            a = call(
                ham_kernel,
                "ham",
                sds((blocks // 2, tall, 3 * LANES), BF16),
                (SMEM, SMEM, pltpu.HBM),
                VMEM,
                [
                    pltpu.SMEM((rows, blocks), jnp.int32),
                    VMEM(ham_tiles.shape, F32),
                    pltpu.SemaphoreType.DMA((rows,)),
                ],
            )(ham_cols, ham_count, ham_tiles)
            now[-1], a, *tables = lax.optimization_barrier((now[-1], a, *tables))
        else:
            now[0], acc = lax.optimization_barrier((now[0], acc))
        if step == 2:
            pick = call(
                functools.partial(pick_kernel, per_shard - 1),
                "pick",
                sds((2, dens_tiles.shape[2], width), BF16),
                (SMEM,),
                VMEM,
                [],
            )(tables[-1])
            now[-1], m_hi, m_lo, pick = lax.optimization_barrier((now[-1], m_hi, m_lo, pick))
        acc = add(step - 1, arrivals[-2], acc)
        arrivals.append([pass_on(h, 1) for h in now])
    acc = add(count - 2, arrivals[-2], acc)
    acc = add(count - 1, arrivals[-1][:-1], acc)

    parts, befores, afters = [], [], []
    for i, piece in enumerate(pieces):
        part, above, below = call(
            functools.partial(last_kernel, count - 1, per_shard - 1, sum(pieces[:i])),
            "last%d" % i,
            [sds((tall, piece), F32)] * 3,
            (VMEM,) * 6,
            [VMEM] * 3,
            [VMEM((4 * tile, piece), BF16)],
        )(a, acc, arrivals[-1][-1], pick, m_hi, m_lo)
        if i + 1 < len(pieces):
            part, acc = lax.optimization_barrier((part, acc))
        parts.append(part)
        befores.append(rotate(below, 1))
        afters.append(rotate(above, -1))
    product, window = call(
        own_kernel,
        "own",
        (sds((rows, tile, width), F32), sds((rows, tile, 3 * width), F32)),
        (VMEM,) * (2 + len(pieces)),
        (pl.ANY, pl.ANY),
        [VMEM((tall, width), F32), pltpu.SemaphoreType.DMA((2 * len(pieces) * rows,))],
    )(m_hi, m_lo, *parts)
    for i in range(len(pieces)):
        window = call(
            functools.partial(arrived_kernel, sum(pieces[:i])),
            "arrived%d" % i,
            sds((rows, tile, 3 * width), F32),
            (VMEM, VMEM, pl.ANY),
            pl.ANY,
            [pltpu.SemaphoreType.DMA((2, rows))],
            {2: 0},
        )(befores[i], afters[i], window)
    return (product, window)


def solution(mesh):
    whole = P(AXES)
    return jax.shard_map(
        shards,
        mesh=mesh,
        in_specs=(whole,) * 7,
        out_specs=(whole, whole),
        check_vma=False,
    )
```

```python
import functools

import jax
import jax.numpy as jnp
from jax import lax
from jax.experimental import pallas as pl
from jax.experimental.pallas import tpu as pltpu
from jax.sharding import PartitionSpec as P

LANES = 128
F32 = jnp.float32
BF16 = jnp.bfloat16
VMEM = pltpu.VMEM
SMEM = pltpu.SMEM


AXES = ("parts", "line", "cross")


def permute(x, target):
    parts, line, cross = (lax.axis_size(axis) for axis in AXES)
    flat = lambda p, g, c: (p % parts * line + g % line) * cross + c
    places = [(p, g, c) for p in range(parts) for g in range(line) for c in range(cross)]
    return lax.ppermute(x, AXES, [(flat(*place), flat(*target(*place))) for place in places])


def rotate(x, by):
    return permute(x, lambda p, g, c: (p, g + by, c))


def ring_order(count):
    return list(range(0, count, 2))[:1] + list(range(1, count, 2)) + list(range(0, count, 2))[:0:-1]


def pass_on(x, by):
    order = ring_order(lax.axis_size("cross"))
    after = {d: order[(i + by) % len(order)] for i, d in enumerate(order)}
    return permute(x, lambda p, g, c: (p, g, after[c]))


def shard_of(step):
    order = ring_order(lax.axis_size("cross"))
    me = lax.axis_index("cross")
    owner = jnp.int32(0)
    for i, d in enumerate(order):
        owner = jnp.where(me == d, order[i - step], owner)
    return owner


def fill_table(table, columns, counts):
    rows, width = table.shape
    for r in range(rows):
        for c in range(width):
            table[r, c] = 0
        for slot in range(columns.shape[1]):

            @pl.when(slot < counts[r])
            def _(r=r, slot=slot):
                table[r, columns[r, slot]] = slot + 1


def cut_kernel(half, dens, out, sem):
    copy = pltpu.make_async_copy(dens.at[pl.ds(2 * half, 2)], out, sem)
    copy.start()
    copy.wait()


def table_kernel(columns, counts, table):
    fill_table(table, columns, counts)


def split(v):
    hi = v.astype(BF16)
    return hi, (v - hi.astype(F32)).astype(BF16)


def low_lanes(rows):
    return lax.broadcasted_iota(jnp.int32, (rows, LANES), 1) < LANES // 2


def block_at(row_ref, code, upper):
    slot = jnp.maximum(code - 1, 0)
    v = row_ref[:, pl.ds(pl.multiple_of((slot >> 1) * LANES, LANES), LANES)]
    v = jnp.where((slot & 1) != upper, pltpu.roll(v, LANES // 2, 1), v)
    return jnp.where(code > 0, v, jnp.zeros_like(v))


def pair_at(row_ref, table, r, pair):
    v0 = block_at(row_ref, table[r, 2 * pair], 0)
    v1 = block_at(row_ref, table[r, 2 * pair + 1], 1)
    return jnp.where(low_lanes(v0.shape[0]), v0, v1)


def densify_half(chunk, table, half, b, first=0):
    tile = chunk.shape[1]
    for r in range(2):
        for pair in range(b.shape[1] // LANES):
            hi, lo = split(pair_at(chunk.at[r], table, 2 * half + r, first + pair))
            lanes = slice(pair * LANES, (pair + 1) * LANES)
            b[r * tile : (r + 1) * tile, lanes] = hi
            b[(2 + r) * tile : (3 + r) * tile, lanes] = lo


def times_half(a, b, lanes):
    depth = b.shape[0]
    return jnp.dot(a[:, :depth], b[:, lanes], preferred_element_type=F32) + jnp.dot(
        a[:, depth:], b[: depth // 2, lanes], preferred_element_type=F32
    )


def lane_blocks(width, step=256):
    return [slice(i, i + step) for i in range(0, width, step)]


def ham_kernel(ham_cols, ham_count, ham, a, ham_table, ham_here, sems):
    rows, tile, _ = ham.shape
    copies = [
        pltpu.make_async_copy(ham.at[q], ham_here.at[q], sems.at[q]) for q in range(rows)
    ]
    for copy in copies:
        copy.start()
    fill_table(ham_table, ham_cols, ham_count)
    for q in range(rows):
        copies[q].wait()
        for pair in range(ham_table.shape[1] // 2):
            hi, lo = split(pair_at(ham_here.at[q], ham_table, q, pair))
            a[pair, q * tile : (q + 1) * tile, 0:LANES] = hi
            a[pair, q * tile : (q + 1) * tile, LANES : 2 * LANES] = hi
            a[pair, q * tile : (q + 1) * tile, 2 * LANES : 3 * LANES] = lo


def add_half(step, half, first, dens_table, a, acc_in, chunk, out, b):
    densify_half(chunk, dens_table, half, b, first // LANES)
    pair = shard_of(step) * (dens_table.shape[0] // 2) + half
    for lanes in lane_blocks(out.shape[1]):
        part = times_half(a[pair], b, lanes)
        if acc_in is not None:
            part += acc_in[:, first + lanes.start : first + lanes.stop]
        out[:, lanes] = part


def add_kernel(step, halves, dens_table, a, *rest):
    (acc, b), chunks = rest[-2:], rest[-2 - len(halves) : -2]
    before = rest[0] if step > 0 else None
    for half, chunk in zip(halves, chunks):
        add_half(step, half, 0, dens_table, a, before, chunk, acc, b)
        before = acc


def pick_kernel(half, dens_table, pick):
    rows, deep, width = pick.shape
    here = lax.broadcasted_iota(jnp.int32, (deep, LANES), 0)
    lane = lax.broadcasted_iota(jnp.int32, (deep, LANES), 1)
    block = LANES // 2
    for r in range(rows):
        for pair in range(width // LANES):
            codes = [dens_table[2 * half + r, 2 * pair + side] for side in range(2)]
            wanted = jnp.where(
                lane < block, codes[0] * block - block, codes[1] * block - LANES
            )
            pick[r, :, pair * LANES : (pair + 1) * LANES] = jnp.where(
                here == lane + wanted, 1.0, 0.0
            ).astype(BF16)


def last_kernel(step, half, first, a, acc_in, chunk, pick, m_hi, m_lo, p, above, below, b):
    rows, tile, _ = chunk.shape
    width = p.shape[1]
    for r in range(rows):
        hi, lo = split(chunk[r])
        placed = jnp.dot(
            jnp.concatenate([hi, lo], axis=0),
            pick[r, :, first : first + width],
            preferred_element_type=F32,
        ).astype(BF16)
        b[r * tile : (r + 1) * tile, :] = placed[:tile]
        b[(rows + r) * tile : (rows + r + 1) * tile, :] = placed[tile:]
    pair = shard_of(step) * (a.shape[0] // lax.axis_size("cross")) + half
    tall = p.shape[0]
    both_hi = m_hi[0:2].reshape(2 * tall, tall)
    both_lo = m_lo[0:2].reshape(2 * tall, tall)
    for lanes in lane_blocks(width):
        part = acc_in[:, first + lanes.start : first + lanes.stop] + times_half(a[pair], b, lanes)
        p[:, lanes] = part
        hi, lo = split(part)
        terms = (
            jnp.dot(both_hi, hi, preferred_element_type=F32)
            + jnp.dot(both_hi, lo, preferred_element_type=F32)
            + jnp.dot(both_lo, hi, preferred_element_type=F32)
        )
        above[:, lanes] = terms[:tall]
        below[:, lanes] = terms[tall:]


def margin_kernel(over, hi_out, lo_out):
    rows, tile, _ = over.shape
    for place, s in enumerate((0, 2, 1)):
        for j in range(rows):
            for pair in range(rows // 2):
                at = (s * rows + j) * tile
                lanes = slice(at // LANES * LANES, at // LANES * LANES + LANES)
                v0, v1 = over[2 * pair, :, lanes], over[2 * pair + 1, :, lanes]
                if at % LANES == 0:
                    v1 = pltpu.roll(v1, LANES // 2, 1)
                else:
                    v0 = pltpu.roll(v0, LANES // 2, 1)
                hi, lo = split(jnp.where(low_lanes(tile), v0, v1))
                to = slice(pair * LANES, (pair + 1) * LANES)
                hi_out[place, j * tile : (j + 1) * tile, to] = hi
                lo_out[place, j * tile : (j + 1) * tile, to] = lo


def weigh(out, m_hi, m_lo, s, p):
    for lanes in lane_blocks(p.shape[1]):
        hi, lo = split(p[:, lanes])
        out[:, lanes] = (
            jnp.dot(m_hi[s], hi, preferred_element_type=F32)
            + jnp.dot(m_hi[s], lo, preferred_element_type=F32)
            + jnp.dot(m_lo[s], hi, preferred_element_type=F32)
        )


def own_kernel(m_hi, m_lo, *rest):
    parts, (product, window, term, sems) = rest[:-4], rest[-4:]
    rows, tile, width = product.shape
    copies = []

    def start(ref, out, at):
        for q in range(rows):
            copies.append(
                pltpu.make_async_copy(
                    ref.at[pl.ds(q * tile, tile)],
                    out.at[q, :, pl.ds(at, ref.shape[1])],
                    sems.at[len(copies)],
                )
            )
            copies[-1].start()

    at = 0
    for part in parts:
        start(part, product, at)
        at += part.shape[1]
    at = 0
    for part in parts:
        here = term.at[:, pl.ds(at, part.shape[1])]
        weigh(here, m_hi, m_lo, 2, part)
        start(here, window, width + at)
        at += part.shape[1]
    for copy in copies:
        copy.wait()


def arrived_kernel(at, above, below, window_in, window, sems):
    rows, tile, triple = window.shape
    copies = [
        pltpu.make_async_copy(
            term.at[pl.ds(q * tile, tile)],
            window.at[q, :, pl.ds(start + at, term.shape[1])],
            sems.at[i, q],
        )
        for i, (term, start) in enumerate(((above, 0), (below, triple // 3 * 2)))
        for q in range(rows)
    ]
    for copy in copies:
        copy.start()
    for copy in copies:
        copy.wait()


def call(kernel, name, out_shape, in_spaces, out_spaces, scratch, aliases=None):
    return pl.pallas_call(
        kernel,
        name=name,
        out_shape=out_shape,
        in_specs=[pl.BlockSpec(memory_space=s) for s in in_spaces],
        out_specs=jax.tree.map(lambda s: pl.BlockSpec(memory_space=s), out_spaces),
        scratch_shapes=scratch,
        input_output_aliases=aliases or {},
        cost_estimate=pl.CostEstimate(flops=1024, bytes_accessed=1024, transcendentals=0),
        compiler_params=pltpu.CompilerParams(vmem_limit_bytes=24 << 20),
    )


def shards(ham_tiles, ham_cols, ham_count, dens_tiles, dens_cols, dens_count, over_tiles):
    count = lax.axis_size("cross")
    rows, tile, _ = ham_tiles.shape
    blocks = rows * count
    width = blocks * tile
    tall = rows * tile
    per_shard = rows // 2
    sds = jax.ShapeDtypeStruct

    dens_here = pltpu.with_memory_space_constraint(dens_tiles, pltpu.HBM)
    halves = []
    for h in range(per_shard):
        half = call(
            functools.partial(cut_kernel, h),
            "cut%d" % h,
            sds((2, tile, dens_tiles.shape[2]), F32),
            (pltpu.HBM,),
            VMEM,
            [pltpu.SemaphoreType.DMA],
        )(dens_here)
        half, dens_here = lax.optimization_barrier((half, dens_here))
        halves.append(half)
    halves[0], dens_cols = lax.optimization_barrier((halves[0], dens_cols))
    arrivals = [halves, [pass_on(h, 1) for h in halves]]
    ham_cols, ham_count, dens_cols, dens_count, ham_tiles = (
        pltpu.with_memory_space_constraint(x, pltpu.HBM)
        for x in (ham_cols, ham_count, dens_cols, dens_count, ham_tiles)
    )
    table = call(
        table_kernel,
        "table",
        sds((rows, blocks), jnp.int32),
        (SMEM, SMEM),
        SMEM,
        [],
    )(dens_cols, dens_count)
    tables = [table] + [pass_on(table, step) for step in range(1, count)]
    m_hi, m_lo = call(
        margin_kernel,
        "margin",
        (sds((3, tall, tall), BF16),) * 2,
        (VMEM,),
        (VMEM, VMEM),
        [],
    )(over_tiles)
    a = None

    def add(step, chunks, acc):
        return call(
            functools.partial(add_kernel, step, list(range(len(chunks)))),
            "add%d" % step,
            sds((tall, width), F32),
            (SMEM,) + (VMEM,) * (1 + len(chunks) + (step > 0)),
            VMEM,
            [VMEM((4 * tile, width), BF16)],
        )(tables[step], a, *([acc] if step > 0 else []), *chunks)

    pieces = (width // 4,) * 4
    acc = None
    for step in range(1, count - 1):
        now = arrivals[-1]
        if step == 1:
            now[0], ham_tiles = lax.optimization_barrier((now[0], ham_tiles))
            a = call(
                ham_kernel,
                "ham",
                sds((blocks // 2, tall, 3 * LANES), BF16),
                (SMEM, SMEM, pltpu.HBM),
                VMEM,
                [
                    pltpu.SMEM((rows, blocks), jnp.int32),
                    VMEM(ham_tiles.shape, F32),
                    pltpu.SemaphoreType.DMA((rows,)),
                ],
            )(ham_cols, ham_count, ham_tiles)
            now[-1], a, *tables = lax.optimization_barrier((now[-1], a, *tables))
        else:
            now[0], acc = lax.optimization_barrier((now[0], acc))
        if step == 2:
            pick = call(
                functools.partial(pick_kernel, per_shard - 1),
                "pick",
                sds((2, dens_tiles.shape[2], width), BF16),
                (SMEM,),
                VMEM,
                [],
            )(tables[-1])
            now[-1], m_hi, m_lo, pick = lax.optimization_barrier((now[-1], m_hi, m_lo, pick))
        acc = add(step - 1, arrivals[-2], acc)
        arrivals.append([pass_on(h, 1) for h in now])
    acc = add(count - 2, arrivals[-2], acc)
    acc = add(count - 1, arrivals[-1][:-1], acc)

    parts, befores, afters = [], [], []
    for i, piece in enumerate(pieces):
        part, above, below = call(
            functools.partial(last_kernel, count - 1, per_shard - 1, sum(pieces[:i])),
            "last%d" % i,
            [sds((tall, piece), F32)] * 3,
            (VMEM,) * 6,
            [VMEM] * 3,
            [VMEM((4 * tile, piece), BF16)],
        )(a, acc, arrivals[-1][-1], pick, m_hi, m_lo)
        if i + 1 < len(pieces):
            part, acc = lax.optimization_barrier((part, acc))
        parts.append(part)
        befores.append(rotate(below, 1))
        afters.append(rotate(above, -1))
    product, window = call(
        own_kernel,
        "own",
        (sds((rows, tile, width), F32), sds((rows, tile, 3 * width), F32)),
        (VMEM,) * (2 + len(pieces)),
        (pl.ANY, pl.ANY),
        [VMEM((tall, width), F32), pltpu.SemaphoreType.DMA((2 * len(pieces) * rows,))],
    )(m_hi, m_lo, *parts)
    for i in range(len(pieces)):
        window = call(
            functools.partial(arrived_kernel, sum(pieces[:i])),
            "arrived%d" % i,
            sds((rows, tile, 3 * width), F32),
            (VMEM, VMEM, pl.ANY),
            pl.ANY,
            [pltpu.SemaphoreType.DMA((2, rows))],
            {2: 0},
        )(befores[i], afters[i], window)
    return (product, window)


def solution(mesh):
    whole = P(AXES)
    return jax.shard_map(
        shards,
        mesh=mesh,
        in_specs=(whole,) * 7,
        out_specs=(whole, whole),
        check_vma=False,
    )
```
